32 devices in a mesh: dom: 4 (over y, core), expert: 4 (over z), rep: 2 (over x).
Axes of the slice: x: 2, y: 2, z: 4, core: 2. Of those that a mesh axis runs over, the one named last changes fastest.
Arguments:
- features: bfloat16 [2048, 512], P(('dom', 'expert'), 'rep'), may hold values from -6 to 6
- tile_values: bfloat16 [4, 4, 4, 4, 128, 128], P('dom', 'expert'), may hold values from -0.125 to 0.125
- tile_pairs: int32 [4, 4, 4, 4], P('dom', 'expert'), may hold values from 0 to 3
- dispatch: int32 [32, 64], P(('dom', 'expert', 'rep')), may hold values from 0 to 63, each once within a row
- w_in: bfloat16 [4, 512, 2048], P('expert', None, 'dom'), may hold values from -0.25 to 0.25
- w_out: bfloat16 [4, 2048, 512], P('expert', 'dom'), may hold values from -0.125 to 0.125
- cotangent: bfloat16 [2048, 512], P(('dom', 'expert', 'rep')), may hold values from -1.5 to 1.5
Outputs:
- out: bfloat16 [2048, 512], P(('dom', 'expert', 'rep'))
- grad_features: float32 [2048, 512], P(('dom', 'expert'), 'rep')
- grad_w_in: float32 [4, 512, 2048], P('expert', None, 'dom')
- grad_w_out: float32 [4, 2048, 512], P('expert', 'dom')
The draws below stay inside these ranges and needn't reach their ends.
Inputs may be any that keep to these rules, and one draw needn't show every extreme that they name: Each row of dispatch is a permutation of 0 to 63. `tile_pairs`: A value v names destination tile v of its partition; the source tile is the whole 128-row source block.
All inputs are finite; a program needn't handle non-finite values.
Results may differ from the reference program's by a relative error of at most 0.0095.
Values may be sent and summed in bfloat16 or wider, within the bound.
A program may use at most 64 MiB of HBM per device.

```python
import jax
import jax.numpy as jnp
from jax import lax

D = 512
FF = 2048
TILE = 128
TPS = 4
ROWS_DEV = 128
EXPERTS = 4
NODES = 2048
SRC_TILES = 1
DEST_TILES = 4
MR = 64
SLOTS = 16
FSLICE = 512
N_DOM = 4
N_EXPERT = 4


def with_ends(entries, own_key, least, high):
    place = [jax.random.randint(jax.random.fold_in(own_key, axis), (), 0, length) for axis, length in enumerate(entries.shape)]
    main_axis = entries.shape.index(max(entries.shape))
    neighbour = place[:main_axis] + [(place[main_axis] + 1) % entries.shape[main_axis]] + place[main_axis + 1:]
    return entries.at[tuple(place)].set(least).at[tuple(neighbour)].set(high)


def shard_levels(key, extent, cuts, low, largest):
    def one(position, blocks):
        heights = jax.random.uniform(jax.random.fold_in(jax.random.fold_in(key, 6), position), (blocks,), jnp.float32, low / len(cuts), largest / len(cuts))
        return jnp.repeat(jnp.exp(heights), extent[position] // blocks).reshape((-1,) + (1,) * (len(extent) - position - 1))

    loudness = one(*cuts[0])
    for cut in cuts[1:]:
        loudness = loudness * one(*cut)
    return loudness


def scatter_about(stream_key, shape, width, bound, split=(), kind=jnp.bfloat16):
    result = jax.random.normal(stream_key, shape, jnp.float32) * width
    if len(split) > 0:
        result = shard_levels(stream_key, shape, split, -0.22, 0.18) * result
    return jnp.clip(result, min=-bound, max=bound).astype(kind)


def setup_inputs(seed: int = 0) -> dict:
    key_of = jax.random.split(jax.random.key(seed), 8)
    return {
        "features": scatter_about(key_of[0], (NODES, D), 1.0, 6.0, ((0, 16), (1, 2))),
        "tile_values": scatter_about(key_of[1], (N_DOM, N_EXPERT, N_DOM, TPS, TILE, TILE), (N_DOM * TPS * TILE * TILE // ROWS_DEV) ** -0.5, 0.125, ((0, 4), (1, 4))),
        "tile_pairs": with_ends(jax.random.randint(key_of[2], (N_DOM, N_EXPERT, N_DOM, TPS), 0, DEST_TILES * SRC_TILES), jax.random.fold_in(key_of[2], 1), 0, (DEST_TILES * SRC_TILES) - 1).astype(jnp.int32),
        "dispatch": jax.vmap(lambda own: jax.random.permutation(own, MR))(jax.random.split(key_of[3], (NODES // MR))).reshape((NODES // MR, MR)).astype(jnp.int32),
        "w_in": scatter_about(key_of[4], (EXPERTS, D, FF), D ** -0.5, 0.25, ((0, 4), (2, 4))),
        "w_out": scatter_about(key_of[5], (EXPERTS, FF, D), FF ** -0.5, 0.125, ((0, 4), (1, 4))),
        "cotangent": scatter_about(key_of[6], (NODES, D), 0.25, 1.5, ((0, 32),)),
    }


epsilon = 1e-06
gelu_scale = 0.7978845608028654
gelu_cubic = 0.044715
highest = lax.Precision.HIGHEST

def gelu_tanh(value):
    inner = gelu_scale * (value + gelu_cubic * value * value * value)
    return 0.5 * value * (1.0 + jnp.tanh(inner))

def gelu_slope(value):
    tangent = jnp.tanh(gelu_scale * (value + gelu_cubic * value * value * value))
    return 0.5 * (1.0 + tangent) + 0.5 * value * (1.0 - tangent * tangent) * gelu_scale * (1.0 + 3.0 * gelu_cubic * value * value)

def aggregate(features, tile_values, tile_pairs):
    tiles = features.reshape(N_DOM, N_EXPERT, SRC_TILES, TILE, D)
    source_ids = jnp.arange(N_DOM, dtype=jnp.int32)[None, :, None]
    column_ids = jnp.arange(N_EXPERT, dtype=jnp.int32)[:, None, None]
    dest_ids = jnp.arange(DEST_TILES, dtype=jnp.int32)

    def one_part(part):
        values = tile_values[part].astype(jnp.float32)
        pair_list = tile_pairs[part]
        chosen = tiles[source_ids, column_ids, pair_list % SRC_TILES].astype(jnp.float32)
        contrib = jnp.einsum('eskij,eskjf->eskif', values, chosen, precision=highest)
        hot = (pair_list[..., None] // SRC_TILES == dest_ids).astype(jnp.float32)
        column_terms = jnp.einsum('eskq,eskif->eqif', hot, contrib, precision=highest).astype(jnp.bfloat16)
        column_terms = lax.optimization_barrier(column_terms)
        return lax.optimization_barrier(jnp.sum(column_terms.astype(jnp.float32), axis=0))
    parts = lax.map(one_part, jnp.arange(N_DOM, dtype=jnp.int32))
    return parts.reshape(NODES, D)

def spread_back(grad_agg, tile_values, tile_pairs):
    tiles = grad_agg.reshape(N_DOM, DEST_TILES, TILE, D)
    part_ids = jnp.arange(N_DOM, dtype=jnp.int32)[:, None, None]
    src_ids = jnp.arange(SRC_TILES, dtype=jnp.int32)

    def one_source(source):
        values = jnp.take(tile_values, source, axis=2).astype(jnp.float32)
        pair_list = jnp.take(tile_pairs, source, axis=2)
        chosen = tiles[part_ids, pair_list // SRC_TILES].astype(jnp.float32)
        contrib = jnp.einsum('dekji,dekjf->dekif', values, chosen, precision=highest)
        hot = (pair_list[..., None] % SRC_TILES == src_ids).astype(jnp.float32)
        placed = jnp.einsum('dekr,dekif->derif', hot, contrib, precision=highest).astype(jnp.bfloat16)
        placed = lax.optimization_barrier(placed)
        summed = lax.optimization_barrier(jnp.sum(placed.astype(jnp.float32), axis=0))
        return summed.reshape(N_EXPERT, ROWS_DEV, D)
    return lax.map(one_source, jnp.arange(N_DOM, dtype=jnp.int32)).reshape(NODES, D)

def block_sum(left, right):
    count = left.shape[0]
    left_parts = left.reshape(count, N_DOM, FSLICE).astype(jnp.float32)
    right_parts = right.reshape(N_DOM, FSLICE, D).astype(jnp.float32)
    partial_value = jnp.einsum('tbh,bhd->btd', left_parts, right_parts, precision=highest).astype(jnp.bfloat16)
    partial_value = lax.optimization_barrier(partial_value)
    return lax.optimization_barrier(jnp.sum(partial_value.astype(jnp.float32), axis=0)).astype(jnp.bfloat16)

def reference(features, tile_values, tile_pairs, dispatch, w_in, w_out, cotangent):
    agg = aggregate(features, tile_values, tile_pairs).astype(jnp.bfloat16)
    agg_f = agg.astype(jnp.float32)
    scale = lax.rsqrt(lax.optimization_barrier(jnp.mean(agg_f * agg_f, axis=-1, keepdims=True)) + epsilon)
    normed = (agg_f * scale).astype(jnp.bfloat16)
    groups = NODES // MR
    base = (jnp.arange(groups, dtype=jnp.int32) * MR)[:, None]
    rows_all = dispatch + base

    def expert_work(expert):
        rows = lax.dynamic_slice_in_dim(rows_all, expert * SLOTS, SLOTS, 1).reshape(-1)
        tokens = normed[rows]
        grads = cotangent[rows]
        first = w_in[expert]
        second = w_out[expert]
        hidden_pre = jnp.dot(tokens, first, preferred_element_type=jnp.float32)
        act = gelu_tanh(hidden_pre).astype(jnp.bfloat16)
        expert_out = block_sum(act, second)
        grad_act = jnp.dot(grads, second.T, preferred_element_type=jnp.float32)
        grad_hidden = (grad_act * gelu_slope(hidden_pre)).astype(jnp.bfloat16)
        grad_second = jnp.dot(act.T, grads, preferred_element_type=jnp.float32)
        grad_first = jnp.dot(tokens.T, grad_hidden, preferred_element_type=jnp.float32)
        grad_normed = block_sum(grad_hidden, first.T)
        return (rows, expert_out, grad_normed, grad_first, grad_second)
    rows, expert_out, grad_normed, grad_w_in, grad_w_out = lax.map(expert_work, jnp.arange(EXPERTS, dtype=jnp.int32))
    flat_rows = rows.reshape(-1)
    routed = jnp.zeros((NODES, D), jnp.bfloat16).at[flat_rows].set(expert_out.reshape(-1, D))
    out = (agg_f + routed.astype(jnp.float32)).astype(jnp.bfloat16)
    back_normed = jnp.zeros((NODES, D), jnp.bfloat16).at[flat_rows].set(grad_normed.reshape(-1, D)).astype(jnp.float32)
    dot_mean = lax.optimization_barrier(jnp.mean(agg_f * back_normed, axis=-1, keepdims=True))
    grad_agg = (cotangent.astype(jnp.float32) + scale * back_normed - agg_f * (scale * scale * scale) * dot_mean).astype(jnp.bfloat16)
    grad_features = spread_back(grad_agg, tile_values, tile_pairs)
    return (out, grad_features, grad_w_in, grad_w_out)
```

```python
import functools

import jax
import jax.numpy as jnp
from jax import lax
from jax.experimental import pallas as pl
from jax.experimental.pallas import tpu as pltpu
from jax.sharding import PartitionSpec as P

epsilon = 1e-06
gelu_scale = 0.7978845608028654
gelu_cubic = 0.044715
bf16 = jnp.bfloat16
f32 = jnp.float32


def mm(left, right, dims):
    return lax.dot_general(left, right, (dims, ((), ())), preferred_element_type=f32)


plain = ((1,), (0,))
rows_rows = ((0,), (0,))
cols_cols = ((1,), (1,))


def body(sizes, *refs):
    nd, ne, nr, slots, chunk, keep_turned = sizes
    (feat, tv_hbm, pairs, disp, win_hbm, wout_hbm, cot,
     out, gf, gwi_hbm, gwo_hbm,
     tv, win, wout, gwi, gwo, fall, adj, turned, csend, crecv,
     tsend, tg, tx, ksend, kg, kx,
     gsend, grecv, gred, gback, osend, orecv, ored, oback,
     asend, gall, bsend, brecv, ga, acts, ghid,
     lsem, fs, fr, cs, cr, tzs, tzr, tds, tdr, txs, txr, kzs, kzr, kds, kdr, kxs, kxr,
     gds, gdr, gzs, gzr, ods, odr, ozs, ozr, ps, pr, bs, br) = refs
    me_d, me_e, me_r = lax.axis_index("dom"), lax.axis_index("expert"), lax.axis_index("rep")
    tile = feat.shape[0]
    half = feat.shape[1]
    tps = tv.shape[1]
    mr = cot.shape[0]
    seg = ne * slots
    rows = nd * seg
    pending = []

    def ring(me, step, count):
        return lax.rem(me + step, count)

    def send(src, dst, ssem, rsem, d, e, r):
        copy = pltpu.make_async_remote_copy(
            src_ref=src, dst_ref=dst, send_sem=ssem, recv_sem=rsem,
            device_id={"dom": d, "expert": e, "rep": r},
            device_id_type=pl.DeviceIdType.MESH,
        )
        copy.start()
        pending.append(copy)
        return copy

    def local(src, dst, index):
        copy = pltpu.make_async_copy(src, dst, lsem.at[index])
        copy.start()
        return copy

    def arrive(copies):
        for copy in copies:
            copy.wait_recv()

    def span(start, size):
        return pl.ds(pl.multiple_of(start, size), size)

    load_tv = local(tv_hbm.at[0, 0], tv, 0)
    load_wout = local(wout_hbm.at[0], wout, 1)
    load_win = local(win_hbm.at[0], win, 2)

    dom_steps = list(range(1, nd))
    flips = nd & (nd - 1) == 0

    def dom_to(k):
        if not flips:
            return ring(me_d, k, nd)
        place, bit = me_d, 1
        while bit < nd:
            if k & bit:
                place = place + bit - 2 * bit * lax.rem(me_d // bit, 2)
            bit *= 2
        return place

    def dom_from(k):
        return dom_to(k) if flips else ring(me_d, nd - k, nd)

    exp_steps = list(range(1, ne))
    pair_steps = [(a, b) for a in range(ne) for b in range(nr) if (a, b) != (0, 0)]

    barrier = pltpu.get_barrier_semaphore()
    for k in dom_steps:
        pl.semaphore_signal(barrier, inc=1, device_id={"dom": dom_to(k), "expert": me_e, "rep": me_r},
                            device_id_type=pl.DeviceIdType.MESH)
    for a, b in pair_steps:
        pl.semaphore_signal(barrier, inc=1,
                            device_id={"dom": me_d, "expert": ring(me_e, a, ne), "rep": ring(me_r, b, nr)},
                            device_id_type=pl.DeviceIdType.MESH)

    place = (lax.broadcasted_iota(jnp.int32, (mr, seg), 0) == disp[...]).astype(f32).astype(bf16)
    fall[span(me_d * tile, tile), :] = feat[...]
    ksend[...] = mm(place, cot[...], rows_rows).astype(bf16)
    load_tv.wait()

    def build(index, carry):
        q, s = index // nd, lax.rem(index, nd)
        total = jnp.zeros((tile, tile), f32)
        for k in range(tps):
            hit = jnp.where(pairs[0, 0, s, k] == q, 1.0, 0.0).astype(f32)
            total = total + tv[s, k].astype(f32) * hit
        adj[span(q * tile, tile), span(s * tile, tile)] = total.astype(bf16)
        return carry

    lax.fori_loop(0, ne * nd, build, 0)
    pl.semaphore_wait(barrier, len(dom_steps) + len(pair_steps))

    f_copies = [
        send(feat, fall.at[span(me_d * tile, tile)], fs.at[k - 1], fr.at[k - 1], dom_to(k), me_e, me_r)
        for k in dom_steps
    ]

    def to_experts(source, target, ssem, rsem):
        copies = []
        for k in exp_steps:
            x = ring(me_e, k, ne)
            copies.append(send(source.at[span(x * slots, slots)], target.at[span((me_d * ne + me_e) * slots, slots)],
                               ssem.at[k - 1], rsem.at[k - 1], me_d, x, me_r))
        mine = span((me_d * ne + me_e) * slots, slots)
        target[mine, :] = source[span(me_e * slots, slots), :]
        return copies

    def to_doms(target, ssem, rsem):
        block = target.at[span(me_d * seg, seg)]
        return [send(block, block, ssem.at[k - 1], rsem.at[k - 1], dom_to(k), me_e, me_r) for k in dom_steps]

    def to_reps(source, target, ssem, rsem):
        return [send(source, target.at[k - 1], ssem.at[k - 1], rsem.at[k - 1], me_d, me_e, ring(me_r, k, nr))
                for k in range(1, nr)]

    kz = to_experts(ksend, kg, kzs, kzr)

    def turn(index, carry):
        q, s = index // nd, lax.rem(index, nd)
        turned[span(s * tile, tile), span(q * tile, tile)] = adj[span(q * tile, tile), span(s * tile, tile)].T
        return carry


    arrive(f_copies)
    c_copies = []
    for a in list(range(1, ne)) + [0]:
        q = ring(me_e, a, ne)
        column = mm(adj[span(q * tile, tile), :], fall[...], plain).astype(bf16)
        for b in range(nr):
            csend[q, b] = column[b * mr:(b + 1) * mr, :]
        for b in range(nr):
            r = ring(me_r, b, nr)
            if (a, b) != (0, 0):
                n = a * nr + b - 1
                c_copies.append(send(csend.at[q, r], crecv.at[me_e, me_r], cs.at[n], cr.at[n], me_d, q, r))
    crecv[me_e, me_r] = csend[me_e, me_r]

    arrive(kz)
    kd = to_doms(kg, kds, kdr)
    load_wout.wait()
    load_win.wait()
    if keep_turned:
        lax.fori_loop(0, ne * nd, turn, 0)
    arrive(kd)
    whole_rows = rows == chunk
    if whole_rows:
        ga[...] = mm(kg[...], wout[...], cols_cols)

    arrive(c_copies)
    parts = []
    for r in range(nr):
        total = crecv[0, r].astype(f32)
        for e in range(1, ne):
            total = total + crecv[e, r].astype(f32)
        parts.append(total)
    agg = jnp.concatenate(parts, axis=1).astype(bf16).astype(f32)
    width = agg.shape[1]
    scale = lax.rsqrt(jnp.mean(agg * agg, axis=-1, keepdims=True) + epsilon)
    normed = (agg * scale).astype(bf16)
    tsend[...] = mm(place, normed, rows_rows).astype(bf16)
    tz = to_experts(tsend, tg, tzs, tzr)
    kxc = to_reps(kg, kx, kxs, kxr)
    arrive(tz)
    td = to_doms(tg, tds, tdr)

    def hidden(tokens, grad_act):
        pre = mm(tokens, win[...], plain)
        tangent = jnp.tanh(gelu_scale * (pre + gelu_cubic * pre * pre * pre))
        act = (0.5 * pre * (1.0 + tangent)).astype(bf16)
        slope = 0.5 * (1.0 + tangent) + 0.5 * pre * (1.0 - tangent * tangent) * gelu_scale * (
            1.0 + 3.0 * gelu_cubic * pre * pre)
        return act, (grad_act * slope).astype(bf16)

    def add_grads(tokens, grads, act, grad_hidden, first):
        one = mm(tokens, grad_hidden, rows_rows)
        two = mm(act, grads, rows_rows)
        if first:
            gwi[...] = one
            gwo[...] = two
        else:
            gwi[...] += one
            gwo[...] += two

    def scatter(source, target, ssem, rsem):
        copies = [
            send(source.at[span(dom_to(k) * seg, seg)], target.at[me_d], ssem.at[k - 1], rsem.at[k - 1],
                 dom_to(k), me_e, me_r)
            for k in dom_steps
        ]
        target[me_d] = source[span(me_d * seg, seg), :]
        return copies

    if whole_rows:
        gd = []
        for k in [0] + dom_steps:
            if k > 0:
                arrive([td[k - 1]])
            d = dom_from(k)
            where = span(d * seg, seg)
            act, grad_hidden = hidden(tg[where, :], ga[where, :])
            term = mm(grad_hidden, win[...], cols_cols).astype(bf16)
            acts[where, :] = act
            ghid[where, :] = grad_hidden
            if k == 0:
                grecv[me_d] = term
            else:
                gsend[where, :] = term
                gd.append(send(gsend.at[where], grecv.at[me_d], gds.at[k - 1], gdr.at[k - 1], d, me_e, me_r))
        txc = to_reps(tg, tx, txs, txr)
        osend[...] = mm(acts[...], wout[...], plain).astype(bf16)
        add_grads(tg[...], kg[...], acts[...], ghid[...], True)
    else:
        arrive(td)
        txc = to_reps(tg, tx, txs, txr)
        gwi[...] = jnp.zeros_like(gwi)
        gwo[...] = jnp.zeros_like(gwo)

        def one_chunk(index, carry):
            where = span(index * chunk, chunk)
            act, grad_hidden = hidden(tg[where, :], mm(kg[where, :], wout[...], cols_cols))
            gsend[where, :] = mm(grad_hidden, win[...], cols_cols).astype(bf16)
            osend[where, :] = mm(act, wout[...], plain).astype(bf16)
            add_grads(tg[where, :], kg[where, :], act, grad_hidden, False)
            return carry

        lax.fori_loop(0, rows // chunk, one_chunk, 0)
        gd = scatter(gsend, grecv, gds, gdr)

    def summed(target):
        total = target[0].astype(f32)
        for d in range(1, nd):
            total = total + target[d].astype(f32)
        return total.astype(bf16)

    def to_nodes(source, target, ssem, rsem):
        copies = []
        for k in exp_steps:
            e = ring(me_e, k, ne)
            copies.append(send(source.at[span(e * slots, slots)], target.at[span(me_e * slots, slots)],
                               ssem.at[k - 1], rsem.at[k - 1], me_d, e, me_r))
        mine = span(me_e * slots, slots)
        target[mine, :] = source[mine, :]
        return copies

    arrive(gd)
    gred[...] = summed(grecv)
    gz = to_nodes(gred, gback, gzs, gzr)
    od = scatter(osend, orecv, ods, odr)

    arrive(gz)
    back = mm(place, gback[...], plain)
    dot_mean = jnp.mean(agg * back, axis=-1, keepdims=True)
    grad_agg = (cot[...].astype(f32) + scale * back - agg * (scale * scale * scale) * dot_mean).astype(bf16)
    for r in range(nr):
        asend[r] = grad_agg[:, r * half:(r + 1) * half]
    here = span(me_e * tile + me_r * mr, mr)
    p_copies = []
    for a, b in pair_steps:
        n = a * nr + b - 1
        r = ring(me_r, b, nr)
        p_copies.append(send(asend.at[r], gall.at[here], ps.at[n], pr.at[n], me_d, ring(me_e, a, ne), r))
    gall[here, :] = asend[me_r]

    arrive(kxc)
    arrive(txc)
    for n in range(nr - 1):
        if whole_rows:
            act, grad_hidden = hidden(tx[n], mm(kx[n], wout[...], cols_cols))
            add_grads(tx[n], kx[n], act, grad_hidden, False)
        else:
            def other_chunk(index, carry):
                where = span(index * chunk, chunk)
                act, grad_hidden = hidden(tx[n, where, :], mm(kx[n, where, :], wout[...], cols_cols))
                add_grads(tx[n, where, :], kx[n, where, :], act, grad_hidden, False)
                return carry

            lax.fori_loop(0, rows // chunk, other_chunk, 0)
    store_i = local(gwi, gwi_hbm.at[0], 3)
    store_o = local(gwo, gwo_hbm.at[0], 4)

    arrive(od)
    ored[...] = summed(orecv)
    arrive(p_copies)
    oz = to_nodes(ored, oback, ozs, ozr)
    b_copies = []
    for k in dom_steps[::-1] + [0]:
        s = dom_to(k)
        if keep_turned:
            term = mm(turned[span(s * tile, tile), :], gall[...], plain)
        else:
            term = mm(adj[:, span(s * tile, tile)], gall[...], rows_rows)
        if k > 0:
            bsend[s] = term.astype(bf16)
            b_copies.append(send(bsend.at[s], brecv.at[me_d], bs.at[k - 1], br.at[k - 1], s, me_e, me_r))
        else:
            brecv[me_d] = term.astype(bf16)
    arrive(oz)
    out[...] = (agg + mm(place, oback[...], plain)).astype(bf16)
    arrive(b_copies)
    total = brecv[0].astype(f32)
    for d in range(1, nd):
        total = total + brecv[d].astype(f32)
    gf[...] = total
    store_i.wait()
    store_o.wait()
    for copy in pending:
        copy.wait_send()


def flip(me, k):
    place, bit = me, 1
    while bit <= k:
        if k & bit:
            place = place + bit - 2 * bit * lax.rem(me // bit, 2)
        bit *= 2
    return place


def body_paired(sizes, *refs):
    nd, ne, nr, slots, cuts = sizes
    (feat_hbm, tv_hbm, pairs_hbm, disp_hbm, win_hbm, wout_hbm, cot_hbm,
     out, gf, gwi, gwo,
     tv, pairs, disp, cot, win, wout, fall, adj, sorted_adj, turned, dsend, dall, csend, crecv,
     ksend, kg, kx, tg, tx, ga, acts, ghid, acts_far, gown, gsend, grecv, oown, osend, orecv, ored, oback,
     asend, gall, bsend, brecv, lsem, ssem, rsem) = refs
    me_d, me_e, me_r = lax.axis_index("dom"), lax.axis_index("expert"), lax.axis_index("rep")
    tile, half = fall.shape[0] // nd, fall.shape[1]
    tps = tv.shape[1]
    mr, width = cot.shape
    inner = win.shape[2]
    cut = mr // cuts
    pending = []

    def send(src, dst, d, e, r):
        n = len(pending)
        copy = pltpu.make_async_remote_copy(
            src_ref=src, dst_ref=dst, send_sem=ssem.at[n], recv_sem=rsem.at[n],
            device_id={"dom": flip(me_d, d), "expert": flip(me_e, e), "rep": flip(me_r, r)},
            device_id_type=pl.DeviceIdType.MESH,
        )
        copy.start()
        pending.append(copy)
        return copy

    def local(src, dst, index):
        copy = pltpu.make_async_copy(src, dst, lsem.at[index])
        copy.start()
        return copy

    def arrive(copies):
        for copy in copies:
            copy.wait_recv()

    def span(start, size):
        return pl.ds(pl.multiple_of(start, size), size)

    pair_steps = [(a, b) for a in (2, 3, 1, 0) for b in range(nr) if (a, b) != (0, 0)]
    barrier = pltpu.get_barrier_semaphore()
    for k in range(1, nd):
        pl.semaphore_signal(barrier, inc=1, device_id={"dom": flip(me_d, k), "expert": me_e, "rep": me_r},
                            device_id_type=pl.DeviceIdType.MESH)
    for a, b in pair_steps:
        pl.semaphore_signal(barrier, inc=1,
                            device_id={"dom": me_d, "expert": flip(me_e, a), "rep": flip(me_r, b)},
                            device_id_type=pl.DeviceIdType.MESH)
    own_feat = fall.at[span(me_d * tile, tile)]
    load_feat = local(feat_hbm, own_feat, 0)
    load_disp = local(disp_hbm, disp, 1)
    load_cot = local(cot_hbm, cot, 2)
    load_pairs = local(pairs_hbm, pairs, 3)
    load_tv = local(tv_hbm.at[0, 0], tv, 4)
    load_win = local(win_hbm.at[0], win.at[0], 5)
    load_wout = local(wout_hbm.at[0], wout.at[0], 6)

    load_disp.wait()
    dsend[...] = jnp.zeros_like(dsend)
    dsend[:, 0:mr] = jnp.broadcast_to(disp[...], (dsend.shape[0], mr))
    dall[me_e, me_r] = dsend[...]
    load_feat.wait()
    pl.semaphore_wait(barrier, nd - 1 + len(pair_steps))
    f_copies = [send(own_feat, own_feat, k, 0, 0) for k in (2, 3)]
    d_copies = [send(dsend, dall.at[me_e, me_r], 0, a, b) for a, b in pair_steps]
    f_copies.append(send(own_feat, own_feat, 1, 0, 0))

    place = (lax.broadcasted_iota(jnp.int32, (mr, ne * slots), 0) == disp[...]).astype(f32).astype(bf16)
    load_cot.wait()
    ksend[...] = mm(place, cot[...], rows_rows).astype(bf16)
    here = span(me_e * slots, slots)
    kz = [send(ksend.at[span(flip(me_e, a) * slots, slots)], kg.at[here], 0, a, 0) for a in (2, 3, 1)]
    kg[here, :] = ksend[here, :]
    load_pairs.wait()
    load_tv.wait()

    def build(index, carry):
        q, s = index // nd, lax.rem(index, nd)
        total = jnp.zeros((tile, tile), f32)
        for k in range(tps):
            hit = jnp.where(pairs[0, 0, s, k] == q, 1.0, 0.0).astype(f32)
            total = total + tv[s, k].astype(f32) * hit
        adj[span(q * tile, tile), span(s * tile, tile)] = total.astype(bf16)
        return carry

    lax.fori_loop(0, ne * nd, build, 0)
    load_win.wait()
    load_wout.wait()
    w_copies = [send(win.at[0], win.at[1], 1, 0, 0), send(wout.at[0], wout.at[1], 1, 0, 0)]

    arrive(d_copies)
    for e in range(ne):
        for r in range(nr):
            group = (lax.broadcasted_iota(jnp.int32, (mr, mr), 0) == dall[e, r, 0:1, 0:mr]).astype(f32).astype(bf16)
            begin = e * tile + r * mr
            moved = mm(group, adj[begin:begin + mr, :], rows_rows).astype(bf16)
            for x in range(ne):
                begin = x * tile + r * mr + e * slots
                sorted_adj[begin:begin + slots, :] = moved[x * slots:(x + 1) * slots, :]

    arrive(f_copies)
    c_copies = [[] for _ in range(cuts)]

    def send_column(a, h):
        rows = pl.ds(h * cut, cut)
        for b in (0, 1):
            if (a, b) != (0, 0):
                c_copies[h].append(send(csend.at[a, flip(me_r, b), rows], crecv.at[me_e, me_r, rows], 0, a, b))

    for a in (2, 3, 1, 0):
        column = mm(sorted_adj[span(flip(me_e, a) * tile, tile), :], fall[...], plain).astype(bf16)
        for b in range(nr):
            csend[a, b] = column[b * mr:(b + 1) * mr, :]
        send_column(a, 0)
    for h in range(1, cuts):
        for a in (2, 3, 1, 0):
            send_column(a, h)
    crecv[me_e, me_r] = csend[0, me_r]

    arrive(kz)
    own, far = pl.ds(0, mr), pl.ds(mr, mr)
    near, last = pl.ds(2 * mr, mr), pl.ds(3 * mr, mr)
    kd = [send(kg.at[own], kg.at[far], 2, 0, 0), send(kg.at[own], kg.at[near], 1, 0, 0)]

    def turn(index, carry):
        q, s = index // nd, lax.rem(index, nd)
        turned[span(s * tile, tile), span(q * tile, tile)] = sorted_adj[span(q * tile, tile), span(s * tile, tile)].T
        return carry

    lax.fori_loop(0, ne * nd, turn, 0)
    arrive(w_copies)
    arrive(kd)
    kd = [send(kg.at[far], kg.at[last], 1, 0, 0)]
    for w in range(2):
        for j in range(2):
            ga[w, j] = mm(kg[w * mr:(w + 1) * mr, :], wout[j], cols_cols)

    def hidden(tokens, grad_act, j):
        pre = mm(tokens, win[j], plain)
        tangent = jnp.tanh(gelu_scale * (pre + gelu_cubic * pre * pre * pre))
        act = (0.5 * pre * (1.0 + tangent)).astype(bf16)
        slope = 0.5 * (1.0 + tangent) + 0.5 * pre * (1.0 - tangent * tangent) * gelu_scale * (
            1.0 + 3.0 * gelu_cubic * pre * pre)
        return act, (grad_act * slope).astype(bf16)

    def work(w, h):
        begin = w * mr + h * cut
        rows = pl.ds(begin, cut)
        tokens = tg[rows, :]
        total = None
        for j in range(2):
            act, grad_hidden = hidden(tokens, ga[w, j, h * cut:(h + 1) * cut, :], j)
            if j == 0:
                acts[rows, :] = act
                ghid[rows, :] = grad_hidden
            else:
                acts_far[rows, :] = act
            term = mm(grad_hidden, win[j], cols_cols)
            total = term if total is None else total + term
        return total

    aggs, scales, td, gd = [], [], [], []
    for h in range(cuts):
        arrive(c_copies[h])
        halves = []
        for r in range(nr):
            total = crecv[0, r, h * cut:(h + 1) * cut, :].astype(f32)
            for e in range(1, ne):
                total = total + crecv[e, r, h * cut:(h + 1) * cut, :].astype(f32)
            halves.append(total)
        agg = jnp.concatenate(halves, axis=1).astype(bf16).astype(f32)
        scale = lax.rsqrt(jnp.mean(agg * agg, axis=-1, keepdims=True) + epsilon)
        tg[h * cut:(h + 1) * cut, :] = (agg * scale).astype(bf16)
        td.append(send(tg.at[pl.ds(h * cut, cut)], tg.at[pl.ds(mr + h * cut, cut)], 2, 0, 0))
        aggs.append(agg)
        scales.append(scale)
        if h == 0:
            gown[0:cut, :] = work(0, 0)
    tn = [send(tg.at[own], tg.at[near], 1, 0, 0)]
    arrive(kd)
    kxc = [send(kg, kx, 0, 0, 1)]
    for h in range(cuts):
        arrive([td[h]])
        rows = pl.ds(h * cut, cut)
        gsend[rows, :] = work(1, h).astype(bf16)
        gd.append(send(gsend.at[rows], grecv.at[rows], 2, 0, 0))
        if h + 1 < cuts:
            gown[(h + 1) * cut:(h + 2) * cut, :] = work(0, h + 1)
    tn.append(send(tg.at[far], tg.at[last], 1, 0, 0))

    p_copies = []
    for h in range(cuts):
        arrive([gd[h]])
        rows = slice(h * cut, (h + 1) * cut)
        agg, scale = aggs[h], scales[h]
        back = (gown[rows, :] + grecv[rows, :].astype(f32)).astype(bf16).astype(f32)
        dot_mean = jnp.mean(agg * back, axis=-1, keepdims=True)
        grad_agg = (kg[rows, :].astype(f32) + scale * back - agg * (scale * scale * scale) * dot_mean).astype(bf16)
        for r in range(nr):
            asend[r, rows, :] = grad_agg[:, r * half:(r + 1) * half]
        there = span(me_e * tile + me_r * mr + h * cut, cut)
        for a, b in pair_steps:
            p_copies.append(send(asend.at[flip(me_r, b), pl.ds(h * cut, cut)], gall.at[there], 0, a, b))
        gall[there, :] = asend[me_r, rows, :]

    def outputs(w):
        rows = slice(w * mr, (w + 1) * mr)
        return mm(acts[rows, :], wout[0], plain) + mm(acts_far[rows, :], wout[1], plain)

    osend[...] = outputs(1).astype(bf16)
    od = [send(osend, orecv, 2, 0, 0)]
    oown[...] = outputs(0)
    arrive(tn)
    txc = [send(tg, tx, 0, 0, 1)]
    act, grad_hidden = hidden(tg[2 * mr:, :], mm(kg[2 * mr:, :], wout[0], cols_cols), 0)
    acts[2 * mr:, :] = act
    ghid[2 * mr:, :] = grad_hidden
    gwi[0] = mm(tg[...], ghid[...], rows_rows)
    gwo[0] = mm(acts[...], kg[...], rows_rows)

    arrive(od)
    agg = jnp.concatenate(aggs, axis=0)
    routed = (oown[...] + orecv[...].astype(f32)).astype(bf16).astype(f32)
    ored[...] = (agg + routed).astype(bf16)
    oz = [send(ored.at[span(flip(me_e, a) * slots, slots)], oback.at[here], 0, a, 0) for a in (2, 3, 1)]
    oback[here, :] = ored[here, :]

    arrive(p_copies)
    b_copies = []
    for k in (3, 2, 1, 0):
        term = mm(turned[span(flip(me_d, k) * tile, tile), :], gall[...], plain)
        bsend[k] = term.astype(bf16)
        if k > 0:
            b_copies.append(send(bsend.at[k], brecv.at[k - 1], k, 0, 0))
    arrive(kxc)
    arrive(txc)
    act, grad_hidden = hidden(tx[...], mm(kx[...], wout[0], cols_cols), 0)
    gwi[0] += mm(tx[...], grad_hidden, rows_rows)
    gwo[0] += mm(act, kx[...], rows_rows)
    arrive(oz)
    out[...] = mm(place, oback[...], plain).astype(bf16)
    arrive(b_copies)
    total = bsend[0].astype(f32)
    for k in range(1, nd):
        total = total + brecv[k - 1].astype(f32)
    gf[...] = total
    for copy in pending:
        copy.wait_send()


def paired(nd, ne, nr, slots, features, tile_values, tile_pairs, dispatch, w_in, w_out, cotangent):
    tile, half = features.shape
    tps = tile_values.shape[3]
    mr, width = cotangent.shape
    inner = w_in.shape[2]
    rows = nd * mr
    cuts = 2
    vm = pltpu.VMEM
    count = 8 + 3 + 3 + 2 + 8 * cuts * 2 + 2 * cuts + 24
    scratch = [
        vm((nd, tps, tile, tile), bf16), pltpu.SMEM(tile_pairs.shape, jnp.int32), vm(dispatch.shape, jnp.int32),
        vm((mr, width), bf16), vm((2, width, inner), bf16), vm((2, inner, width), bf16),
        vm((nd * tile, half), bf16), vm((ne * tile, nd * tile), bf16), vm((ne * tile, nd * tile), bf16),
        vm((nd * tile, ne * tile), bf16), vm((8, 128), jnp.int32), vm((ne, nr, 8, 128), jnp.int32),
        vm((ne, nr, mr, half), bf16), vm((ne, nr, mr, half), bf16),
        vm((mr, width), bf16), vm((rows, width), bf16), vm((rows, width), bf16),
        vm((rows, width), bf16), vm((rows, width), bf16),
        vm((2, 2, mr, inner), f32), vm((rows, inner), bf16), vm((rows, inner), bf16), vm((2 * mr, inner), bf16),
        vm((mr, width), f32), vm((mr, width), bf16), vm((mr, width), bf16),
        vm((mr, width), f32), vm((mr, width), bf16), vm((mr, width), bf16), vm((mr, width), bf16), vm((mr, width), bf16),
        vm((nr, mr, half), bf16), vm((ne * tile, half), bf16),
        vm((nd, tile, half), bf16), vm((nd - 1, tile, half), bf16),
        pltpu.SemaphoreType.DMA((7,)), pltpu.SemaphoreType.DMA((count,)), pltpu.SemaphoreType.DMA((count,)),
    ]
    in_vmem = pl.BlockSpec(memory_space=pltpu.VMEM)
    in_hbm = pl.BlockSpec(memory_space=pl.ANY)
    arguments = (features, tile_values, tile_pairs, dispatch, w_in, w_out, cotangent)
    return leave(pl.pallas_call(
        functools.partial(body_paired, (nd, ne, nr, slots, cuts)),
        name="layer",
        out_shape=(
            vm((mr, width), bf16), vm((tile, half), f32), vm((1, width, inner), f32), vm((1, inner, width), f32),
        ),
        in_specs=[in_hbm] * 7,
        out_specs=[in_vmem] * 4,
        scratch_shapes=scratch,
        compiler_params=pltpu.CompilerParams(
            collective_id=0, has_side_effects=True, vmem_limit_bytes=56 * 1024 * 1024
        ),
    )(*[pltpu.with_memory_space_constraint(a, pltpu.HBM) for a in arguments]))


def store(*refs):
    count = len(refs) // 2
    copies = [pltpu.make_async_copy(refs[n], refs[count + n], refs[-1].at[n]) for n in range(count)]
    for copy in copies:
        copy.start()
    for copy in copies:
        copy.wait()


def leave(arrays):
    arrays = [pltpu.with_memory_space_constraint(a, pltpu.VMEM) for a in arrays]
    return pl.pallas_call(
        store,
        name="leave",
        out_shape=tuple(jax.ShapeDtypeStruct(a.shape, a.dtype) for a in arrays),
        in_specs=[pl.BlockSpec(memory_space=pltpu.VMEM)] * len(arrays),
        out_specs=[pl.BlockSpec(memory_space=pl.ANY)] * len(arrays),
        scratch_shapes=[pltpu.SemaphoreType.DMA((len(arrays),))],
    )(*arrays)


def on_device(nd, ne, nr, features, tile_values, tile_pairs, dispatch, w_in, w_out, cotangent):
    tile, half = features.shape
    tps = tile_values.shape[3]
    mr, width = cotangent.shape
    inner = w_in.shape[2]
    own = mr // ne
    slots = -(-own // 16) * 16
    if (nd, ne, nr) == (4, 4, 2) and slots == own and mr <= 128:
        return paired(nd, ne, nr, slots, features, tile_values, tile_pairs, dispatch, w_in, w_out, cotangent)
    if slots != own:
        dispatch = jnp.pad(dispatch.reshape(ne, own), ((0, 0), (0, slots - own)), constant_values=-1).reshape(1, -1)
    seg = ne * slots
    rows = nd * seg
    chunk = min(rows, 256)
    keep_turned = ne * nd <= 64
    dma = pltpu.SemaphoreType.DMA
    vm = pltpu.VMEM
    scratch = [
        vm((nd, tps, tile, tile), bf16), vm((width, inner), bf16), vm((inner, width), bf16),
        vm((width, inner), f32), vm((inner, width), f32),
        vm((nd * tile, half), bf16), vm((ne * tile, nd * tile), bf16),
        vm((nd * tile, ne * tile) if keep_turned else (16, 128), bf16),
        vm((ne, nr, mr, half), bf16), vm((ne, nr, mr, half), bf16),
        vm((seg, width), bf16), vm((rows, width), bf16), vm((nr - 1, rows, width), bf16),
        vm((seg, width), bf16), vm((rows, width), bf16), vm((nr - 1, rows, width), bf16),
        vm((rows, width), bf16), vm((nd, seg, width), bf16), vm((seg, width), bf16), vm((seg, width), bf16),
        vm((rows, width), bf16), vm((nd, seg, width), bf16), vm((seg, width), bf16), vm((seg, width), bf16),
        vm((nr, mr, half), bf16), vm((ne * tile, half), bf16),
        vm((nd, tile, half), bf16), vm((nd, tile, half), bf16),
        vm((chunk, inner), f32), vm((chunk, inner), bf16), vm((chunk, inner), bf16),
        dma((5,)),
    ]
    for count in (nd - 1, ne * nr - 1, ne - 1, nd - 1, nr - 1, ne - 1, nd - 1, nr - 1,
                  nd - 1, ne - 1, nd - 1, ne - 1, ne * nr - 1, nd - 1):
        scratch += [dma((count,)), dma((count,))]
    in_vmem = pl.BlockSpec(memory_space=pltpu.VMEM)
    in_hbm = pl.BlockSpec(memory_space=pl.ANY)
    return placed(pl.pallas_call(
        functools.partial(body, (nd, ne, nr, slots, chunk, keep_turned)),
        name="layer",
        out_shape=(
            jax.ShapeDtypeStruct((mr, width), bf16),
            jax.ShapeDtypeStruct((tile, half), f32),
            jax.ShapeDtypeStruct((1, width, inner), f32),
            jax.ShapeDtypeStruct((1, inner, width), f32),
        ),
        in_specs=[in_vmem, in_hbm, pl.BlockSpec(memory_space=pltpu.SMEM), in_vmem, in_hbm, in_hbm, in_vmem],
        out_specs=[in_vmem, in_vmem, in_hbm, in_hbm],
        scratch_shapes=scratch,
        compiler_params=pltpu.CompilerParams(
            collective_id=0, has_side_effects=True, vmem_limit_bytes=60 * 1024 * 1024
        ),
    )(features, tile_values, tile_pairs, dispatch, w_in, w_out, cotangent))


def hand_over(pieces, *refs):
    count = len(refs) // 3
    sources, targets, held = refs[:count], refs[count:2 * count], refs[2 * count:3 * count]
    come, go = refs[3 * count:]
    cuts = []
    for source, target, middle, number in zip(sources, targets, held, pieces):
        size = source.shape[-2] // number
        for piece in range(number):
            where = (0,) * (len(source.shape) - 2) + (pl.ds(piece * size, size),)
            n = len(cuts)
            cuts.append((
                pltpu.make_async_copy(source.at[where], middle.at[where], come.at[n]),
                pltpu.make_async_copy(middle.at[where], target.at[where], go.at[n]),
            ))
    for first, _ in cuts:
        first.start()
    for first, second in cuts:
        first.wait()
        second.start()
    for _, second in cuts:
        second.wait()


def placed(arrays):
    in_hbm = pl.BlockSpec(memory_space=pl.ANY)
    pieces = tuple(4 if a.size * a.dtype.itemsize >= 2 ** 19 else 1 for a in arrays)
    return pl.pallas_call(
        functools.partial(hand_over, pieces),
        name="hand_over",
        out_shape=tuple(jax.ShapeDtypeStruct(a.shape, a.dtype) for a in arrays),
        in_specs=[in_hbm] * len(arrays),
        out_specs=[in_hbm] * len(arrays),
        scratch_shapes=[pltpu.VMEM(a.shape, a.dtype) for a in arrays]
        + [pltpu.SemaphoreType.DMA((sum(pieces),)), pltpu.SemaphoreType.DMA((sum(pieces),))],
    )(*arrays)


def solution(mesh):
    in_specs = (
        P(("dom", "expert"), "rep"),
        P("dom", "expert", None, None, None, None),
        P("dom", "expert", None, None),
        P(("dom", "expert", "rep"), None),
        P("expert", None, "dom"),
        P("expert", "dom", None),
        P(("dom", "expert", "rep"), None),
    )
    out_specs = (
        P(("dom", "expert", "rep"), None),
        P(("dom", "expert"), "rep"),
        P("expert", None, "dom"),
        P("expert", "dom", None),
    )
    sizes = (mesh.shape["dom"], mesh.shape["expert"], mesh.shape["rep"])
    return jax.shard_map(
        functools.partial(on_device, *sizes), mesh=mesh, in_specs=in_specs, out_specs=out_specs, check_vma=False
    )
```

```python
import functools

import jax
import jax.numpy as jnp
from jax import lax
from jax.experimental import pallas as pl
from jax.experimental.pallas import tpu as pltpu
from jax.sharding import PartitionSpec as P

epsilon = 1e-06
gelu_scale = 0.7978845608028654
gelu_cubic = 0.044715
bf16 = jnp.bfloat16
f32 = jnp.float32


def mm(left, right, dims):
    return lax.dot_general(left, right, (dims, ((), ())), preferred_element_type=f32)


plain = ((1,), (0,))
rows_rows = ((0,), (0,))
cols_cols = ((1,), (1,))


def body(sizes, *refs):
    nd, ne, nr, slots, chunk, keep_turned = sizes
    (feat, tv_hbm, pairs, disp, win_hbm, wout_hbm, cot,
     out, gf, gwi_hbm, gwo_hbm,
     tv, win, wout, gwi, gwo, fall, adj, turned, csend, crecv,
     tsend, tg, tx, ksend, kg, kx,
     gsend, grecv, gred, gback, osend, orecv, ored, oback,
     asend, gall, bsend, brecv, ga, acts, ghid,
     lsem, fs, fr, cs, cr, tzs, tzr, tds, tdr, txs, txr, kzs, kzr, kds, kdr, kxs, kxr,
     gds, gdr, gzs, gzr, ods, odr, ozs, ozr, ps, pr, bs, br) = refs
    me_d, me_e, me_r = lax.axis_index("dom"), lax.axis_index("expert"), lax.axis_index("rep")
    tile = feat.shape[0]
    half = feat.shape[1]
    tps = tv.shape[1]
    mr = cot.shape[0]
    seg = ne * slots
    rows = nd * seg
    pending = []

    def ring(me, step, count):
        return lax.rem(me + step, count)

    def send(src, dst, ssem, rsem, d, e, r):
        copy = pltpu.make_async_remote_copy(
            src_ref=src, dst_ref=dst, send_sem=ssem, recv_sem=rsem,
            device_id={"dom": d, "expert": e, "rep": r},
            device_id_type=pl.DeviceIdType.MESH,
        )
        copy.start()
        pending.append(copy)
        return copy

    def local(src, dst, index):
        copy = pltpu.make_async_copy(src, dst, lsem.at[index])
        copy.start()
        return copy

    def arrive(copies):
        for copy in copies:
            copy.wait_recv()

    def span(start, size):
        return pl.ds(pl.multiple_of(start, size), size)

    load_tv = local(tv_hbm.at[0, 0], tv, 0)
    load_wout = local(wout_hbm.at[0], wout, 1)
    load_win = local(win_hbm.at[0], win, 2)

    dom_steps = list(range(1, nd))
    flips = nd & (nd - 1) == 0

    def dom_to(k):
        if not flips:
            return ring(me_d, k, nd)
        place, bit = me_d, 1
        while bit < nd:
            if k & bit:
                place = place + bit - 2 * bit * lax.rem(me_d // bit, 2)
            bit *= 2
        return place

    def dom_from(k):
        return dom_to(k) if flips else ring(me_d, nd - k, nd)

    exp_steps = list(range(1, ne))
    pair_steps = [(a, b) for a in range(ne) for b in range(nr) if (a, b) != (0, 0)]

    barrier = pltpu.get_barrier_semaphore()
    for k in dom_steps:
        pl.semaphore_signal(barrier, inc=1, device_id={"dom": dom_to(k), "expert": me_e, "rep": me_r},
                            device_id_type=pl.DeviceIdType.MESH)
    for a, b in pair_steps:
        pl.semaphore_signal(barrier, inc=1,
                            device_id={"dom": me_d, "expert": ring(me_e, a, ne), "rep": ring(me_r, b, nr)},
                            device_id_type=pl.DeviceIdType.MESH)

    place = (lax.broadcasted_iota(jnp.int32, (mr, seg), 0) == disp[...]).astype(f32).astype(bf16)
    fall[span(me_d * tile, tile), :] = feat[...]
    ksend[...] = mm(place, cot[...], rows_rows).astype(bf16)
    load_tv.wait()

    def build(index, carry):
        q, s = index // nd, lax.rem(index, nd)
        total = jnp.zeros((tile, tile), f32)
        for k in range(tps):
            hit = jnp.where(pairs[0, 0, s, k] == q, 1.0, 0.0).astype(f32)
            total = total + tv[s, k].astype(f32) * hit
        adj[span(q * tile, tile), span(s * tile, tile)] = total.astype(bf16)
        return carry

    lax.fori_loop(0, ne * nd, build, 0)
    pl.semaphore_wait(barrier, len(dom_steps) + len(pair_steps))

    f_copies = [
        send(feat, fall.at[span(me_d * tile, tile)], fs.at[k - 1], fr.at[k - 1], dom_to(k), me_e, me_r)
        for k in dom_steps
    ]

    def to_experts(source, target, ssem, rsem):
        copies = []
        for k in exp_steps:
            x = ring(me_e, k, ne)
            copies.append(send(source.at[span(x * slots, slots)], target.at[span((me_d * ne + me_e) * slots, slots)],
                               ssem.at[k - 1], rsem.at[k - 1], me_d, x, me_r))
        mine = span((me_d * ne + me_e) * slots, slots)
        target[mine, :] = source[span(me_e * slots, slots), :]
        return copies

    def to_doms(target, ssem, rsem):
        block = target.at[span(me_d * seg, seg)]
        return [send(block, block, ssem.at[k - 1], rsem.at[k - 1], dom_to(k), me_e, me_r) for k in dom_steps]

    def to_reps(source, target, ssem, rsem):
        return [send(source, target.at[k - 1], ssem.at[k - 1], rsem.at[k - 1], me_d, me_e, ring(me_r, k, nr))
                for k in range(1, nr)]

    kz = to_experts(ksend, kg, kzs, kzr)

    def turn(index, carry):
        q, s = index // nd, lax.rem(index, nd)
        turned[span(s * tile, tile), span(q * tile, tile)] = adj[span(q * tile, tile), span(s * tile, tile)].T
        return carry


    arrive(f_copies)
    c_copies = []
    for a in list(range(1, ne)) + [0]:
        q = ring(me_e, a, ne)
        column = mm(adj[span(q * tile, tile), :], fall[...], plain).astype(bf16)
        for b in range(nr):
            csend[q, b] = column[b * mr:(b + 1) * mr, :]
        for b in range(nr):
            r = ring(me_r, b, nr)
            if (a, b) != (0, 0):
                n = a * nr + b - 1
                c_copies.append(send(csend.at[q, r], crecv.at[me_e, me_r], cs.at[n], cr.at[n], me_d, q, r))
    crecv[me_e, me_r] = csend[me_e, me_r]

    arrive(kz)
    kd = to_doms(kg, kds, kdr)
    load_wout.wait()
    load_win.wait()
    if keep_turned:
        lax.fori_loop(0, ne * nd, turn, 0)
    arrive(kd)
    whole_rows = rows == chunk
    if whole_rows:
        ga[...] = mm(kg[...], wout[...], cols_cols)

    arrive(c_copies)
    parts = []
    for r in range(nr):
        total = crecv[0, r].astype(f32)
        for e in range(1, ne):
            total = total + crecv[e, r].astype(f32)
        parts.append(total)
    agg = jnp.concatenate(parts, axis=1).astype(bf16).astype(f32)
    width = agg.shape[1]
    scale = lax.rsqrt(jnp.mean(agg * agg, axis=-1, keepdims=True) + epsilon)
    normed = (agg * scale).astype(bf16)
    tsend[...] = mm(place, normed, rows_rows).astype(bf16)
    tz = to_experts(tsend, tg, tzs, tzr)
    kxc = to_reps(kg, kx, kxs, kxr)
    arrive(tz)
    td = to_doms(tg, tds, tdr)

    def hidden(tokens, grad_act):
        pre = mm(tokens, win[...], plain)
        tangent = jnp.tanh(gelu_scale * (pre + gelu_cubic * pre * pre * pre))
        act = (0.5 * pre * (1.0 + tangent)).astype(bf16)
        slope = 0.5 * (1.0 + tangent) + 0.5 * pre * (1.0 - tangent * tangent) * gelu_scale * (
            1.0 + 3.0 * gelu_cubic * pre * pre)
        return act, (grad_act * slope).astype(bf16)

    def add_grads(tokens, grads, act, grad_hidden, first):
        one = mm(tokens, grad_hidden, rows_rows)
        two = mm(act, grads, rows_rows)
        if first:
            gwi[...] = one
            gwo[...] = two
        else:
            gwi[...] += one
            gwo[...] += two

    def scatter(source, target, ssem, rsem):
        copies = [
            send(source.at[span(dom_to(k) * seg, seg)], target.at[me_d], ssem.at[k - 1], rsem.at[k - 1],
                 dom_to(k), me_e, me_r)
            for k in dom_steps
        ]
        target[me_d] = source[span(me_d * seg, seg), :]
        return copies

    if whole_rows:
        gd = []
        for k in [0] + dom_steps:
            if k > 0:
                arrive([td[k - 1]])
            d = dom_from(k)
            where = span(d * seg, seg)
            act, grad_hidden = hidden(tg[where, :], ga[where, :])
            term = mm(grad_hidden, win[...], cols_cols).astype(bf16)
            acts[where, :] = act
            ghid[where, :] = grad_hidden
            if k == 0:
                grecv[me_d] = term
            else:
                gsend[where, :] = term
                gd.append(send(gsend.at[where], grecv.at[me_d], gds.at[k - 1], gdr.at[k - 1], d, me_e, me_r))
        txc = to_reps(tg, tx, txs, txr)
        osend[...] = mm(acts[...], wout[...], plain).astype(bf16)
        add_grads(tg[...], kg[...], acts[...], ghid[...], True)
    else:
        arrive(td)
        txc = to_reps(tg, tx, txs, txr)
        gwi[...] = jnp.zeros_like(gwi)
        gwo[...] = jnp.zeros_like(gwo)

        def one_chunk(index, carry):
            where = span(index * chunk, chunk)
            act, grad_hidden = hidden(tg[where, :], mm(kg[where, :], wout[...], cols_cols))
            gsend[where, :] = mm(grad_hidden, win[...], cols_cols).astype(bf16)
            osend[where, :] = mm(act, wout[...], plain).astype(bf16)
            add_grads(tg[where, :], kg[where, :], act, grad_hidden, False)
            return carry

        lax.fori_loop(0, rows // chunk, one_chunk, 0)
        gd = scatter(gsend, grecv, gds, gdr)

    def summed(target):
        total = target[0].astype(f32)
        for d in range(1, nd):
            total = total + target[d].astype(f32)
        return total.astype(bf16)

    def to_nodes(source, target, ssem, rsem):
        copies = []
        for k in exp_steps:
            e = ring(me_e, k, ne)
            copies.append(send(source.at[span(e * slots, slots)], target.at[span(me_e * slots, slots)],
                               ssem.at[k - 1], rsem.at[k - 1], me_d, e, me_r))
        mine = span(me_e * slots, slots)
        target[mine, :] = source[mine, :]
        return copies

    arrive(gd)
    gred[...] = summed(grecv)
    gz = to_nodes(gred, gback, gzs, gzr)
    od = scatter(osend, orecv, ods, odr)

    arrive(gz)
    back = mm(place, gback[...], plain)
    dot_mean = jnp.mean(agg * back, axis=-1, keepdims=True)
    grad_agg = (cot[...].astype(f32) + scale * back - agg * (scale * scale * scale) * dot_mean).astype(bf16)
    for r in range(nr):
        asend[r] = grad_agg[:, r * half:(r + 1) * half]
    here = span(me_e * tile + me_r * mr, mr)
    p_copies = []
    for a, b in pair_steps:
        n = a * nr + b - 1
        r = ring(me_r, b, nr)
        p_copies.append(send(asend.at[r], gall.at[here], ps.at[n], pr.at[n], me_d, ring(me_e, a, ne), r))
    gall[here, :] = asend[me_r]

    arrive(kxc)
    arrive(txc)
    for n in range(nr - 1):
        if whole_rows:
            act, grad_hidden = hidden(tx[n], mm(kx[n], wout[...], cols_cols))
            add_grads(tx[n], kx[n], act, grad_hidden, False)
        else:
            def other_chunk(index, carry):
                where = span(index * chunk, chunk)
                act, grad_hidden = hidden(tx[n, where, :], mm(kx[n, where, :], wout[...], cols_cols))
                add_grads(tx[n, where, :], kx[n, where, :], act, grad_hidden, False)
                return carry

            lax.fori_loop(0, rows // chunk, other_chunk, 0)
    store_i = local(gwi, gwi_hbm.at[0], 3)
    store_o = local(gwo, gwo_hbm.at[0], 4)

    arrive(od)
    ored[...] = summed(orecv)
    arrive(p_copies)
    oz = to_nodes(ored, oback, ozs, ozr)
    b_copies = []
    for k in dom_steps[::-1] + [0]:
        s = dom_to(k)
        if keep_turned:
            term = mm(turned[span(s * tile, tile), :], gall[...], plain)
        else:
            term = mm(adj[:, span(s * tile, tile)], gall[...], rows_rows)
        if k > 0:
            bsend[s] = term.astype(bf16)
            b_copies.append(send(bsend.at[s], brecv.at[me_d], bs.at[k - 1], br.at[k - 1], s, me_e, me_r))
        else:
            brecv[me_d] = term.astype(bf16)
    arrive(oz)
    out[...] = (agg + mm(place, oback[...], plain)).astype(bf16)
    arrive(b_copies)
    total = brecv[0].astype(f32)
    for d in range(1, nd):
        total = total + brecv[d].astype(f32)
    gf[...] = total
    store_i.wait()
    store_o.wait()
    for copy in pending:
        copy.wait_send()


def flip(me, k):
    place, bit = me, 1
    while bit <= k:
        if k & bit:
            place = place + bit - 2 * bit * lax.rem(me // bit, 2)
        bit *= 2
    return place


def body_paired(sizes, *refs):
    nd, ne, nr, slots, cuts = sizes
    (feat_hbm, tv_hbm, pairs_hbm, disp_hbm, win_hbm, wout_hbm, cot_hbm,
     out, gf, gwi, gwo,
     tv, pairs, disp, cot, win, wout, fall, adj, sorted_adj, turned, dsend, dall, csend, crecv,
     ksend, kg, kx, tg, tx, ga, acts, ghid, acts_far, gown, gsend, grecv, oown, osend, orecv, ored, oback,
     asend, gall, bsend, brecv, sent, lsem, ssem, rsem) = refs
    me_d, me_e, me_r = lax.axis_index("dom"), lax.axis_index("expert"), lax.axis_index("rep")
    tile, half = fall.shape[0] // nd, fall.shape[1]
    tps = tv.shape[1]
    mr, width = cot.shape
    inner = win.shape[2]
    cut = mr // cuts
    groups = {}

    def copy_of(src, dst, d, e, r, group):
        return pltpu.make_async_remote_copy(
            src_ref=src, dst_ref=dst, send_sem=ssem.at[0], recv_sem=rsem.at[groups.setdefault(group, len(groups))],
            device_id={"dom": flip(me_d, d), "expert": flip(me_e, e), "rep": flip(me_r, r)},
            device_id_type=pl.DeviceIdType.MESH,
        )

    def send(src, dst, d, e, r, group):
        copy_of(src, dst, d, e, r, group).start()

    def local(src, dst, index):
        copy = pltpu.make_async_copy(src, dst, lsem.at[index])
        copy.start()
        return copy

    def arrive(group, ref):
        copy_of(ref, ref, 0, 0, 0, group).wait_recv()

    def span(start, size):
        return pl.ds(pl.multiple_of(start, size), size)

    pair_steps = [(a, b) for a in (2, 3, 1, 0) for b in range(nr) if (a, b) != (0, 0)]
    barrier = pltpu.get_barrier_semaphore()
    for k in range(1, nd):
        pl.semaphore_signal(barrier, inc=1, device_id={"dom": flip(me_d, k), "expert": me_e, "rep": me_r},
                            device_id_type=pl.DeviceIdType.MESH)
    for a, b in pair_steps:
        pl.semaphore_signal(barrier, inc=1,
                            device_id={"dom": me_d, "expert": flip(me_e, a), "rep": flip(me_r, b)},
                            device_id_type=pl.DeviceIdType.MESH)
    own_feat = fall.at[span(me_d * tile, tile)]
    load_feat = local(feat_hbm, own_feat, 0)
    load_disp = local(disp_hbm, disp, 1)
    load_cot = local(cot_hbm, cot, 2)
    load_pairs = local(pairs_hbm, pairs, 3)
    load_tv = local(tv_hbm.at[0, 0], tv, 4)
    load_win = local(win_hbm.at[0], win.at[0], 5)
    load_wout = local(wout_hbm.at[0], wout.at[0], 6)

    load_disp.wait()
    dsend[...] = jnp.zeros_like(dsend)
    dsend[:, 0:mr] = jnp.broadcast_to(disp[...], (dsend.shape[0], mr))
    dall[me_e * nr + me_r] = dsend[...]
    load_feat.wait()
    pl.semaphore_wait(barrier, nd - 1 + len(pair_steps))
    for k in (2, 3):
        send(own_feat, own_feat, k, 0, 0, "features")
    for a, b in pair_steps:
        send(dsend, dall.at[me_e * nr + me_r], 0, a, b, "order")
    send(own_feat, own_feat, 1, 0, 0, "features")

    place = (lax.broadcasted_iota(jnp.int32, (mr, ne * slots), 0) == disp[...]).astype(f32).astype(bf16)
    load_cot.wait()
    ksend[...] = mm(place, cot[...], rows_rows).astype(bf16)
    here = span(me_e * slots, slots)
    for a in (2, 3, 1):
        send(ksend.at[span(flip(me_e, a) * slots, slots)], kg.at[here], 0, a, 0, "cotangent")
    kg[here, :] = ksend[here, :]
    load_pairs.wait()
    load_tv.wait()

    def build(index, carry):
        q, s = index // nd, lax.rem(index, nd)
        total = jnp.zeros((tile, tile), f32)
        for k in range(tps):
            hit = jnp.where(pairs[0, 0, s, k] == q, 1.0, 0.0).astype(f32)
            total = total + tv[s, k].astype(f32) * hit
        adj[span(q * tile, tile), span(s * tile, tile)] = total.astype(bf16)
        return carry

    lax.fori_loop(0, ne * nd, build, 0)
    load_win.wait()
    load_wout.wait()
    send(win.at[0], win.at[1], 1, 0, 0, "weights")
    send(wout.at[0], wout.at[1], 1, 0, 0, "weights")

    arrive("order", dall.at[pl.ds(0, ne * nr - 1)])
    for e in range(ne):
        for r in range(nr):
            group = (lax.broadcasted_iota(jnp.int32, (mr, mr), 0) == dall[e * nr + r, 0:1, 0:mr]).astype(f32).astype(bf16)
            begin = e * tile + r * mr
            moved = mm(group, adj[begin:begin + mr, :], rows_rows).astype(bf16)
            for x in range(ne):
                begin = x * tile + r * mr + e * slots
                sorted_adj[begin:begin + slots, :] = moved[x * slots:(x + 1) * slots, :]

    arrive("features", fall.at[pl.ds(0, (nd - 1) * tile)])

    def send_column(a, h):
        rows = pl.ds(h * cut, cut)
        for b in (0, 1):
            if (a, b) != (0, 0):
                send(csend.at[a * nr + flip(me_r, b), rows], crecv.at[me_e * nr + me_r, rows], 0, a, b, ("column", h))

    for a in (2, 3, 1, 0):
        column = mm(sorted_adj[span(flip(me_e, a) * tile, tile), :], fall[...], plain).astype(bf16)
        for b in range(nr):
            csend[a * nr + b] = column[b * mr:(b + 1) * mr, :]
        send_column(a, 0)
    for h in range(1, cuts):
        for a in (2, 3, 1, 0):
            send_column(a, h)
    crecv[me_e * nr + me_r] = csend[me_r]

    arrive("cotangent", kg.at[pl.ds(0, (ne - 1) * slots)])
    own, far = pl.ds(0, mr), pl.ds(mr, mr)
    near, last = pl.ds(2 * mr, mr), pl.ds(3 * mr, mr)
    send(kg.at[own], kg.at[far], 2, 0, 0, "far cotangent")
    send(kg.at[own], kg.at[near], 1, 0, 0, "near cotangent")

    def turn(index, carry):
        q, s = index // nd, lax.rem(index, nd)
        turned[span(s * tile, tile), span(q * tile, tile)] = sorted_adj[span(q * tile, tile), span(s * tile, tile)].T
        return carry

    lax.fori_loop(0, ne * nd, turn, 0)
    arrive("weights", win.at[pl.ds(0, 2)])
    arrive("far cotangent", kg.at[far])
    send(kg.at[far], kg.at[last], 1, 0, 0, "near cotangent")
    for w in range(2):
        for j in range(2):
            ga[w, j] = mm(kg[w * mr:(w + 1) * mr, :], wout[j], cols_cols)

    def hidden(tokens, grad_act, j):
        pre = mm(tokens, win[j], plain)
        tangent = jnp.tanh(gelu_scale * (pre + gelu_cubic * pre * pre * pre))
        act = (0.5 * pre * (1.0 + tangent)).astype(bf16)
        slope = 0.5 * (1.0 + tangent) + 0.5 * pre * (1.0 - tangent * tangent) * gelu_scale * (
            1.0 + 3.0 * gelu_cubic * pre * pre)
        return act, (grad_act * slope).astype(bf16)

    def work(w, h):
        begin = w * mr + h * cut
        rows = pl.ds(begin, cut)
        tokens = tg[rows, :]
        total = None
        for j in range(2):
            act, grad_hidden = hidden(tokens, ga[w, j, h * cut:(h + 1) * cut, :], j)
            if j == 0:
                acts[rows, :] = act
                ghid[rows, :] = grad_hidden
            else:
                acts_far[rows, :] = act
            term = mm(grad_hidden, win[j], cols_cols)
            total = term if total is None else total + term
        return total

    aggs, scales = [], []
    for h in range(cuts):
        arrive(("column", h), crecv.at[pl.ds(0, ne * nr - 1), pl.ds(0, cut)])
        halves = []
        for r in range(nr):
            total = crecv[r, h * cut:(h + 1) * cut, :].astype(f32)
            for e in range(1, ne):
                total = total + crecv[e * nr + r, h * cut:(h + 1) * cut, :].astype(f32)
            halves.append(total)
        agg = jnp.concatenate(halves, axis=1).astype(bf16).astype(f32)
        scale = lax.rsqrt(jnp.mean(agg * agg, axis=-1, keepdims=True) + epsilon)
        tg[h * cut:(h + 1) * cut, :] = (agg * scale).astype(bf16)
        send(tg.at[pl.ds(h * cut, cut)], tg.at[pl.ds(mr + h * cut, cut)], 2, 0, 0, ("tokens", h))
        aggs.append(agg)
        scales.append(scale)
        if h == 0:
            gown[0:cut, :] = work(0, 0)
    send(tg.at[own], tg.at[near], 1, 0, 0, "near tokens")
    arrive("near cotangent", kg.at[pl.ds(0, 2 * mr)])
    send(kg, kx, 0, 0, 1, "across")
    for h in range(cuts):
        arrive(("tokens", h), tg.at[pl.ds(0, cut)])
        rows = pl.ds(h * cut, cut)
        gsend[rows, :] = work(1, h).astype(bf16)
        send(gsend.at[rows], grecv.at[rows], 2, 0, 0, ("terms", h))
        if h + 1 < cuts:
            gown[(h + 1) * cut:(h + 2) * cut, :] = work(0, h + 1)
    send(tg.at[far], tg.at[last], 1, 0, 0, "near tokens")

    for h in range(cuts):
        arrive(("terms", h), grecv.at[pl.ds(0, cut)])
        rows = slice(h * cut, (h + 1) * cut)
        agg, scale = aggs[h], scales[h]
        back = (gown[rows, :] + grecv[rows, :].astype(f32)).astype(bf16).astype(f32)
        dot_mean = jnp.mean(agg * back, axis=-1, keepdims=True)
        grad_agg = (kg[rows, :].astype(f32) + scale * back - agg * (scale * scale * scale) * dot_mean).astype(bf16)
        for r in range(nr):
            asend[r, rows, :] = grad_agg[:, r * half:(r + 1) * half]
        there = span(me_e * tile + me_r * mr + h * cut, cut)
        for a, b in pair_steps:
            send(asend.at[flip(me_r, b), pl.ds(h * cut, cut)], gall.at[there], 0, a, b, "gradients")
        gall[there, :] = asend[me_r, rows, :]

    def outputs(w):
        rows = slice(w * mr, (w + 1) * mr)
        return mm(acts[rows, :], wout[0], plain) + mm(acts_far[rows, :], wout[1], plain)

    osend[...] = outputs(1).astype(bf16)
    send(osend, orecv, 2, 0, 0, "halves")
    oown[...] = outputs(0)
    arrive("near tokens", tg.at[pl.ds(0, 2 * mr)])
    send(tg, tx, 0, 0, 1, "across")
    act, grad_hidden = hidden(tg[2 * mr:, :], mm(kg[2 * mr:, :], wout[0], cols_cols), 0)
    acts[2 * mr:, :] = act
    ghid[2 * mr:, :] = grad_hidden
    gwi[0] = mm(tg[...], ghid[...], rows_rows)
    gwo[0] = mm(acts[...], kg[...], rows_rows)

    arrive("halves", orecv)
    agg = jnp.concatenate(aggs, axis=0)
    routed = (oown[...] + orecv[...].astype(f32)).astype(bf16).astype(f32)
    ored[...] = (agg + routed).astype(bf16)
    for a in (2, 3, 1):
        send(ored.at[span(flip(me_e, a) * slots, slots)], oback.at[here], 0, a, 0, "results")
    oback[here, :] = ored[here, :]

    arrive("gradients", gall.at[pl.ds(0, (ne * nr - 1) * mr)])
    for k in (3, 2, 1, 0):
        term = mm(turned[span(flip(me_d, k) * tile, tile), :], gall[...], plain)
        bsend[k] = term.astype(bf16)
        if k > 0:
            send(bsend.at[k], brecv.at[k - 1], k, 0, 0, "backterms")
    arrive("across", win.at[0])
    act, grad_hidden = hidden(tx[...], mm(kx[...], wout[0], cols_cols), 0)
    gwi[0] += mm(tx[...], grad_hidden, rows_rows)
    gwo[0] += mm(act, kx[...], rows_rows)
    arrive("results", oback.at[pl.ds(0, (ne - 1) * slots)])
    out[...] = mm(place, oback[...], plain).astype(bf16)
    arrive("backterms", brecv)
    total = bsend[0].astype(f32)
    for k in range(1, nd):
        total = total + brecv[k - 1].astype(f32)
    gf[...] = total
    copy_of(sent, sent, 0, 0, 0, "features").wait_send()


def paired(nd, ne, nr, slots, features, tile_values, tile_pairs, dispatch, w_in, w_out, cotangent):
    tile, half = features.shape
    tps = tile_values.shape[3]
    mr, width = cotangent.shape
    inner = w_in.shape[2]
    rows = nd * mr
    cuts = 2
    vm = pltpu.VMEM
    steps = ne * nr - 1
    words = (2 * (nd - 1) * tile * half + 2 * steps * 8 * 128 + 2 * (ne - 1) * slots * width + 2 * width * inner
             + 2 * steps * mr * half + 8 * mr * width + 2 * rows * width)
    scratch = [
        vm((nd, tps, tile, tile), bf16), pltpu.SMEM(tile_pairs.shape, jnp.int32), vm(dispatch.shape, jnp.int32),
        vm((mr, width), bf16), vm((2, width, inner), bf16), vm((2, inner, width), bf16),
        vm((nd * tile, half), bf16), vm((ne * tile, nd * tile), bf16), vm((ne * tile, nd * tile), bf16),
        vm((nd * tile, ne * tile), bf16), vm((8, 128), jnp.int32), vm((ne * nr, 8, 128), jnp.int32),
        vm((ne * nr, mr, half), bf16), vm((ne * nr, mr, half), bf16),
        vm((mr, width), bf16), vm((rows, width), bf16), vm((rows, width), bf16),
        vm((rows, width), bf16), vm((rows, width), bf16),
        vm((2, 2, mr, inner), f32), vm((rows, inner), bf16), vm((rows, inner), bf16), vm((2 * mr, inner), bf16),
        vm((mr, width), f32), vm((mr, width), bf16), vm((mr, width), bf16),
        vm((mr, width), f32), vm((mr, width), bf16), vm((mr, width), bf16), vm((mr, width), bf16), vm((mr, width), bf16),
        vm((nr, mr, half), bf16), vm((ne * tile, half), bf16),
        vm((nd, tile, half), bf16), vm((nd - 1, tile, half), bf16),
        vm((words // 128, 128), bf16),
        pltpu.SemaphoreType.DMA((7,)), pltpu.SemaphoreType.DMA((1,)), pltpu.SemaphoreType.DMA((15 + 3 * (cuts - 1),)),
    ]
    in_vmem = pl.BlockSpec(memory_space=pltpu.VMEM)
    in_hbm = pl.BlockSpec(memory_space=pl.ANY)
    arguments = (features, tile_values, tile_pairs, dispatch, w_in, w_out, cotangent)
    return leave(pl.pallas_call(
        functools.partial(body_paired, (nd, ne, nr, slots, cuts)),
        name="layer",
        out_shape=(
            vm((mr, width), bf16), vm((tile, half), f32), vm((1, width, inner), f32), vm((1, inner, width), f32),
        ),
        in_specs=[in_hbm] * 7,
        out_specs=[in_vmem] * 4,
        scratch_shapes=scratch,
        compiler_params=pltpu.CompilerParams(
            collective_id=0, has_side_effects=True, vmem_limit_bytes=56 * 1024 * 1024
        ),
    )(*[pltpu.with_memory_space_constraint(a, pltpu.HBM) for a in arguments]))


def store(*refs):
    count = len(refs) // 2
    copies = [pltpu.make_async_copy(refs[n], refs[count + n], refs[-1].at[n]) for n in range(count)]
    for copy in copies:
        copy.start()
    for copy in copies:
        copy.wait()


def leave(arrays):
    arrays = [pltpu.with_memory_space_constraint(a, pltpu.VMEM) for a in arrays]
    return pl.pallas_call(
        store,
        name="leave",
        out_shape=tuple(jax.ShapeDtypeStruct(a.shape, a.dtype) for a in arrays),
        in_specs=[pl.BlockSpec(memory_space=pltpu.VMEM)] * len(arrays),
        out_specs=[pl.BlockSpec(memory_space=pl.ANY)] * len(arrays),
        scratch_shapes=[pltpu.SemaphoreType.DMA((len(arrays),))],
    )(*arrays)


def on_device(nd, ne, nr, features, tile_values, tile_pairs, dispatch, w_in, w_out, cotangent):
    tile, half = features.shape
    tps = tile_values.shape[3]
    mr, width = cotangent.shape
    inner = w_in.shape[2]
    own = mr // ne
    slots = -(-own // 16) * 16
    if (nd, ne, nr) == (4, 4, 2) and slots == own and mr <= 128:
        return paired(nd, ne, nr, slots, features, tile_values, tile_pairs, dispatch, w_in, w_out, cotangent)
    if slots != own:
        dispatch = jnp.pad(dispatch.reshape(ne, own), ((0, 0), (0, slots - own)), constant_values=-1).reshape(1, -1)
    seg = ne * slots
    rows = nd * seg
    chunk = min(rows, 256)
    keep_turned = ne * nd <= 64
    dma = pltpu.SemaphoreType.DMA
    vm = pltpu.VMEM
    scratch = [
        vm((nd, tps, tile, tile), bf16), vm((width, inner), bf16), vm((inner, width), bf16),
        vm((width, inner), f32), vm((inner, width), f32),
        vm((nd * tile, half), bf16), vm((ne * tile, nd * tile), bf16),
        vm((nd * tile, ne * tile) if keep_turned else (16, 128), bf16),
        vm((ne, nr, mr, half), bf16), vm((ne, nr, mr, half), bf16),
        vm((seg, width), bf16), vm((rows, width), bf16), vm((nr - 1, rows, width), bf16),
        vm((seg, width), bf16), vm((rows, width), bf16), vm((nr - 1, rows, width), bf16),
        vm((rows, width), bf16), vm((nd, seg, width), bf16), vm((seg, width), bf16), vm((seg, width), bf16),
        vm((rows, width), bf16), vm((nd, seg, width), bf16), vm((seg, width), bf16), vm((seg, width), bf16),
        vm((nr, mr, half), bf16), vm((ne * tile, half), bf16),
        vm((nd, tile, half), bf16), vm((nd, tile, half), bf16),
        vm((chunk, inner), f32), vm((chunk, inner), bf16), vm((chunk, inner), bf16),
        dma((5,)),
    ]
    for count in (nd - 1, ne * nr - 1, ne - 1, nd - 1, nr - 1, ne - 1, nd - 1, nr - 1,
                  nd - 1, ne - 1, nd - 1, ne - 1, ne * nr - 1, nd - 1):
        scratch += [dma((count,)), dma((count,))]
    in_vmem = pl.BlockSpec(memory_space=pltpu.VMEM)
    in_hbm = pl.BlockSpec(memory_space=pl.ANY)
    return placed(pl.pallas_call(
        functools.partial(body, (nd, ne, nr, slots, chunk, keep_turned)),
        name="layer",
        out_shape=(
            jax.ShapeDtypeStruct((mr, width), bf16),
            jax.ShapeDtypeStruct((tile, half), f32),
            jax.ShapeDtypeStruct((1, width, inner), f32),
            jax.ShapeDtypeStruct((1, inner, width), f32),
        ),
        in_specs=[in_vmem, in_hbm, pl.BlockSpec(memory_space=pltpu.SMEM), in_vmem, in_hbm, in_hbm, in_vmem],
        out_specs=[in_vmem, in_vmem, in_hbm, in_hbm],
        scratch_shapes=scratch,
        compiler_params=pltpu.CompilerParams(
            collective_id=0, has_side_effects=True, vmem_limit_bytes=60 * 1024 * 1024
        ),
    )(features, tile_values, tile_pairs, dispatch, w_in, w_out, cotangent))


def hand_over(pieces, *refs):
    count = len(refs) // 3
    sources, targets, held = refs[:count], refs[count:2 * count], refs[2 * count:3 * count]
    come, go = refs[3 * count:]
    cuts = []
    for source, target, middle, number in zip(sources, targets, held, pieces):
        size = source.shape[-2] // number
        for piece in range(number):
            where = (0,) * (len(source.shape) - 2) + (pl.ds(piece * size, size),)
            n = len(cuts)
            cuts.append((
                pltpu.make_async_copy(source.at[where], middle.at[where], come.at[n]),
                pltpu.make_async_copy(middle.at[where], target.at[where], go.at[n]),
            ))
    for first, _ in cuts:
        first.start()
    for first, second in cuts:
        first.wait()
        second.start()
    for _, second in cuts:
        second.wait()


def placed(arrays):
    in_hbm = pl.BlockSpec(memory_space=pl.ANY)
    pieces = tuple(4 if a.size * a.dtype.itemsize >= 2 ** 19 else 1 for a in arrays)
    return pl.pallas_call(
        functools.partial(hand_over, pieces),
        name="hand_over",
        out_shape=tuple(jax.ShapeDtypeStruct(a.shape, a.dtype) for a in arrays),
        in_specs=[in_hbm] * len(arrays),
        out_specs=[in_hbm] * len(arrays),
        scratch_shapes=[pltpu.VMEM(a.shape, a.dtype) for a in arrays]
        + [pltpu.SemaphoreType.DMA((sum(pieces),)), pltpu.SemaphoreType.DMA((sum(pieces),))],
    )(*arrays)


def solution(mesh):
    in_specs = (
        P(("dom", "expert"), "rep"),
        P("dom", "expert", None, None, None, None),
        P("dom", "expert", None, None),
        P(("dom", "expert", "rep"), None),
        P("expert", None, "dom"),
        P("expert", "dom", None),
        P(("dom", "expert", "rep"), None),
    )
    out_specs = (
        P(("dom", "expert", "rep"), None),
        P(("dom", "expert"), "rep"),
        P("expert", None, "dom"),
        P("expert", "dom", None),
    )
    sizes = (mesh.shape["dom"], mesh.shape["expert"], mesh.shape["rep"])
    return jax.shard_map(
        functools.partial(on_device, *sizes), mesh=mesh, in_specs=in_specs, out_specs=out_specs, check_vma=False
    )
```

```python
import functools

import jax
import jax.numpy as jnp
from jax import lax
from jax.experimental import pallas as pl
from jax.experimental.pallas import tpu as pltpu
from jax.sharding import PartitionSpec as P

epsilon = 1e-06
gelu_scale = 0.7978845608028654
gelu_cubic = 0.044715
bf16 = jnp.bfloat16
f32 = jnp.float32


def mm(left, right, dims):
    return lax.dot_general(left, right, (dims, ((), ())), preferred_element_type=f32)


plain = ((1,), (0,))
rows_rows = ((0,), (0,))
cols_cols = ((1,), (1,))


def body(sizes, *refs):
    nd, ne, nr, slots, chunk, keep_turned = sizes
    (feat, tv_hbm, pairs, disp, win_hbm, wout_hbm, cot,
     out, gf, gwi_hbm, gwo_hbm,
     tv, win, wout, gwi, gwo, fall, adj, turned, csend, crecv,
     tsend, tg, tx, ksend, kg, kx,
     gsend, grecv, gred, gback, osend, orecv, ored, oback,
     asend, gall, bsend, brecv, ga, acts, ghid,
     lsem, fs, fr, cs, cr, tzs, tzr, tds, tdr, txs, txr, kzs, kzr, kds, kdr, kxs, kxr,
     gds, gdr, gzs, gzr, ods, odr, ozs, ozr, ps, pr, bs, br) = refs
    me_d, me_e, me_r = lax.axis_index("dom"), lax.axis_index("expert"), lax.axis_index("rep")
    tile = feat.shape[0]
    half = feat.shape[1]
    tps = tv.shape[1]
    mr = cot.shape[0]
    seg = ne * slots
    rows = nd * seg
    pending = []

    def ring(me, step, count):
        return lax.rem(me + step, count)

    def send(src, dst, ssem, rsem, d, e, r):
        copy = pltpu.make_async_remote_copy(
            src_ref=src, dst_ref=dst, send_sem=ssem, recv_sem=rsem,
            device_id={"dom": d, "expert": e, "rep": r},
            device_id_type=pl.DeviceIdType.MESH,
        )
        copy.start()
        pending.append(copy)
        return copy

    def local(src, dst, index):
        copy = pltpu.make_async_copy(src, dst, lsem.at[index])
        copy.start()
        return copy

    def arrive(copies):
        for copy in copies:
            copy.wait_recv()

    def span(start, size):
        return pl.ds(pl.multiple_of(start, size), size)

    load_tv = local(tv_hbm.at[0, 0], tv, 0)
    load_wout = local(wout_hbm.at[0], wout, 1)
    load_win = local(win_hbm.at[0], win, 2)

    dom_steps = list(range(1, nd))
    flips = nd & (nd - 1) == 0

    def dom_to(k):
        if not flips:
            return ring(me_d, k, nd)
        place, bit = me_d, 1
        while bit < nd:
            if k & bit:
                place = place + bit - 2 * bit * lax.rem(me_d // bit, 2)
            bit *= 2
        return place

    def dom_from(k):
        return dom_to(k) if flips else ring(me_d, nd - k, nd)

    exp_steps = list(range(1, ne))
    pair_steps = [(a, b) for a in range(ne) for b in range(nr) if (a, b) != (0, 0)]

    barrier = pltpu.get_barrier_semaphore()
    for k in dom_steps:
        pl.semaphore_signal(barrier, inc=1, device_id={"dom": dom_to(k), "expert": me_e, "rep": me_r},
                            device_id_type=pl.DeviceIdType.MESH)
    for a, b in pair_steps:
        pl.semaphore_signal(barrier, inc=1,
                            device_id={"dom": me_d, "expert": ring(me_e, a, ne), "rep": ring(me_r, b, nr)},
                            device_id_type=pl.DeviceIdType.MESH)

    place = (lax.broadcasted_iota(jnp.int32, (mr, seg), 0) == disp[...]).astype(f32).astype(bf16)
    fall[span(me_d * tile, tile), :] = feat[...]
    ksend[...] = mm(place, cot[...], rows_rows).astype(bf16)
    load_tv.wait()

    def build(index, carry):
        q, s = index // nd, lax.rem(index, nd)
        total = jnp.zeros((tile, tile), f32)
        for k in range(tps):
            hit = jnp.where(pairs[0, 0, s, k] == q, 1.0, 0.0).astype(f32)
            total = total + tv[s, k].astype(f32) * hit
        adj[span(q * tile, tile), span(s * tile, tile)] = total.astype(bf16)
        return carry

    lax.fori_loop(0, ne * nd, build, 0)
    pl.semaphore_wait(barrier, len(dom_steps) + len(pair_steps))

    f_copies = [
        send(feat, fall.at[span(me_d * tile, tile)], fs.at[k - 1], fr.at[k - 1], dom_to(k), me_e, me_r)
        for k in dom_steps
    ]

    def to_experts(source, target, ssem, rsem):
        copies = []
        for k in exp_steps:
            x = ring(me_e, k, ne)
            copies.append(send(source.at[span(x * slots, slots)], target.at[span((me_d * ne + me_e) * slots, slots)],
                               ssem.at[k - 1], rsem.at[k - 1], me_d, x, me_r))
        mine = span((me_d * ne + me_e) * slots, slots)
        target[mine, :] = source[span(me_e * slots, slots), :]
        return copies

    def to_doms(target, ssem, rsem):
        block = target.at[span(me_d * seg, seg)]
        return [send(block, block, ssem.at[k - 1], rsem.at[k - 1], dom_to(k), me_e, me_r) for k in dom_steps]

    def to_reps(source, target, ssem, rsem):
        return [send(source, target.at[k - 1], ssem.at[k - 1], rsem.at[k - 1], me_d, me_e, ring(me_r, k, nr))
                for k in range(1, nr)]

    kz = to_experts(ksend, kg, kzs, kzr)

    def turn(index, carry):
        q, s = index // nd, lax.rem(index, nd)
        turned[span(s * tile, tile), span(q * tile, tile)] = adj[span(q * tile, tile), span(s * tile, tile)].T
        return carry


    arrive(f_copies)
    c_copies = []
    for a in list(range(1, ne)) + [0]:
        q = ring(me_e, a, ne)
        column = mm(adj[span(q * tile, tile), :], fall[...], plain).astype(bf16)
        for b in range(nr):
            csend[q, b] = column[b * mr:(b + 1) * mr, :]
        for b in range(nr):
            r = ring(me_r, b, nr)
            if (a, b) != (0, 0):
                n = a * nr + b - 1
                c_copies.append(send(csend.at[q, r], crecv.at[me_e, me_r], cs.at[n], cr.at[n], me_d, q, r))
    crecv[me_e, me_r] = csend[me_e, me_r]

    arrive(kz)
    kd = to_doms(kg, kds, kdr)
    load_wout.wait()
    load_win.wait()
    if keep_turned:
        lax.fori_loop(0, ne * nd, turn, 0)
    arrive(kd)
    whole_rows = rows == chunk
    if whole_rows:
        ga[...] = mm(kg[...], wout[...], cols_cols)

    arrive(c_copies)
    parts = []
    for r in range(nr):
        total = crecv[0, r].astype(f32)
        for e in range(1, ne):
            total = total + crecv[e, r].astype(f32)
        parts.append(total)
    agg = jnp.concatenate(parts, axis=1).astype(bf16).astype(f32)
    width = agg.shape[1]
    scale = lax.rsqrt(jnp.mean(agg * agg, axis=-1, keepdims=True) + epsilon)
    normed = (agg * scale).astype(bf16)
    tsend[...] = mm(place, normed, rows_rows).astype(bf16)
    tz = to_experts(tsend, tg, tzs, tzr)
    kxc = to_reps(kg, kx, kxs, kxr)
    arrive(tz)
    td = to_doms(tg, tds, tdr)

    def hidden(tokens, grad_act):
        pre = mm(tokens, win[...], plain)
        tangent = jnp.tanh(gelu_scale * (pre + gelu_cubic * pre * pre * pre))
        act = (0.5 * pre * (1.0 + tangent)).astype(bf16)
        slope = 0.5 * (1.0 + tangent) + 0.5 * pre * (1.0 - tangent * tangent) * gelu_scale * (
            1.0 + 3.0 * gelu_cubic * pre * pre)
        return act, (grad_act * slope).astype(bf16)

    def add_grads(tokens, grads, act, grad_hidden, first):
        one = mm(tokens, grad_hidden, rows_rows)
        two = mm(act, grads, rows_rows)
        if first:
            gwi[...] = one
            gwo[...] = two
        else:
            gwi[...] += one
            gwo[...] += two

    def scatter(source, target, ssem, rsem):
        copies = [
            send(source.at[span(dom_to(k) * seg, seg)], target.at[me_d], ssem.at[k - 1], rsem.at[k - 1],
                 dom_to(k), me_e, me_r)
            for k in dom_steps
        ]
        target[me_d] = source[span(me_d * seg, seg), :]
        return copies

    if whole_rows:
        gd = []
        for k in [0] + dom_steps:
            if k > 0:
                arrive([td[k - 1]])
            d = dom_from(k)
            where = span(d * seg, seg)
            act, grad_hidden = hidden(tg[where, :], ga[where, :])
            term = mm(grad_hidden, win[...], cols_cols).astype(bf16)
            acts[where, :] = act
            ghid[where, :] = grad_hidden
            if k == 0:
                grecv[me_d] = term
            else:
                gsend[where, :] = term
                gd.append(send(gsend.at[where], grecv.at[me_d], gds.at[k - 1], gdr.at[k - 1], d, me_e, me_r))
        txc = to_reps(tg, tx, txs, txr)
        osend[...] = mm(acts[...], wout[...], plain).astype(bf16)
        add_grads(tg[...], kg[...], acts[...], ghid[...], True)
    else:
        arrive(td)
        txc = to_reps(tg, tx, txs, txr)
        gwi[...] = jnp.zeros_like(gwi)
        gwo[...] = jnp.zeros_like(gwo)

        def one_chunk(index, carry):
            where = span(index * chunk, chunk)
            act, grad_hidden = hidden(tg[where, :], mm(kg[where, :], wout[...], cols_cols))
            gsend[where, :] = mm(grad_hidden, win[...], cols_cols).astype(bf16)
            osend[where, :] = mm(act, wout[...], plain).astype(bf16)
            add_grads(tg[where, :], kg[where, :], act, grad_hidden, False)
            return carry

        lax.fori_loop(0, rows // chunk, one_chunk, 0)
        gd = scatter(gsend, grecv, gds, gdr)

    def summed(target):
        total = target[0].astype(f32)
        for d in range(1, nd):
            total = total + target[d].astype(f32)
        return total.astype(bf16)

    def to_nodes(source, target, ssem, rsem):
        copies = []
        for k in exp_steps:
            e = ring(me_e, k, ne)
            copies.append(send(source.at[span(e * slots, slots)], target.at[span(me_e * slots, slots)],
                               ssem.at[k - 1], rsem.at[k - 1], me_d, e, me_r))
        mine = span(me_e * slots, slots)
        target[mine, :] = source[mine, :]
        return copies

    arrive(gd)
    gred[...] = summed(grecv)
    gz = to_nodes(gred, gback, gzs, gzr)
    od = scatter(osend, orecv, ods, odr)

    arrive(gz)
    back = mm(place, gback[...], plain)
    dot_mean = jnp.mean(agg * back, axis=-1, keepdims=True)
    grad_agg = (cot[...].astype(f32) + scale * back - agg * (scale * scale * scale) * dot_mean).astype(bf16)
    for r in range(nr):
        asend[r] = grad_agg[:, r * half:(r + 1) * half]
    here = span(me_e * tile + me_r * mr, mr)
    p_copies = []
    for a, b in pair_steps:
        n = a * nr + b - 1
        r = ring(me_r, b, nr)
        p_copies.append(send(asend.at[r], gall.at[here], ps.at[n], pr.at[n], me_d, ring(me_e, a, ne), r))
    gall[here, :] = asend[me_r]

    arrive(kxc)
    arrive(txc)
    for n in range(nr - 1):
        if whole_rows:
            act, grad_hidden = hidden(tx[n], mm(kx[n], wout[...], cols_cols))
            add_grads(tx[n], kx[n], act, grad_hidden, False)
        else:
            def other_chunk(index, carry):
                where = span(index * chunk, chunk)
                act, grad_hidden = hidden(tx[n, where, :], mm(kx[n, where, :], wout[...], cols_cols))
                add_grads(tx[n, where, :], kx[n, where, :], act, grad_hidden, False)
                return carry

            lax.fori_loop(0, rows // chunk, other_chunk, 0)
    store_i = local(gwi, gwi_hbm.at[0], 3)
    store_o = local(gwo, gwo_hbm.at[0], 4)

    arrive(od)
    ored[...] = summed(orecv)
    arrive(p_copies)
    oz = to_nodes(ored, oback, ozs, ozr)
    b_copies = []
    for k in dom_steps[::-1] + [0]:
        s = dom_to(k)
        if keep_turned:
            term = mm(turned[span(s * tile, tile), :], gall[...], plain)
        else:
            term = mm(adj[:, span(s * tile, tile)], gall[...], rows_rows)
        if k > 0:
            bsend[s] = term.astype(bf16)
            b_copies.append(send(bsend.at[s], brecv.at[me_d], bs.at[k - 1], br.at[k - 1], s, me_e, me_r))
        else:
            brecv[me_d] = term.astype(bf16)
    arrive(oz)
    out[...] = (agg + mm(place, oback[...], plain)).astype(bf16)
    arrive(b_copies)
    total = brecv[0].astype(f32)
    for d in range(1, nd):
        total = total + brecv[d].astype(f32)
    gf[...] = total
    store_i.wait()
    store_o.wait()
    for copy in pending:
        copy.wait_send()


def flip(me, k):
    place, bit = me, 1
    while bit <= k:
        if k & bit:
            place = place + bit - 2 * bit * lax.rem(me // bit, 2)
        bit *= 2
    return place


def body_paired(sizes, *refs):
    nd, ne, nr, slots, cuts = sizes
    (feat_hbm, tv_hbm, pairs_hbm, disp_hbm, win_hbm, wout_hbm, cot_hbm,
     out, gf, gwi, gwo,
     tv, pairs, disp, cot, win, wout, fall, adj, sorted_adj, turned, dsend, dall, csend, crecv,
     ksend, kg, kx, tg, tx, ga, acts, ghid, acts_far, gown, gsend, grecv, oown, osend, orecv, ored, oback,
     asend, gall, bsend, brecv, sent, ready, lsem, ssem, rsem) = refs
    me_d, me_e, me_r = lax.axis_index("dom"), lax.axis_index("expert"), lax.axis_index("rep")
    tile, half = fall.shape[0] // nd, fall.shape[1]
    tps = tv.shape[1]
    mr, width = cot.shape
    inner = win.shape[2]
    cut = mr // cuts
    groups = {}

    def copy_of(src, dst, d, e, r, group):
        return pltpu.make_async_remote_copy(
            src_ref=src, dst_ref=dst, send_sem=ssem.at[0], recv_sem=rsem.at[groups.setdefault(group, len(groups))],
            device_id={"dom": flip(me_d, d), "expert": flip(me_e, e), "rep": flip(me_r, r)},
            device_id_type=pl.DeviceIdType.MESH,
        )

    def send(src, dst, d, e, r, group):
        copy_of(src, dst, d, e, r, group).start()

    def local(src, dst, index):
        copy = pltpu.make_async_copy(src, dst, lsem.at[index])
        copy.start()
        return copy

    def arrive(group, ref):
        copy_of(ref, ref, 0, 0, 0, group).wait_recv()

    def span(start, size):
        return pl.ds(pl.multiple_of(start, size), size)

    pair_steps = [(a, b) for a in (2, 3, 1, 0) for b in range(nr) if (a, b) != (0, 0)]
    barrier = pltpu.get_barrier_semaphore()
    core = lax.rem(me_d, 2)

    def tell(semaphore, d, e, r):
        pl.semaphore_signal(semaphore, inc=1,
                            device_id={"dom": flip(me_d, d), "expert": flip(me_e, e), "rep": flip(me_r, r)},
                            device_id_type=pl.DeviceIdType.MESH)

    @pl.when(core == 0)
    def _():
        tell(barrier, 2, 0, 0)
        for a, b in pair_steps:
            tell(barrier, 1, a, b)

    @pl.when(core == 1)
    def _():
        tell(barrier, 1, 0, 0)
        tell(barrier, 3, 0, 0)
        for a, b in pair_steps:
            tell(barrier, 0, a, b)

    own_feat = fall.at[span(me_d * tile, tile)]
    load_feat = local(feat_hbm, own_feat, 0)
    load_disp = local(disp_hbm, disp, 1)
    load_cot = local(cot_hbm, cot, 2)
    load_pairs = local(pairs_hbm, pairs, 3)
    load_tv = local(tv_hbm.at[0, 0], tv, 4)
    load_win = local(win_hbm.at[0], win.at[0], 5)
    load_wout = local(wout_hbm.at[0], wout.at[0], 6)

    load_disp.wait()
    dsend[...] = jnp.zeros_like(dsend)
    dsend[:, 0:mr] = jnp.broadcast_to(disp[...], (dsend.shape[0], mr))
    dall[me_e * nr + me_r] = dsend[...]
    load_feat.wait()

    @pl.when(core == 0)
    def _():
        pl.semaphore_wait(barrier, nd - 1)
        tell(ready.at[0], 1, 0, 0)

    @pl.when(core == 1)
    def _():
        pl.semaphore_wait(ready.at[0], 1)

    for k in (2, 3, 1):
        send(own_feat, own_feat, k, 0, 0, "features")

    @pl.when(core == 1)
    def _():
        pl.semaphore_wait(barrier, 2 * len(pair_steps))
        tell(ready.at[1], 1, 0, 0)

    @pl.when(core == 0)
    def _():
        pl.semaphore_wait(ready.at[1], 1)

    for a, b in pair_steps:
        send(dsend, dall.at[me_e * nr + me_r], 0, a, b, "order")

    place = (lax.broadcasted_iota(jnp.int32, (mr, ne * slots), 0) == disp[...]).astype(f32).astype(bf16)
    load_cot.wait()
    ksend[...] = mm(place, cot[...], rows_rows).astype(bf16)
    here = span(me_e * slots, slots)
    for a in (2, 3, 1):
        send(ksend.at[span(flip(me_e, a) * slots, slots)], kg.at[here], 0, a, 0, "cotangent")
    kg[here, :] = ksend[here, :]
    load_pairs.wait()
    load_tv.wait()

    def build(index, carry):
        q, s = index // nd, lax.rem(index, nd)
        total = jnp.zeros((tile, tile), f32)
        for k in range(tps):
            hit = jnp.where(pairs[0, 0, s, k] == q, 1.0, 0.0).astype(f32)
            total = total + tv[s, k].astype(f32) * hit
        adj[span(q * tile, tile), span(s * tile, tile)] = total.astype(bf16)
        return carry

    lax.fori_loop(0, ne * nd, build, 0)
    load_win.wait()
    load_wout.wait()
    send(win.at[0], win.at[1], 1, 0, 0, "weights")
    send(wout.at[0], wout.at[1], 1, 0, 0, "weights")

    arrive("order", dall.at[pl.ds(0, ne * nr - 1)])
    for e in range(ne):
        for r in range(nr):
            group = (lax.broadcasted_iota(jnp.int32, (mr, mr), 0) == dall[e * nr + r, 0:1, 0:mr]).astype(f32).astype(bf16)
            begin = e * tile + r * mr
            moved = mm(group, adj[begin:begin + mr, :], rows_rows).astype(bf16)
            for x in range(ne):
                begin = x * tile + r * mr + e * slots
                sorted_adj[begin:begin + slots, :] = moved[x * slots:(x + 1) * slots, :]

    arrive("features", fall.at[pl.ds(0, (nd - 1) * tile)])

    def send_column(a, h):
        rows = pl.ds(h * cut, cut)
        for b in (0, 1):
            if (a, b) != (0, 0):
                send(csend.at[a * nr + flip(me_r, b), rows], crecv.at[me_e * nr + me_r, rows], 0, a, b, ("column", h))

    for a in (2, 3, 1, 0):
        column = mm(sorted_adj[span(flip(me_e, a) * tile, tile), :], fall[...], plain).astype(bf16)
        for b in range(nr):
            csend[a * nr + b] = column[b * mr:(b + 1) * mr, :]
        send_column(a, 0)
    for h in range(1, cuts):
        for a in (2, 3, 1, 0):
            send_column(a, h)
    crecv[me_e * nr + me_r] = csend[me_r]

    arrive("cotangent", kg.at[pl.ds(0, (ne - 1) * slots)])
    own, far = pl.ds(0, mr), pl.ds(mr, mr)
    near, last = pl.ds(2 * mr, mr), pl.ds(3 * mr, mr)
    send(kg.at[own], kg.at[far], 2, 0, 0, "far cotangent")
    send(kg.at[own], kg.at[near], 1, 0, 0, "near cotangent")

    def turn(index, carry):
        q, s = index // nd, lax.rem(index, nd)
        turned[span(s * tile, tile), span(q * tile, tile)] = sorted_adj[span(q * tile, tile), span(s * tile, tile)].T
        return carry

    lax.fori_loop(0, ne * nd, turn, 0)
    arrive("weights", win.at[pl.ds(0, 2)])
    arrive("far cotangent", kg.at[far])
    send(kg.at[far], kg.at[last], 1, 0, 0, "near cotangent")
    pair, other = pl.ds(0, 2 * mr), pl.ds(2 * mr, 2 * mr)
    send(kg.at[pair], kx.at[pair], 0, 0, 1, "across cotangent")
    for w in range(2):
        for j in range(2):
            ga[w, j] = mm(kg[w * mr:(w + 1) * mr, :], wout[j], cols_cols)

    def hidden(tokens, grad_act, j):
        pre = mm(tokens, win[j], plain)
        tangent = jnp.tanh(gelu_scale * (pre + gelu_cubic * pre * pre * pre))
        act = (0.5 * pre * (1.0 + tangent)).astype(bf16)
        slope = 0.5 * (1.0 + tangent) + 0.5 * pre * (1.0 - tangent * tangent) * gelu_scale * (
            1.0 + 3.0 * gelu_cubic * pre * pre)
        return act, (grad_act * slope).astype(bf16)

    def work(w, h):
        begin = w * mr + h * cut
        rows = pl.ds(begin, cut)
        tokens = tg[rows, :]
        total = None
        for j in range(2):
            act, grad_hidden = hidden(tokens, ga[w, j, h * cut:(h + 1) * cut, :], j)
            if j == 0:
                acts[rows, :] = act
                ghid[rows, :] = grad_hidden
            else:
                acts_far[rows, :] = act
            term = mm(grad_hidden, win[j], cols_cols)
            total = term if total is None else total + term
        return total

    aggs, scales = [], []
    for h in range(cuts):
        arrive(("column", h), crecv.at[pl.ds(0, ne * nr - 1), pl.ds(0, cut)])
        halves = []
        for r in range(nr):
            total = crecv[r, h * cut:(h + 1) * cut, :].astype(f32)
            for e in range(1, ne):
                total = total + crecv[e * nr + r, h * cut:(h + 1) * cut, :].astype(f32)
            halves.append(total)
        agg = jnp.concatenate(halves, axis=1).astype(bf16).astype(f32)
        scale = lax.rsqrt(jnp.mean(agg * agg, axis=-1, keepdims=True) + epsilon)
        tg[h * cut:(h + 1) * cut, :] = (agg * scale).astype(bf16)
        send(tg.at[pl.ds(h * cut, cut)], tg.at[pl.ds(mr + h * cut, cut)], 2, 0, 0, ("tokens", h))
        aggs.append(agg)
        scales.append(scale)
        if h == 0:
            gown[0:cut, :] = work(0, 0)
    send(tg.at[own], tg.at[near], 1, 0, 0, "near tokens")
    for h in range(cuts):
        arrive(("tokens", h), tg.at[pl.ds(0, cut)])
        rows = pl.ds(h * cut, cut)
        gsend[rows, :] = work(1, h).astype(bf16)
        send(gsend.at[rows], grecv.at[rows], 2, 0, 0, ("terms", h))
        if h + 1 < cuts:
            gown[(h + 1) * cut:(h + 2) * cut, :] = work(0, h + 1)
    send(tg.at[pair], tx.at[pair], 0, 0, 1, "across tokens")
    send(tg.at[far], tg.at[last], 1, 0, 0, "near tokens")
    arrive("across cotangent", kx.at[pair])
    send(kx.at[pair], kx.at[other], 1, 0, 0, "near across")

    for h in range(cuts):
        arrive(("terms", h), grecv.at[pl.ds(0, cut)])
        rows = slice(h * cut, (h + 1) * cut)
        agg, scale = aggs[h], scales[h]
        back = (gown[rows, :] + grecv[rows, :].astype(f32)).astype(bf16).astype(f32)
        dot_mean = jnp.mean(agg * back, axis=-1, keepdims=True)
        grad_agg = (kg[rows, :].astype(f32) + scale * back - agg * (scale * scale * scale) * dot_mean).astype(bf16)
        for r in range(nr):
            asend[r, rows, :] = grad_agg[:, r * half:(r + 1) * half]
        there = span(me_e * tile + me_r * mr + h * cut, cut)
        for a, b in pair_steps:
            send(asend.at[flip(me_r, b), pl.ds(h * cut, cut)], gall.at[there], 0, a, b, "gradients")
        gall[there, :] = asend[me_r, rows, :]

    def outputs(w):
        rows = slice(w * mr, (w + 1) * mr)
        return mm(acts[rows, :], wout[0], plain) + mm(acts_far[rows, :], wout[1], plain)

    osend[...] = outputs(1).astype(bf16)
    send(osend, orecv, 2, 0, 0, "halves")
    oown[...] = outputs(0)
    arrive("near cotangent", kg.at[pair])
    arrive("near tokens", tg.at[pair])
    act, grad_hidden = hidden(tg[2 * mr:, :], mm(kg[2 * mr:, :], wout[0], cols_cols), 0)
    acts[2 * mr:, :] = act
    ghid[2 * mr:, :] = grad_hidden
    gwi[0] = mm(tg[...], ghid[...], rows_rows)
    gwo[0] = mm(acts[...], kg[...], rows_rows)

    arrive("across tokens", tx.at[pair])
    send(tx.at[pair], tx.at[other], 1, 0, 0, "near across")
    arrive("halves", orecv)
    agg = jnp.concatenate(aggs, axis=0)
    routed = (oown[...] + orecv[...].astype(f32)).astype(bf16).astype(f32)
    ored[...] = (agg + routed).astype(bf16)
    for a in (2, 3, 1):
        send(ored.at[span(flip(me_e, a) * slots, slots)], oback.at[here], 0, a, 0, "results")
    oback[here, :] = ored[here, :]

    arrive("gradients", gall.at[pl.ds(0, (ne * nr - 1) * mr)])
    for k in (3, 2, 1, 0):
        term = mm(turned[span(flip(me_d, k) * tile, tile), :], gall[...], plain)
        bsend[k] = term.astype(bf16)
        if k > 0:
            send(bsend.at[k], brecv.at[k - 1], k, 0, 0, "backterms")
    arrive("near across", kx)
    act, grad_hidden = hidden(tx[...], mm(kx[...], wout[0], cols_cols), 0)
    gwi[0] += mm(tx[...], grad_hidden, rows_rows)
    gwo[0] += mm(act, kx[...], rows_rows)
    arrive("results", oback.at[pl.ds(0, (ne - 1) * slots)])
    out[...] = mm(place, oback[...], plain).astype(bf16)
    arrive("backterms", brecv)
    total = bsend[0].astype(f32)
    for k in range(1, nd):
        total = total + brecv[k - 1].astype(f32)
    gf[...] = total
    copy_of(sent, sent, 0, 0, 0, "features").wait_send()


def paired(nd, ne, nr, slots, features, tile_values, tile_pairs, dispatch, w_in, w_out, cotangent):
    tile, half = features.shape
    tps = tile_values.shape[3]
    mr, width = cotangent.shape
    inner = w_in.shape[2]
    rows = nd * mr
    cuts = 2
    vm = pltpu.VMEM
    steps = ne * nr - 1
    words = (2 * (nd - 1) * tile * half + 2 * steps * 8 * 128 + 2 * (ne - 1) * slots * width + 2 * width * inner
             + 2 * steps * mr * half + 8 * mr * width + 2 * rows * width)
    scratch = [
        vm((nd, tps, tile, tile), bf16), pltpu.SMEM(tile_pairs.shape, jnp.int32), vm(dispatch.shape, jnp.int32),
        vm((mr, width), bf16), vm((2, width, inner), bf16), vm((2, inner, width), bf16),
        vm((nd * tile, half), bf16), vm((ne * tile, nd * tile), bf16), vm((ne * tile, nd * tile), bf16),
        vm((nd * tile, ne * tile), bf16), vm((8, 128), jnp.int32), vm((ne * nr, 8, 128), jnp.int32),
        vm((ne * nr, mr, half), bf16), vm((ne * nr, mr, half), bf16),
        vm((mr, width), bf16), vm((rows, width), bf16), vm((rows, width), bf16),
        vm((rows, width), bf16), vm((rows, width), bf16),
        vm((2, 2, mr, inner), f32), vm((rows, inner), bf16), vm((rows, inner), bf16), vm((2 * mr, inner), bf16),
        vm((mr, width), f32), vm((mr, width), bf16), vm((mr, width), bf16),
        vm((mr, width), f32), vm((mr, width), bf16), vm((mr, width), bf16), vm((mr, width), bf16), vm((mr, width), bf16),
        vm((nr, mr, half), bf16), vm((ne * tile, half), bf16),
        vm((nd, tile, half), bf16), vm((nd - 1, tile, half), bf16),
        vm((words // 128, 128), bf16),
        pltpu.SemaphoreType.REGULAR((2,)), pltpu.SemaphoreType.DMA((7,)), pltpu.SemaphoreType.DMA((1,)), pltpu.SemaphoreType.DMA((17 + 3 * (cuts - 1),)),
    ]
    in_vmem = pl.BlockSpec(memory_space=pltpu.VMEM)
    in_hbm = pl.BlockSpec(memory_space=pl.ANY)
    arguments = (features, tile_values, tile_pairs, dispatch, w_in, w_out, cotangent)
    return leave(pl.pallas_call(
        functools.partial(body_paired, (nd, ne, nr, slots, cuts)),
        name="layer",
        out_shape=(
            vm((mr, width), bf16), vm((tile, half), f32), vm((1, width, inner), f32), vm((1, inner, width), f32),
        ),
        in_specs=[in_hbm] * 7,
        out_specs=[in_vmem] * 4,
        scratch_shapes=scratch,
        compiler_params=pltpu.CompilerParams(
            collective_id=0, has_side_effects=True, vmem_limit_bytes=56 * 1024 * 1024
        ),
    )(*[pltpu.with_memory_space_constraint(a, pltpu.HBM) for a in arguments]))


def store(*refs):
    count = len(refs) // 2
    copies = [pltpu.make_async_copy(refs[n], refs[count + n], refs[-1].at[n]) for n in range(count)]
    for copy in copies:
        copy.start()
    for copy in copies:
        copy.wait()


def leave(arrays):
    arrays = [pltpu.with_memory_space_constraint(a, pltpu.VMEM) for a in arrays]
    return pl.pallas_call(
        store,
        name="leave",
        out_shape=tuple(jax.ShapeDtypeStruct(a.shape, a.dtype) for a in arrays),
        in_specs=[pl.BlockSpec(memory_space=pltpu.VMEM)] * len(arrays),
        out_specs=[pl.BlockSpec(memory_space=pl.ANY)] * len(arrays),
        scratch_shapes=[pltpu.SemaphoreType.DMA((len(arrays),))],
    )(*arrays)


def on_device(nd, ne, nr, features, tile_values, tile_pairs, dispatch, w_in, w_out, cotangent):
    tile, half = features.shape
    tps = tile_values.shape[3]
    mr, width = cotangent.shape
    inner = w_in.shape[2]
    own = mr // ne
    slots = -(-own // 16) * 16
    if (nd, ne, nr) == (4, 4, 2) and slots == own and mr <= 128:
        return paired(nd, ne, nr, slots, features, tile_values, tile_pairs, dispatch, w_in, w_out, cotangent)
    if slots != own:
        dispatch = jnp.pad(dispatch.reshape(ne, own), ((0, 0), (0, slots - own)), constant_values=-1).reshape(1, -1)
    seg = ne * slots
    rows = nd * seg
    chunk = min(rows, 256)
    keep_turned = ne * nd <= 64
    dma = pltpu.SemaphoreType.DMA
    vm = pltpu.VMEM
    scratch = [
        vm((nd, tps, tile, tile), bf16), vm((width, inner), bf16), vm((inner, width), bf16),
        vm((width, inner), f32), vm((inner, width), f32),
        vm((nd * tile, half), bf16), vm((ne * tile, nd * tile), bf16),
        vm((nd * tile, ne * tile) if keep_turned else (16, 128), bf16),
        vm((ne, nr, mr, half), bf16), vm((ne, nr, mr, half), bf16),
        vm((seg, width), bf16), vm((rows, width), bf16), vm((nr - 1, rows, width), bf16),
        vm((seg, width), bf16), vm((rows, width), bf16), vm((nr - 1, rows, width), bf16),
        vm((rows, width), bf16), vm((nd, seg, width), bf16), vm((seg, width), bf16), vm((seg, width), bf16),
        vm((rows, width), bf16), vm((nd, seg, width), bf16), vm((seg, width), bf16), vm((seg, width), bf16),
        vm((nr, mr, half), bf16), vm((ne * tile, half), bf16),
        vm((nd, tile, half), bf16), vm((nd, tile, half), bf16),
        vm((chunk, inner), f32), vm((chunk, inner), bf16), vm((chunk, inner), bf16),
        dma((5,)),
    ]
    for count in (nd - 1, ne * nr - 1, ne - 1, nd - 1, nr - 1, ne - 1, nd - 1, nr - 1,
                  nd - 1, ne - 1, nd - 1, ne - 1, ne * nr - 1, nd - 1):
        scratch += [dma((count,)), dma((count,))]
    in_vmem = pl.BlockSpec(memory_space=pltpu.VMEM)
    in_hbm = pl.BlockSpec(memory_space=pl.ANY)
    return placed(pl.pallas_call(
        functools.partial(body, (nd, ne, nr, slots, chunk, keep_turned)),
        name="layer",
        out_shape=(
            jax.ShapeDtypeStruct((mr, width), bf16),
            jax.ShapeDtypeStruct((tile, half), f32),
            jax.ShapeDtypeStruct((1, width, inner), f32),
            jax.ShapeDtypeStruct((1, inner, width), f32),
        ),
        in_specs=[in_vmem, in_hbm, pl.BlockSpec(memory_space=pltpu.SMEM), in_vmem, in_hbm, in_hbm, in_vmem],
        out_specs=[in_vmem, in_vmem, in_hbm, in_hbm],
        scratch_shapes=scratch,
        compiler_params=pltpu.CompilerParams(
            collective_id=0, has_side_effects=True, vmem_limit_bytes=60 * 1024 * 1024
        ),
    )(features, tile_values, tile_pairs, dispatch, w_in, w_out, cotangent))


def hand_over(pieces, *refs):
    count = len(refs) // 3
    sources, targets, held = refs[:count], refs[count:2 * count], refs[2 * count:3 * count]
    come, go = refs[3 * count:]
    cuts = []
    for source, target, middle, number in zip(sources, targets, held, pieces):
        size = source.shape[-2] // number
        for piece in range(number):
            where = (0,) * (len(source.shape) - 2) + (pl.ds(piece * size, size),)
            n = len(cuts)
            cuts.append((
                pltpu.make_async_copy(source.at[where], middle.at[where], come.at[n]),
                pltpu.make_async_copy(middle.at[where], target.at[where], go.at[n]),
            ))
    for first, _ in cuts:
        first.start()
    for first, second in cuts:
        first.wait()
        second.start()
    for _, second in cuts:
        second.wait()


def placed(arrays):
    in_hbm = pl.BlockSpec(memory_space=pl.ANY)
    pieces = tuple(4 if a.size * a.dtype.itemsize >= 2 ** 19 else 1 for a in arrays)
    return pl.pallas_call(
        functools.partial(hand_over, pieces),
        name="hand_over",
        out_shape=tuple(jax.ShapeDtypeStruct(a.shape, a.dtype) for a in arrays),
        in_specs=[in_hbm] * len(arrays),
        out_specs=[in_hbm] * len(arrays),
        scratch_shapes=[pltpu.VMEM(a.shape, a.dtype) for a in arrays]
        + [pltpu.SemaphoreType.DMA((sum(pieces),)), pltpu.SemaphoreType.DMA((sum(pieces),))],
    )(*arrays)


def solution(mesh):
    in_specs = (
        P(("dom", "expert"), "rep"),
        P("dom", "expert", None, None, None, None),
        P("dom", "expert", None, None),
        P(("dom", "expert", "rep"), None),
        P("expert", None, "dom"),
        P("expert", "dom", None),
        P(("dom", "expert", "rep"), None),
    )
    out_specs = (
        P(("dom", "expert", "rep"), None),
        P(("dom", "expert"), "rep"),
        P("expert", None, "dom"),
        P("expert", "dom", None),
    )
    sizes = (mesh.shape["dom"], mesh.shape["expert"], mesh.shape["rep"])
    return jax.shard_map(
        functools.partial(on_device, *sizes), mesh=mesh, in_specs=in_specs, out_specs=out_specs, check_vma=False
    )
```

```python
import functools

import jax
import jax.numpy as jnp
from jax import lax
from jax.experimental import pallas as pl
from jax.experimental.pallas import tpu as pltpu
from jax.sharding import PartitionSpec as P

epsilon = 1e-06
gelu_scale = 0.7978845608028654
gelu_cubic = 0.044715
bf16 = jnp.bfloat16
f32 = jnp.float32


def mm(left, right, dims):
    return lax.dot_general(left, right, (dims, ((), ())), preferred_element_type=f32)


plain = ((1,), (0,))
rows_rows = ((0,), (0,))
cols_cols = ((1,), (1,))


def body(sizes, *refs):
    nd, ne, nr, slots, chunk, keep_turned = sizes
    (feat, tv_hbm, pairs, disp, win_hbm, wout_hbm, cot,
     out, gf, gwi_hbm, gwo_hbm,
     tv, win, wout, gwi, gwo, fall, adj, turned, csend, crecv,
     tsend, tg, tx, ksend, kg, kx,
     gsend, grecv, gred, gback, osend, orecv, ored, oback,
     asend, gall, bsend, brecv, ga, acts, ghid,
     lsem, fs, fr, cs, cr, tzs, tzr, tds, tdr, txs, txr, kzs, kzr, kds, kdr, kxs, kxr,
     gds, gdr, gzs, gzr, ods, odr, ozs, ozr, ps, pr, bs, br) = refs
    me_d, me_e, me_r = lax.axis_index("dom"), lax.axis_index("expert"), lax.axis_index("rep")
    tile = feat.shape[0]
    half = feat.shape[1]
    tps = tv.shape[1]
    mr = cot.shape[0]
    seg = ne * slots
    rows = nd * seg
    pending = []

    def ring(me, step, count):
        return lax.rem(me + step, count)

    def send(src, dst, ssem, rsem, d, e, r):
        copy = pltpu.make_async_remote_copy(
            src_ref=src, dst_ref=dst, send_sem=ssem, recv_sem=rsem,
            device_id={"dom": d, "expert": e, "rep": r},
            device_id_type=pl.DeviceIdType.MESH,
        )
        copy.start()
        pending.append(copy)
        return copy

    def local(src, dst, index):
        copy = pltpu.make_async_copy(src, dst, lsem.at[index])
        copy.start()
        return copy

    def arrive(copies):
        for copy in copies:
            copy.wait_recv()

    def span(start, size):
        return pl.ds(pl.multiple_of(start, size), size)

    load_tv = local(tv_hbm.at[0, 0], tv, 0)
    load_wout = local(wout_hbm.at[0], wout, 1)
    load_win = local(win_hbm.at[0], win, 2)

    dom_steps = list(range(1, nd))
    flips = nd & (nd - 1) == 0

    def dom_to(k):
        if not flips:
            return ring(me_d, k, nd)
        place, bit = me_d, 1
        while bit < nd:
            if k & bit:
                place = place + bit - 2 * bit * lax.rem(me_d // bit, 2)
            bit *= 2
        return place

    def dom_from(k):
        return dom_to(k) if flips else ring(me_d, nd - k, nd)

    exp_steps = list(range(1, ne))
    pair_steps = [(a, b) for a in range(ne) for b in range(nr) if (a, b) != (0, 0)]

    barrier = pltpu.get_barrier_semaphore()
    for k in dom_steps:
        pl.semaphore_signal(barrier, inc=1, device_id={"dom": dom_to(k), "expert": me_e, "rep": me_r},
                            device_id_type=pl.DeviceIdType.MESH)
    for a, b in pair_steps:
        pl.semaphore_signal(barrier, inc=1,
                            device_id={"dom": me_d, "expert": ring(me_e, a, ne), "rep": ring(me_r, b, nr)},
                            device_id_type=pl.DeviceIdType.MESH)

    place = (lax.broadcasted_iota(jnp.int32, (mr, seg), 0) == disp[...]).astype(f32).astype(bf16)
    fall[span(me_d * tile, tile), :] = feat[...]
    ksend[...] = mm(place, cot[...], rows_rows).astype(bf16)
    load_tv.wait()

    def build(index, carry):
        q, s = index // nd, lax.rem(index, nd)
        total = jnp.zeros((tile, tile), f32)
        for k in range(tps):
            hit = jnp.where(pairs[0, 0, s, k] == q, 1.0, 0.0).astype(f32)
            total = total + tv[s, k].astype(f32) * hit
        adj[span(q * tile, tile), span(s * tile, tile)] = total.astype(bf16)
        return carry

    lax.fori_loop(0, ne * nd, build, 0)
    pl.semaphore_wait(barrier, len(dom_steps) + len(pair_steps))

    f_copies = [
        send(feat, fall.at[span(me_d * tile, tile)], fs.at[k - 1], fr.at[k - 1], dom_to(k), me_e, me_r)
        for k in dom_steps
    ]

    def to_experts(source, target, ssem, rsem):
        copies = []
        for k in exp_steps:
            x = ring(me_e, k, ne)
            copies.append(send(source.at[span(x * slots, slots)], target.at[span((me_d * ne + me_e) * slots, slots)],
                               ssem.at[k - 1], rsem.at[k - 1], me_d, x, me_r))
        mine = span((me_d * ne + me_e) * slots, slots)
        target[mine, :] = source[span(me_e * slots, slots), :]
        return copies

    def to_doms(target, ssem, rsem):
        block = target.at[span(me_d * seg, seg)]
        return [send(block, block, ssem.at[k - 1], rsem.at[k - 1], dom_to(k), me_e, me_r) for k in dom_steps]

    def to_reps(source, target, ssem, rsem):
        return [send(source, target.at[k - 1], ssem.at[k - 1], rsem.at[k - 1], me_d, me_e, ring(me_r, k, nr))
                for k in range(1, nr)]

    kz = to_experts(ksend, kg, kzs, kzr)

    def turn(index, carry):
        q, s = index // nd, lax.rem(index, nd)
        turned[span(s * tile, tile), span(q * tile, tile)] = adj[span(q * tile, tile), span(s * tile, tile)].T
        return carry


    arrive(f_copies)
    c_copies = []
    for a in list(range(1, ne)) + [0]:
        q = ring(me_e, a, ne)
        column = mm(adj[span(q * tile, tile), :], fall[...], plain).astype(bf16)
        for b in range(nr):
            csend[q, b] = column[b * mr:(b + 1) * mr, :]
        for b in range(nr):
            r = ring(me_r, b, nr)
            if (a, b) != (0, 0):
                n = a * nr + b - 1
                c_copies.append(send(csend.at[q, r], crecv.at[me_e, me_r], cs.at[n], cr.at[n], me_d, q, r))
    crecv[me_e, me_r] = csend[me_e, me_r]

    arrive(kz)
    kd = to_doms(kg, kds, kdr)
    load_wout.wait()
    load_win.wait()
    if keep_turned:
        lax.fori_loop(0, ne * nd, turn, 0)
    arrive(kd)
    whole_rows = rows == chunk
    if whole_rows:
        ga[...] = mm(kg[...], wout[...], cols_cols)

    arrive(c_copies)
    parts = []
    for r in range(nr):
        total = crecv[0, r].astype(f32)
        for e in range(1, ne):
            total = total + crecv[e, r].astype(f32)
        parts.append(total)
    agg = jnp.concatenate(parts, axis=1).astype(bf16).astype(f32)
    width = agg.shape[1]
    scale = lax.rsqrt(jnp.mean(agg * agg, axis=-1, keepdims=True) + epsilon)
    normed = (agg * scale).astype(bf16)
    tsend[...] = mm(place, normed, rows_rows).astype(bf16)
    tz = to_experts(tsend, tg, tzs, tzr)
    kxc = to_reps(kg, kx, kxs, kxr)
    arrive(tz)
    td = to_doms(tg, tds, tdr)

    def hidden(tokens, grad_act):
        pre = mm(tokens, win[...], plain)
        tangent = jnp.tanh(gelu_scale * (pre + gelu_cubic * pre * pre * pre))
        act = (0.5 * pre * (1.0 + tangent)).astype(bf16)
        slope = 0.5 * (1.0 + tangent) + 0.5 * pre * (1.0 - tangent * tangent) * gelu_scale * (
            1.0 + 3.0 * gelu_cubic * pre * pre)
        return act, (grad_act * slope).astype(bf16)

    def add_grads(tokens, grads, act, grad_hidden, first):
        one = mm(tokens, grad_hidden, rows_rows)
        two = mm(act, grads, rows_rows)
        if first:
            gwi[...] = one
            gwo[...] = two
        else:
            gwi[...] += one
            gwo[...] += two

    def scatter(source, target, ssem, rsem):
        copies = [
            send(source.at[span(dom_to(k) * seg, seg)], target.at[me_d], ssem.at[k - 1], rsem.at[k - 1],
                 dom_to(k), me_e, me_r)
            for k in dom_steps
        ]
        target[me_d] = source[span(me_d * seg, seg), :]
        return copies

    if whole_rows:
        gd = []
        for k in [0] + dom_steps:
            if k > 0:
                arrive([td[k - 1]])
            d = dom_from(k)
            where = span(d * seg, seg)
            act, grad_hidden = hidden(tg[where, :], ga[where, :])
            term = mm(grad_hidden, win[...], cols_cols).astype(bf16)
            acts[where, :] = act
            ghid[where, :] = grad_hidden
            if k == 0:
                grecv[me_d] = term
            else:
                gsend[where, :] = term
                gd.append(send(gsend.at[where], grecv.at[me_d], gds.at[k - 1], gdr.at[k - 1], d, me_e, me_r))
        txc = to_reps(tg, tx, txs, txr)
        osend[...] = mm(acts[...], wout[...], plain).astype(bf16)
        add_grads(tg[...], kg[...], acts[...], ghid[...], True)
    else:
        arrive(td)
        txc = to_reps(tg, tx, txs, txr)
        gwi[...] = jnp.zeros_like(gwi)
        gwo[...] = jnp.zeros_like(gwo)

        def one_chunk(index, carry):
            where = span(index * chunk, chunk)
            act, grad_hidden = hidden(tg[where, :], mm(kg[where, :], wout[...], cols_cols))
            gsend[where, :] = mm(grad_hidden, win[...], cols_cols).astype(bf16)
            osend[where, :] = mm(act, wout[...], plain).astype(bf16)
            add_grads(tg[where, :], kg[where, :], act, grad_hidden, False)
            return carry

        lax.fori_loop(0, rows // chunk, one_chunk, 0)
        gd = scatter(gsend, grecv, gds, gdr)

    def summed(target):
        total = target[0].astype(f32)
        for d in range(1, nd):
            total = total + target[d].astype(f32)
        return total.astype(bf16)

    def to_nodes(source, target, ssem, rsem):
        copies = []
        for k in exp_steps:
            e = ring(me_e, k, ne)
            copies.append(send(source.at[span(e * slots, slots)], target.at[span(me_e * slots, slots)],
                               ssem.at[k - 1], rsem.at[k - 1], me_d, e, me_r))
        mine = span(me_e * slots, slots)
        target[mine, :] = source[mine, :]
        return copies

    arrive(gd)
    gred[...] = summed(grecv)
    gz = to_nodes(gred, gback, gzs, gzr)
    od = scatter(osend, orecv, ods, odr)

    arrive(gz)
    back = mm(place, gback[...], plain)
    dot_mean = jnp.mean(agg * back, axis=-1, keepdims=True)
    grad_agg = (cot[...].astype(f32) + scale * back - agg * (scale * scale * scale) * dot_mean).astype(bf16)
    for r in range(nr):
        asend[r] = grad_agg[:, r * half:(r + 1) * half]
    here = span(me_e * tile + me_r * mr, mr)
    p_copies = []
    for a, b in pair_steps:
        n = a * nr + b - 1
        r = ring(me_r, b, nr)
        p_copies.append(send(asend.at[r], gall.at[here], ps.at[n], pr.at[n], me_d, ring(me_e, a, ne), r))
    gall[here, :] = asend[me_r]

    arrive(kxc)
    arrive(txc)
    for n in range(nr - 1):
        if whole_rows:
            act, grad_hidden = hidden(tx[n], mm(kx[n], wout[...], cols_cols))
            add_grads(tx[n], kx[n], act, grad_hidden, False)
        else:
            def other_chunk(index, carry):
                where = span(index * chunk, chunk)
                act, grad_hidden = hidden(tx[n, where, :], mm(kx[n, where, :], wout[...], cols_cols))
                add_grads(tx[n, where, :], kx[n, where, :], act, grad_hidden, False)
                return carry

            lax.fori_loop(0, rows // chunk, other_chunk, 0)
    store_i = local(gwi, gwi_hbm.at[0], 3)
    store_o = local(gwo, gwo_hbm.at[0], 4)

    arrive(od)
    ored[...] = summed(orecv)
    arrive(p_copies)
    oz = to_nodes(ored, oback, ozs, ozr)
    b_copies = []
    for k in dom_steps[::-1] + [0]:
        s = dom_to(k)
        if keep_turned:
            term = mm(turned[span(s * tile, tile), :], gall[...], plain)
        else:
            term = mm(adj[:, span(s * tile, tile)], gall[...], rows_rows)
        if k > 0:
            bsend[s] = term.astype(bf16)
            b_copies.append(send(bsend.at[s], brecv.at[me_d], bs.at[k - 1], br.at[k - 1], s, me_e, me_r))
        else:
            brecv[me_d] = term.astype(bf16)
    arrive(oz)
    out[...] = (agg + mm(place, oback[...], plain)).astype(bf16)
    arrive(b_copies)
    total = brecv[0].astype(f32)
    for d in range(1, nd):
        total = total + brecv[d].astype(f32)
    gf[...] = total
    store_i.wait()
    store_o.wait()
    for copy in pending:
        copy.wait_send()


def flip(me, k):
    place, bit = me, 1
    while bit <= k:
        if k & bit:
            place = place + bit - 2 * bit * lax.rem(me // bit, 2)
        bit *= 2
    return place


def body_paired(sizes, *refs):
    nd, ne, nr, slots, cuts = sizes
    (feat_hbm, tv_hbm, pairs_hbm, disp_hbm, win_hbm, wout_hbm, cot_hbm,
     out, gf, gwi, gwo,
     tv, pairs, disp, cot, win, wout, fall, adj, sorted_adj, turned, dsend, dall, csend, crecv,
     ksend, kg, kx, tg, tx, ga, acts, ghid, acts_far, gown, gsend, grecv, oown, osend, orecv, ored, oback,
     asend, gall, bsend, brecv, sent, ready, lsem, ssem, rsem) = refs
    me_d, me_e, me_r = lax.axis_index("dom"), lax.axis_index("expert"), lax.axis_index("rep")
    tile, half = fall.shape[0] // nd, fall.shape[1]
    tps = tv.shape[1]
    mr, width = cot.shape
    inner = win.shape[2]
    cut = mr // cuts
    groups = {}

    def copy_of(src, dst, d, e, r, group):
        return pltpu.make_async_remote_copy(
            src_ref=src, dst_ref=dst, send_sem=ssem.at[0], recv_sem=rsem.at[groups.setdefault(group, len(groups))],
            device_id={"dom": flip(me_d, d), "expert": flip(me_e, e), "rep": flip(me_r, r)},
            device_id_type=pl.DeviceIdType.MESH,
        )

    def send(src, dst, d, e, r, group):
        copy_of(src, dst, d, e, r, group).start()

    def local(src, dst, index):
        copy = pltpu.make_async_copy(src, dst, lsem.at[index])
        copy.start()
        return copy

    def arrive(group, ref):
        copy_of(ref, ref, 0, 0, 0, group).wait_recv()

    def span(start, size):
        return pl.ds(pl.multiple_of(start, size), size)

    pair_steps = [(a, b) for a in (2, 3, 1, 0) for b in range(nr) if (a, b) != (0, 0)]
    all_steps = pair_steps + [(0, 0)]
    barrier = pltpu.get_barrier_semaphore()
    core = lax.rem(me_d, 2)

    def tell(semaphore, d, e, r):
        pl.semaphore_signal(semaphore, inc=1,
                            device_id={"dom": flip(me_d, d), "expert": flip(me_e, e), "rep": flip(me_r, r)},
                            device_id_type=pl.DeviceIdType.MESH)

    @pl.when(core == 0)
    def _():
        tell(barrier, 2, 0, 0)
        for a, b in pair_steps:
            tell(barrier, 1, a, b)

    @pl.when(core == 1)
    def _():
        tell(barrier, 1, 0, 0)
        tell(barrier, 3, 0, 0)
        for a, b in pair_steps:
            tell(barrier, 0, a, b)

    own_feat = fall.at[span(me_d * tile, tile)]
    load_feat = local(feat_hbm, own_feat, 0)
    load_disp = local(disp_hbm, disp, 1)
    load_cot = local(cot_hbm, cot, 2)
    load_pairs = local(pairs_hbm, pairs, 3)
    load_tv = local(tv_hbm.at[0, 0], tv, 4)
    load_win = local(win_hbm.at[0], win.at[0], 5)
    load_wout = local(wout_hbm.at[0], wout.at[0], 6)

    load_disp.wait()
    dsend[...] = jnp.zeros_like(dsend)
    dsend[:, 0:mr] = jnp.broadcast_to(disp[...], (dsend.shape[0], mr))
    dall[me_e * nr + me_r] = dsend[...]
    load_feat.wait()

    @pl.when(core == 0)
    def _():
        pl.semaphore_wait(barrier, nd - 1)
        tell(ready.at[0], 1, 0, 0)

    @pl.when(core == 1)
    def _():
        pl.semaphore_wait(ready.at[0], 1)

    for k in (2, 3, 1):
        send(own_feat, own_feat, k, 0, 0, "features")

    @pl.when(core == 1)
    def _():
        pl.semaphore_wait(barrier, 2 * len(pair_steps))
        tell(ready.at[1], 1, 0, 0)

    @pl.when(core == 0)
    def _():
        pl.semaphore_wait(ready.at[1], 1)

    for a, b in pair_steps:
        send(dsend, dall.at[me_e * nr + me_r], 0, a, b, "order")

    place = (lax.broadcasted_iota(jnp.int32, (mr, ne * slots), 0) == disp[...]).astype(f32).astype(bf16)
    load_cot.wait()
    ksend[...] = mm(place, cot[...], rows_rows).astype(bf16)
    here = span(me_e * slots, slots)
    for a in (2, 3, 1, 0):
        send(ksend.at[span(flip(me_e, a) * slots, slots)], kg.at[here], 1, a, 0, "cotangent")
    load_pairs.wait()
    load_tv.wait()

    def build(index, carry):
        q, s = index // nd, lax.rem(index, nd)
        total = jnp.zeros((tile, tile), f32)
        for k in range(tps):
            hit = jnp.where(pairs[0, 0, s, k] == q, 1.0, 0.0).astype(f32)
            total = total + tv[s, k].astype(f32) * hit
        adj[span(q * tile, tile), span(s * tile, tile)] = total.astype(bf16)
        return carry

    lax.fori_loop(0, ne * nd, build, 0)
    load_win.wait()
    load_wout.wait()
    send(win.at[0], win.at[1], 1, 0, 0, "weights")
    send(wout.at[0], wout.at[1], 1, 0, 0, "weights")

    arrive("order", dall.at[pl.ds(0, ne * nr - 1)])
    for e in range(ne):
        for r in range(nr):
            group = (lax.broadcasted_iota(jnp.int32, (mr, mr), 0) == dall[e * nr + r, 0:1, 0:mr]).astype(f32).astype(bf16)
            begin = e * tile + r * mr
            moved = mm(group, adj[begin:begin + mr, :], rows_rows).astype(bf16)
            for x in range(ne):
                begin = x * tile + r * mr + e * slots
                sorted_adj[begin:begin + slots, :] = moved[x * slots:(x + 1) * slots, :]

    arrive("features", fall.at[pl.ds(0, (nd - 1) * tile)])

    def send_column(a, h):
        rows = pl.ds(h * cut, cut)
        for b in range(nr):
            send(csend.at[a * nr + flip(me_r, b), rows], crecv.at[me_e * nr + me_r, rows], 1, a, b, ("column", h))

    for a in (2, 3, 1, 0):
        column = mm(sorted_adj[span(flip(me_e, a) * tile, tile), :], fall[...], plain).astype(bf16)
        for b in range(nr):
            csend[a * nr + b] = column[b * mr:(b + 1) * mr, :]
        send_column(a, 0)
    for h in range(1, cuts):
        for a in (2, 3, 1, 0):
            send_column(a, h)

    arrive("cotangent", kg.at[pl.ds(0, ne * slots)])
    own, far = pl.ds(0, mr), pl.ds(mr, mr)
    near, last = pl.ds(2 * mr, mr), pl.ds(3 * mr, mr)
    send(kg.at[own], kg.at[far], 3, 0, 0, "far cotangent")
    send(kg.at[own], kg.at[near], 1, 0, 0, "near cotangent")

    def turn(index, carry):
        q, s = index // nd, lax.rem(index, nd)
        turned[span(s * tile, tile), span(q * tile, tile)] = sorted_adj[span(q * tile, tile), span(s * tile, tile)].T
        return carry

    lax.fori_loop(0, ne * nd, turn, 0)
    arrive("weights", win.at[pl.ds(0, 2)])
    arrive("far cotangent", kg.at[far])
    send(kg.at[far], kg.at[last], 1, 0, 0, "near cotangent")
    pair, other = pl.ds(0, 2 * mr), pl.ds(2 * mr, 2 * mr)
    send(kg.at[pair], kx.at[pair], 0, 0, 1, "across cotangent")
    for w in range(2):
        for j in range(2):
            ga[w, j] = mm(kg[w * mr:(w + 1) * mr, :], wout[j], cols_cols)

    def hidden(tokens, grad_act, j):
        pre = mm(tokens, win[j], plain)
        tangent = jnp.tanh(gelu_scale * (pre + gelu_cubic * pre * pre * pre))
        act = (0.5 * pre * (1.0 + tangent)).astype(bf16)
        slope = 0.5 * (1.0 + tangent) + 0.5 * pre * (1.0 - tangent * tangent) * gelu_scale * (
            1.0 + 3.0 * gelu_cubic * pre * pre)
        return act, (grad_act * slope).astype(bf16)

    def work(w, h):
        begin = w * mr + h * cut
        rows = pl.ds(begin, cut)
        tokens = tg[rows, :]
        total = None
        for j in range(2):
            act, grad_hidden = hidden(tokens, ga[w, j, h * cut:(h + 1) * cut, :], j)
            if j == 0:
                acts[rows, :] = act
                ghid[rows, :] = grad_hidden
            else:
                acts_far[rows, :] = act
            term = mm(grad_hidden, win[j], cols_cols)
            total = term if total is None else total + term
        return total

    aggs, scales = [], []
    for h in range(cuts):
        arrive(("column", h), crecv.at[pl.ds(0, ne * nr), pl.ds(0, cut)])
        halves = []
        for r in range(nr):
            total = crecv[r, h * cut:(h + 1) * cut, :].astype(f32)
            for e in range(1, ne):
                total = total + crecv[e * nr + r, h * cut:(h + 1) * cut, :].astype(f32)
            halves.append(total)
        agg = jnp.concatenate(halves, axis=1).astype(bf16).astype(f32)
        scale = lax.rsqrt(jnp.mean(agg * agg, axis=-1, keepdims=True) + epsilon)
        tg[h * cut:(h + 1) * cut, :] = (agg * scale).astype(bf16)
        send(tg.at[pl.ds(h * cut, cut)], tg.at[pl.ds(mr + h * cut, cut)], 3, 0, 0, ("tokens", h))
        aggs.append(agg)
        scales.append(scale)
        if h == 0:
            gown[0:cut, :] = work(0, 0)
    send(tg.at[own], tg.at[near], 1, 0, 0, "near tokens")
    for h in range(cuts):
        arrive(("tokens", h), tg.at[pl.ds(0, cut)])
        rows = pl.ds(h * cut, cut)
        gsend[rows, :] = work(1, h).astype(bf16)
        send(gsend.at[rows], grecv.at[rows], 3, 0, 0, ("terms", h))
        if h + 1 < cuts:
            gown[(h + 1) * cut:(h + 2) * cut, :] = work(0, h + 1)
    send(tg.at[pair], tx.at[pair], 0, 0, 1, "across tokens")
    send(tg.at[far], tg.at[last], 1, 0, 0, "near tokens")
    arrive("across cotangent", kx.at[pair])
    send(kx.at[pair], kx.at[other], 1, 0, 0, "near across")

    for h in range(cuts):
        arrive(("terms", h), grecv.at[pl.ds(0, cut)])
        rows = slice(h * cut, (h + 1) * cut)
        agg, scale = aggs[h], scales[h]
        back = (gown[rows, :] + grecv[rows, :].astype(f32)).astype(bf16).astype(f32)
        dot_mean = jnp.mean(agg * back, axis=-1, keepdims=True)
        grad_agg = (kg[rows, :].astype(f32) + scale * back - agg * (scale * scale * scale) * dot_mean).astype(bf16)
        for r in range(nr):
            asend[r, rows, :] = grad_agg[:, r * half:(r + 1) * half]
        there = span(me_e * tile + me_r * mr + h * cut, cut)
        for a, b in all_steps:
            send(asend.at[flip(me_r, b), pl.ds(h * cut, cut)], gall.at[there], 1, a, b, "gradients")

    def outputs(w):
        rows = slice(w * mr, (w + 1) * mr)
        return mm(acts[rows, :], wout[0], plain) + mm(acts_far[rows, :], wout[1], plain)

    osend[...] = outputs(1).astype(bf16)
    send(osend, orecv, 3, 0, 0, "halves")
    oown[...] = outputs(0)
    arrive("near cotangent", kg.at[pair])
    arrive("near tokens", tg.at[pair])
    act, grad_hidden = hidden(tg[2 * mr:, :], mm(kg[2 * mr:, :], wout[0], cols_cols), 0)
    acts[2 * mr:, :] = act
    ghid[2 * mr:, :] = grad_hidden
    gwi[0] = mm(tg[...], ghid[...], rows_rows)
    gwo[0] = mm(acts[...], kg[...], rows_rows)

    arrive("across tokens", tx.at[pair])
    send(tx.at[pair], tx.at[other], 1, 0, 0, "near across")
    arrive("halves", orecv)
    agg = jnp.concatenate(aggs, axis=0)
    routed = (oown[...] + orecv[...].astype(f32)).astype(bf16).astype(f32)
    ored[...] = (agg + routed).astype(bf16)
    for a in (2, 3, 1, 0):
        send(ored.at[span(flip(me_e, a) * slots, slots)], oback.at[here], 1, a, 0, "results")

    arrive("gradients", gall)
    for k in (2, 3, 1, 0):
        term = mm(turned[span(flip(me_d, k) * tile, tile), :], gall[...], plain)
        bsend[k] = term.astype(bf16)
        if k > 0:
            send(bsend.at[k], brecv.at[k - 1], k, 0, 0, "backterms")
    arrive("near across", kx)
    act, grad_hidden = hidden(tx[...], mm(kx[...], wout[0], cols_cols), 0)
    gwi[0] += mm(tx[...], grad_hidden, rows_rows)
    gwo[0] += mm(act, kx[...], rows_rows)
    arrive("results", oback)
    out[...] = mm(place, oback[...], plain).astype(bf16)
    arrive("backterms", brecv)
    total = bsend[0].astype(f32)
    for k in range(1, nd):
        total = total + brecv[k - 1].astype(f32)
    gf[...] = total
    copy_of(sent, sent, 0, 0, 0, "features").wait_send()


def paired(nd, ne, nr, slots, features, tile_values, tile_pairs, dispatch, w_in, w_out, cotangent):
    tile, half = features.shape
    tps = tile_values.shape[3]
    mr, width = cotangent.shape
    inner = w_in.shape[2]
    rows = nd * mr
    cuts = 2
    vm = pltpu.VMEM
    steps = ne * nr - 1
    words = (2 * (nd - 1) * tile * half + 2 * steps * 8 * 128 + 2 * ne * slots * width + 2 * width * inner
             + 2 * ne * nr * mr * half + 8 * mr * width + 2 * rows * width)
    scratch = [
        vm((nd, tps, tile, tile), bf16), pltpu.SMEM(tile_pairs.shape, jnp.int32), vm(dispatch.shape, jnp.int32),
        vm((mr, width), bf16), vm((2, width, inner), bf16), vm((2, inner, width), bf16),
        vm((nd * tile, half), bf16), vm((ne * tile, nd * tile), bf16), vm((ne * tile, nd * tile), bf16),
        vm((nd * tile, ne * tile), bf16), vm((8, 128), jnp.int32), vm((ne * nr, 8, 128), jnp.int32),
        vm((ne * nr, mr, half), bf16), vm((ne * nr, mr, half), bf16),
        vm((mr, width), bf16), vm((rows, width), bf16), vm((rows, width), bf16),
        vm((rows, width), bf16), vm((rows, width), bf16),
        vm((2, 2, mr, inner), f32), vm((rows, inner), bf16), vm((rows, inner), bf16), vm((2 * mr, inner), bf16),
        vm((mr, width), f32), vm((mr, width), bf16), vm((mr, width), bf16),
        vm((mr, width), f32), vm((mr, width), bf16), vm((mr, width), bf16), vm((mr, width), bf16), vm((mr, width), bf16),
        vm((nr, mr, half), bf16), vm((ne * tile, half), bf16),
        vm((nd, tile, half), bf16), vm((nd - 1, tile, half), bf16),
        vm((words // 128, 128), bf16),
        pltpu.SemaphoreType.REGULAR((2,)), pltpu.SemaphoreType.DMA((7,)), pltpu.SemaphoreType.DMA((1,)), pltpu.SemaphoreType.DMA((17 + 3 * (cuts - 1),)),
    ]
    in_vmem = pl.BlockSpec(memory_space=pltpu.VMEM)
    in_hbm = pl.BlockSpec(memory_space=pl.ANY)
    arguments = (features, tile_values, tile_pairs, dispatch, w_in, w_out, cotangent)
    return leave(pl.pallas_call(
        functools.partial(body_paired, (nd, ne, nr, slots, cuts)),
        name="layer",
        out_shape=(
            vm((mr, width), bf16), vm((tile, half), f32), vm((1, width, inner), f32), vm((1, inner, width), f32),
        ),
        in_specs=[in_hbm] * 7,
        out_specs=[in_vmem] * 4,
        scratch_shapes=scratch,
        compiler_params=pltpu.CompilerParams(
            collective_id=0, has_side_effects=True, vmem_limit_bytes=56 * 1024 * 1024
        ),
    )(*[pltpu.with_memory_space_constraint(a, pltpu.HBM) for a in arguments]))


def store(*refs):
    count = len(refs) // 2
    copies = [pltpu.make_async_copy(refs[n], refs[count + n], refs[-1].at[n]) for n in range(count)]
    for copy in copies:
        copy.start()
    for copy in copies:
        copy.wait()


def leave(arrays):
    arrays = [pltpu.with_memory_space_constraint(a, pltpu.VMEM) for a in arrays]
    return pl.pallas_call(
        store,
        name="leave",
        out_shape=tuple(jax.ShapeDtypeStruct(a.shape, a.dtype) for a in arrays),
        in_specs=[pl.BlockSpec(memory_space=pltpu.VMEM)] * len(arrays),
        out_specs=[pl.BlockSpec(memory_space=pl.ANY)] * len(arrays),
        scratch_shapes=[pltpu.SemaphoreType.DMA((len(arrays),))],
    )(*arrays)


def on_device(nd, ne, nr, features, tile_values, tile_pairs, dispatch, w_in, w_out, cotangent):
    tile, half = features.shape
    tps = tile_values.shape[3]
    mr, width = cotangent.shape
    inner = w_in.shape[2]
    own = mr // ne
    slots = -(-own // 16) * 16
    if (nd, ne, nr) == (4, 4, 2) and slots == own and mr <= 128:
        return paired(nd, ne, nr, slots, features, tile_values, tile_pairs, dispatch, w_in, w_out, cotangent)
    if slots != own:
        dispatch = jnp.pad(dispatch.reshape(ne, own), ((0, 0), (0, slots - own)), constant_values=-1).reshape(1, -1)
    seg = ne * slots
    rows = nd * seg
    chunk = min(rows, 256)
    keep_turned = ne * nd <= 64
    dma = pltpu.SemaphoreType.DMA
    vm = pltpu.VMEM
    scratch = [
        vm((nd, tps, tile, tile), bf16), vm((width, inner), bf16), vm((inner, width), bf16),
        vm((width, inner), f32), vm((inner, width), f32),
        vm((nd * tile, half), bf16), vm((ne * tile, nd * tile), bf16),
        vm((nd * tile, ne * tile) if keep_turned else (16, 128), bf16),
        vm((ne, nr, mr, half), bf16), vm((ne, nr, mr, half), bf16),
        vm((seg, width), bf16), vm((rows, width), bf16), vm((nr - 1, rows, width), bf16),
        vm((seg, width), bf16), vm((rows, width), bf16), vm((nr - 1, rows, width), bf16),
        vm((rows, width), bf16), vm((nd, seg, width), bf16), vm((seg, width), bf16), vm((seg, width), bf16),
        vm((rows, width), bf16), vm((nd, seg, width), bf16), vm((seg, width), bf16), vm((seg, width), bf16),
        vm((nr, mr, half), bf16), vm((ne * tile, half), bf16),
        vm((nd, tile, half), bf16), vm((nd, tile, half), bf16),
        vm((chunk, inner), f32), vm((chunk, inner), bf16), vm((chunk, inner), bf16),
        dma((5,)),
    ]
    for count in (nd - 1, ne * nr - 1, ne - 1, nd - 1, nr - 1, ne - 1, nd - 1, nr - 1,
                  nd - 1, ne - 1, nd - 1, ne - 1, ne * nr - 1, nd - 1):
        scratch += [dma((count,)), dma((count,))]
    in_vmem = pl.BlockSpec(memory_space=pltpu.VMEM)
    in_hbm = pl.BlockSpec(memory_space=pl.ANY)
    return placed(pl.pallas_call(
        functools.partial(body, (nd, ne, nr, slots, chunk, keep_turned)),
        name="layer",
        out_shape=(
            jax.ShapeDtypeStruct((mr, width), bf16),
            jax.ShapeDtypeStruct((tile, half), f32),
            jax.ShapeDtypeStruct((1, width, inner), f32),
            jax.ShapeDtypeStruct((1, inner, width), f32),
        ),
        in_specs=[in_vmem, in_hbm, pl.BlockSpec(memory_space=pltpu.SMEM), in_vmem, in_hbm, in_hbm, in_vmem],
        out_specs=[in_vmem, in_vmem, in_hbm, in_hbm],
        scratch_shapes=scratch,
        compiler_params=pltpu.CompilerParams(
            collective_id=0, has_side_effects=True, vmem_limit_bytes=60 * 1024 * 1024
        ),
    )(features, tile_values, tile_pairs, dispatch, w_in, w_out, cotangent))


def hand_over(pieces, *refs):
    count = len(refs) // 3
    sources, targets, held = refs[:count], refs[count:2 * count], refs[2 * count:3 * count]
    come, go = refs[3 * count:]
    cuts = []
    for source, target, middle, number in zip(sources, targets, held, pieces):
        size = source.shape[-2] // number
        for piece in range(number):
            where = (0,) * (len(source.shape) - 2) + (pl.ds(piece * size, size),)
            n = len(cuts)
            cuts.append((
                pltpu.make_async_copy(source.at[where], middle.at[where], come.at[n]),
                pltpu.make_async_copy(middle.at[where], target.at[where], go.at[n]),
            ))
    for first, _ in cuts:
        first.start()
    for first, second in cuts:
        first.wait()
        second.start()
    for _, second in cuts:
        second.wait()


def placed(arrays):
    in_hbm = pl.BlockSpec(memory_space=pl.ANY)
    pieces = tuple(4 if a.size * a.dtype.itemsize >= 2 ** 19 else 1 for a in arrays)
    return pl.pallas_call(
        functools.partial(hand_over, pieces),
        name="hand_over",
        out_shape=tuple(jax.ShapeDtypeStruct(a.shape, a.dtype) for a in arrays),
        in_specs=[in_hbm] * len(arrays),
        out_specs=[in_hbm] * len(arrays),
        scratch_shapes=[pltpu.VMEM(a.shape, a.dtype) for a in arrays]
        + [pltpu.SemaphoreType.DMA((sum(pieces),)), pltpu.SemaphoreType.DMA((sum(pieces),))],
    )(*arrays)


def solution(mesh):
    in_specs = (
        P(("dom", "expert"), "rep"),
        P("dom", "expert", None, None, None, None),
        P("dom", "expert", None, None),
        P(("dom", "expert", "rep"), None),
        P("expert", None, "dom"),
        P("expert", "dom", None),
        P(("dom", "expert", "rep"), None),
    )
    out_specs = (
        P(("dom", "expert", "rep"), None),
        P(("dom", "expert"), "rep"),
        P("expert", None, "dom"),
        P("expert", "dom", None),
    )
    sizes = (mesh.shape["dom"], mesh.shape["expert"], mesh.shape["rep"])
    return jax.shard_map(
        functools.partial(on_device, *sizes), mesh=mesh, in_specs=in_specs, out_specs=out_specs, check_vma=False
    )
```

```python
import functools

import jax
import jax.numpy as jnp
from jax import lax
from jax.experimental import pallas as pl
from jax.experimental.pallas import tpu as pltpu
from jax.sharding import PartitionSpec as P

epsilon = 1e-06
gelu_scale = 0.7978845608028654
gelu_cubic = 0.044715
bf16 = jnp.bfloat16
f32 = jnp.float32


def mm(left, right, dims):
    return lax.dot_general(left, right, (dims, ((), ())), preferred_element_type=f32)


plain = ((1,), (0,))
rows_rows = ((0,), (0,))
cols_cols = ((1,), (1,))


def body(sizes, *refs):
    nd, ne, nr, slots, chunk, keep_turned = sizes
    (feat, tv_hbm, pairs, disp, win_hbm, wout_hbm, cot,
     out, gf, gwi_hbm, gwo_hbm,
     tv, win, wout, gwi, gwo, fall, adj, turned, csend, crecv,
     tsend, tg, tx, ksend, kg, kx,
     gsend, grecv, gred, gback, osend, orecv, ored, oback,
     asend, gall, bsend, brecv, ga, acts, ghid,
     lsem, fs, fr, cs, cr, tzs, tzr, tds, tdr, txs, txr, kzs, kzr, kds, kdr, kxs, kxr,
     gds, gdr, gzs, gzr, ods, odr, ozs, ozr, ps, pr, bs, br) = refs
    me_d, me_e, me_r = lax.axis_index("dom"), lax.axis_index("expert"), lax.axis_index("rep")
    tile = feat.shape[0]
    half = feat.shape[1]
    tps = tv.shape[1]
    mr = cot.shape[0]
    seg = ne * slots
    rows = nd * seg
    pending = []

    def ring(me, step, count):
        return lax.rem(me + step, count)

    def send(src, dst, ssem, rsem, d, e, r):
        copy = pltpu.make_async_remote_copy(
            src_ref=src, dst_ref=dst, send_sem=ssem, recv_sem=rsem,
            device_id={"dom": d, "expert": e, "rep": r},
            device_id_type=pl.DeviceIdType.MESH,
        )
        copy.start()
        pending.append(copy)
        return copy

    def local(src, dst, index):
        copy = pltpu.make_async_copy(src, dst, lsem.at[index])
        copy.start()
        return copy

    def arrive(copies):
        for copy in copies:
            copy.wait_recv()

    def span(start, size):
        return pl.ds(pl.multiple_of(start, size), size)

    load_tv = local(tv_hbm.at[0, 0], tv, 0)
    load_wout = local(wout_hbm.at[0], wout, 1)
    load_win = local(win_hbm.at[0], win, 2)

    dom_steps = list(range(1, nd))
    flips = nd & (nd - 1) == 0

    def dom_to(k):
        if not flips:
            return ring(me_d, k, nd)
        place, bit = me_d, 1
        while bit < nd:
            if k & bit:
                place = place + bit - 2 * bit * lax.rem(me_d // bit, 2)
            bit *= 2
        return place

    def dom_from(k):
        return dom_to(k) if flips else ring(me_d, nd - k, nd)

    exp_steps = list(range(1, ne))
    pair_steps = [(a, b) for a in range(ne) for b in range(nr) if (a, b) != (0, 0)]

    barrier = pltpu.get_barrier_semaphore()
    for k in dom_steps:
        pl.semaphore_signal(barrier, inc=1, device_id={"dom": dom_to(k), "expert": me_e, "rep": me_r},
                            device_id_type=pl.DeviceIdType.MESH)
    for a, b in pair_steps:
        pl.semaphore_signal(barrier, inc=1,
                            device_id={"dom": me_d, "expert": ring(me_e, a, ne), "rep": ring(me_r, b, nr)},
                            device_id_type=pl.DeviceIdType.MESH)

    place = (lax.broadcasted_iota(jnp.int32, (mr, seg), 0) == disp[...]).astype(f32).astype(bf16)
    fall[span(me_d * tile, tile), :] = feat[...]
    ksend[...] = mm(place, cot[...], rows_rows).astype(bf16)
    load_tv.wait()

    def build(index, carry):
        q, s = index // nd, lax.rem(index, nd)
        total = jnp.zeros((tile, tile), f32)
        for k in range(tps):
            hit = jnp.where(pairs[0, 0, s, k] == q, 1.0, 0.0).astype(f32)
            total = total + tv[s, k].astype(f32) * hit
        adj[span(q * tile, tile), span(s * tile, tile)] = total.astype(bf16)
        return carry

    lax.fori_loop(0, ne * nd, build, 0)
    pl.semaphore_wait(barrier, len(dom_steps) + len(pair_steps))

    f_copies = [
        send(feat, fall.at[span(me_d * tile, tile)], fs.at[k - 1], fr.at[k - 1], dom_to(k), me_e, me_r)
        for k in dom_steps
    ]

    def to_experts(source, target, ssem, rsem):
        copies = []
        for k in exp_steps:
            x = ring(me_e, k, ne)
            copies.append(send(source.at[span(x * slots, slots)], target.at[span((me_d * ne + me_e) * slots, slots)],
                               ssem.at[k - 1], rsem.at[k - 1], me_d, x, me_r))
        mine = span((me_d * ne + me_e) * slots, slots)
        target[mine, :] = source[span(me_e * slots, slots), :]
        return copies

    def to_doms(target, ssem, rsem):
        block = target.at[span(me_d * seg, seg)]
        return [send(block, block, ssem.at[k - 1], rsem.at[k - 1], dom_to(k), me_e, me_r) for k in dom_steps]

    def to_reps(source, target, ssem, rsem):
        return [send(source, target.at[k - 1], ssem.at[k - 1], rsem.at[k - 1], me_d, me_e, ring(me_r, k, nr))
                for k in range(1, nr)]

    kz = to_experts(ksend, kg, kzs, kzr)

    def turn(index, carry):
        q, s = index // nd, lax.rem(index, nd)
        turned[span(s * tile, tile), span(q * tile, tile)] = adj[span(q * tile, tile), span(s * tile, tile)].T
        return carry


    arrive(f_copies)
    c_copies = []
    for a in list(range(1, ne)) + [0]:
        q = ring(me_e, a, ne)
        column = mm(adj[span(q * tile, tile), :], fall[...], plain).astype(bf16)
        for b in range(nr):
            csend[q, b] = column[b * mr:(b + 1) * mr, :]
        for b in range(nr):
            r = ring(me_r, b, nr)
            if (a, b) != (0, 0):
                n = a * nr + b - 1
                c_copies.append(send(csend.at[q, r], crecv.at[me_e, me_r], cs.at[n], cr.at[n], me_d, q, r))
    crecv[me_e, me_r] = csend[me_e, me_r]

    arrive(kz)
    kd = to_doms(kg, kds, kdr)
    load_wout.wait()
    load_win.wait()
    if keep_turned:
        lax.fori_loop(0, ne * nd, turn, 0)
    arrive(kd)
    whole_rows = rows == chunk
    if whole_rows:
        ga[...] = mm(kg[...], wout[...], cols_cols)

    arrive(c_copies)
    parts = []
    for r in range(nr):
        total = crecv[0, r].astype(f32)
        for e in range(1, ne):
            total = total + crecv[e, r].astype(f32)
        parts.append(total)
    agg = jnp.concatenate(parts, axis=1).astype(bf16).astype(f32)
    width = agg.shape[1]
    scale = lax.rsqrt(jnp.mean(agg * agg, axis=-1, keepdims=True) + epsilon)
    normed = (agg * scale).astype(bf16)
    tsend[...] = mm(place, normed, rows_rows).astype(bf16)
    tz = to_experts(tsend, tg, tzs, tzr)
    kxc = to_reps(kg, kx, kxs, kxr)
    arrive(tz)
    td = to_doms(tg, tds, tdr)

    def hidden(tokens, grad_act):
        pre = mm(tokens, win[...], plain)
        tangent = jnp.tanh(gelu_scale * (pre + gelu_cubic * pre * pre * pre))
        act = (0.5 * pre * (1.0 + tangent)).astype(bf16)
        slope = 0.5 * (1.0 + tangent) + 0.5 * pre * (1.0 - tangent * tangent) * gelu_scale * (
            1.0 + 3.0 * gelu_cubic * pre * pre)
        return act, (grad_act * slope).astype(bf16)

    def add_grads(tokens, grads, act, grad_hidden, first):
        one = mm(tokens, grad_hidden, rows_rows)
        two = mm(act, grads, rows_rows)
        if first:
            gwi[...] = one
            gwo[...] = two
        else:
            gwi[...] += one
            gwo[...] += two

    def scatter(source, target, ssem, rsem):
        copies = [
            send(source.at[span(dom_to(k) * seg, seg)], target.at[me_d], ssem.at[k - 1], rsem.at[k - 1],
                 dom_to(k), me_e, me_r)
            for k in dom_steps
        ]
        target[me_d] = source[span(me_d * seg, seg), :]
        return copies

    if whole_rows:
        gd = []
        for k in [0] + dom_steps:
            if k > 0:
                arrive([td[k - 1]])
            d = dom_from(k)
            where = span(d * seg, seg)
            act, grad_hidden = hidden(tg[where, :], ga[where, :])
            term = mm(grad_hidden, win[...], cols_cols).astype(bf16)
            acts[where, :] = act
            ghid[where, :] = grad_hidden
            if k == 0:
                grecv[me_d] = term
            else:
                gsend[where, :] = term
                gd.append(send(gsend.at[where], grecv.at[me_d], gds.at[k - 1], gdr.at[k - 1], d, me_e, me_r))
        txc = to_reps(tg, tx, txs, txr)
        osend[...] = mm(acts[...], wout[...], plain).astype(bf16)
        add_grads(tg[...], kg[...], acts[...], ghid[...], True)
    else:
        arrive(td)
        txc = to_reps(tg, tx, txs, txr)
        gwi[...] = jnp.zeros_like(gwi)
        gwo[...] = jnp.zeros_like(gwo)

        def one_chunk(index, carry):
            where = span(index * chunk, chunk)
            act, grad_hidden = hidden(tg[where, :], mm(kg[where, :], wout[...], cols_cols))
            gsend[where, :] = mm(grad_hidden, win[...], cols_cols).astype(bf16)
            osend[where, :] = mm(act, wout[...], plain).astype(bf16)
            add_grads(tg[where, :], kg[where, :], act, grad_hidden, False)
            return carry

        lax.fori_loop(0, rows // chunk, one_chunk, 0)
        gd = scatter(gsend, grecv, gds, gdr)

    def summed(target):
        total = target[0].astype(f32)
        for d in range(1, nd):
            total = total + target[d].astype(f32)
        return total.astype(bf16)

    def to_nodes(source, target, ssem, rsem):
        copies = []
        for k in exp_steps:
            e = ring(me_e, k, ne)
            copies.append(send(source.at[span(e * slots, slots)], target.at[span(me_e * slots, slots)],
                               ssem.at[k - 1], rsem.at[k - 1], me_d, e, me_r))
        mine = span(me_e * slots, slots)
        target[mine, :] = source[mine, :]
        return copies

    arrive(gd)
    gred[...] = summed(grecv)
    gz = to_nodes(gred, gback, gzs, gzr)
    od = scatter(osend, orecv, ods, odr)

    arrive(gz)
    back = mm(place, gback[...], plain)
    dot_mean = jnp.mean(agg * back, axis=-1, keepdims=True)
    grad_agg = (cot[...].astype(f32) + scale * back - agg * (scale * scale * scale) * dot_mean).astype(bf16)
    for r in range(nr):
        asend[r] = grad_agg[:, r * half:(r + 1) * half]
    here = span(me_e * tile + me_r * mr, mr)
    p_copies = []
    for a, b in pair_steps:
        n = a * nr + b - 1
        r = ring(me_r, b, nr)
        p_copies.append(send(asend.at[r], gall.at[here], ps.at[n], pr.at[n], me_d, ring(me_e, a, ne), r))
    gall[here, :] = asend[me_r]

    arrive(kxc)
    arrive(txc)
    for n in range(nr - 1):
        if whole_rows:
            act, grad_hidden = hidden(tx[n], mm(kx[n], wout[...], cols_cols))
            add_grads(tx[n], kx[n], act, grad_hidden, False)
        else:
            def other_chunk(index, carry):
                where = span(index * chunk, chunk)
                act, grad_hidden = hidden(tx[n, where, :], mm(kx[n, where, :], wout[...], cols_cols))
                add_grads(tx[n, where, :], kx[n, where, :], act, grad_hidden, False)
                return carry

            lax.fori_loop(0, rows // chunk, other_chunk, 0)
    store_i = local(gwi, gwi_hbm.at[0], 3)
    store_o = local(gwo, gwo_hbm.at[0], 4)

    arrive(od)
    ored[...] = summed(orecv)
    arrive(p_copies)
    oz = to_nodes(ored, oback, ozs, ozr)
    b_copies = []
    for k in dom_steps[::-1] + [0]:
        s = dom_to(k)
        if keep_turned:
            term = mm(turned[span(s * tile, tile), :], gall[...], plain)
        else:
            term = mm(adj[:, span(s * tile, tile)], gall[...], rows_rows)
        if k > 0:
            bsend[s] = term.astype(bf16)
            b_copies.append(send(bsend.at[s], brecv.at[me_d], bs.at[k - 1], br.at[k - 1], s, me_e, me_r))
        else:
            brecv[me_d] = term.astype(bf16)
    arrive(oz)
    out[...] = (agg + mm(place, oback[...], plain)).astype(bf16)
    arrive(b_copies)
    total = brecv[0].astype(f32)
    for d in range(1, nd):
        total = total + brecv[d].astype(f32)
    gf[...] = total
    store_i.wait()
    store_o.wait()
    for copy in pending:
        copy.wait_send()


def flip(me, k):
    place, bit = me, 1
    while bit <= k:
        if k & bit:
            place = place + bit - 2 * bit * lax.rem(me // bit, 2)
        bit *= 2
    return place


def body_paired(sizes, *refs):
    nd, ne, nr, slots, cuts = sizes
    (feat_hbm, tv_hbm, pairs_hbm, disp_hbm, win_hbm, wout_hbm, cot_hbm,
     out, gf, gwi, gwo,
     tv, pairs, disp, cot, win, wout, fall, adj, sorted_adj, turned, dsend, dall, csend, crecv,
     ksend, kg, kx, tg, tx, ga, acts, ghid, acts_far, gown, gsend, grecv, oown, osend, orecv, ored, oback,
     asend, gall, bsend, brecv, sent, ready, lsem, ssem, rsem) = refs
    me_d, me_e, me_r = lax.axis_index("dom"), lax.axis_index("expert"), lax.axis_index("rep")
    tile, half = fall.shape[0] // nd, fall.shape[1]
    tps = tv.shape[1]
    mr, width = cot.shape
    inner = win.shape[2]
    cut = mr // cuts
    groups = {}

    def copy_of(src, dst, d, e, r, group):
        return pltpu.make_async_remote_copy(
            src_ref=src, dst_ref=dst, send_sem=ssem.at[0], recv_sem=rsem.at[groups.setdefault(group, len(groups))],
            device_id={"dom": flip(me_d, d), "expert": flip(me_e, e), "rep": flip(me_r, r)},
            device_id_type=pl.DeviceIdType.MESH,
        )

    def send(src, dst, d, e, r, group):
        copy_of(src, dst, d, e, r, group).start()

    def local(src, dst, index):
        copy = pltpu.make_async_copy(src, dst, lsem.at[index])
        copy.start()
        return copy

    def arrive(group, ref):
        copy_of(ref, ref, 0, 0, 0, group).wait_recv()

    def span(start, size):
        return pl.ds(pl.multiple_of(start, size), size)

    pair_steps = [(a, b) for a in (2, 3, 1, 0) for b in range(nr) if (a, b) != (0, 0)]
    all_steps = pair_steps + [(0, 0)]
    barrier = pltpu.get_barrier_semaphore()
    core = lax.rem(me_d, 2)

    def tell(semaphore, d, e, r):
        pl.semaphore_signal(semaphore, inc=1,
                            device_id={"dom": flip(me_d, d), "expert": flip(me_e, e), "rep": flip(me_r, r)},
                            device_id_type=pl.DeviceIdType.MESH)

    @pl.when(core == 0)
    def _():
        tell(barrier, 2, 0, 0)
        for a, b in pair_steps:
            tell(barrier, 1, a, b)

    @pl.when(core == 1)
    def _():
        tell(barrier, 1, 0, 0)
        tell(barrier, 3, 0, 0)
        for a, b in pair_steps:
            tell(barrier, 0, a, b)

    own_feat = fall.at[span(me_d * tile, tile)]
    load_feat = local(feat_hbm, own_feat, 0)
    load_disp = local(disp_hbm, disp, 1)
    load_cot = local(cot_hbm, cot, 2)
    load_pairs = local(pairs_hbm, pairs, 3)
    load_tv = local(tv_hbm.at[0, 0], tv, 4)
    load_win = local(win_hbm.at[0], win.at[0], 5)
    load_wout = local(wout_hbm.at[0], wout.at[0], 6)

    load_disp.wait()
    dsend[...] = jnp.zeros_like(dsend)
    dsend[:, 0:mr] = jnp.broadcast_to(disp[...], (dsend.shape[0], mr))
    dall[me_e * nr + me_r] = dsend[...]
    load_feat.wait()

    @pl.when(core == 0)
    def _():
        pl.semaphore_wait(barrier, nd - 1)
        tell(ready.at[0], 1, 0, 0)

    @pl.when(core == 1)
    def _():
        pl.semaphore_wait(ready.at[0], 1)

    for k in (2, 3, 1):
        send(own_feat, own_feat, k, 0, 0, "features")

    @pl.when(core == 1)
    def _():
        pl.semaphore_wait(barrier, 2 * len(pair_steps))
        tell(ready.at[1], 1, 0, 0)

    @pl.when(core == 0)
    def _():
        pl.semaphore_wait(ready.at[1], 1)

    for a, b in pair_steps:
        send(dsend, dall.at[me_e * nr + me_r], 0, a, b, "order")

    place = (lax.broadcasted_iota(jnp.int32, (mr, ne * slots), 0) == disp[...]).astype(f32).astype(bf16)
    load_cot.wait()
    ksend[...] = mm(place, cot[...], rows_rows).astype(bf16)
    here = span(me_e * slots, slots)
    for a in (2, 3, 1, 0):
        send(ksend.at[span(flip(me_e, a) * slots, slots)], kg.at[here], 1, a, 0, "cotangent")
    load_pairs.wait()
    load_tv.wait()

    def build(index, carry):
        q, s = index // nd, lax.rem(index, nd)
        total = jnp.zeros((tile, tile), f32)
        for k in range(tps):
            hit = jnp.where(pairs[0, 0, s, k] == q, 1.0, 0.0).astype(f32)
            total = total + tv[s, k].astype(f32) * hit
        adj[span(q * tile, tile), span(s * tile, tile)] = total.astype(bf16)
        return carry

    lax.fori_loop(0, ne * nd, build, 0)
    load_win.wait()
    load_wout.wait()
    send(win.at[0], win.at[1], 1, 0, 0, "weights")
    send(wout.at[0], wout.at[1], 1, 0, 0, "weights")

    arrive("order", dall.at[pl.ds(0, ne * nr - 1)])
    for e in range(ne):
        for r in range(nr):
            group = (lax.broadcasted_iota(jnp.int32, (mr, mr), 0) == dall[e * nr + r, 0:1, 0:mr]).astype(f32).astype(bf16)
            begin = e * tile + r * mr
            moved = mm(group, adj[begin:begin + mr, :], rows_rows).astype(bf16)
            for x in range(ne):
                begin = x * tile + r * mr + e * slots
                sorted_adj[begin:begin + slots, :] = moved[x * slots:(x + 1) * slots, :]

    arrive("features", fall.at[pl.ds(0, (nd - 1) * tile)])

    def send_column(a, h):
        rows = pl.ds(h * cut, cut)
        for b in range(nr):
            send(csend.at[a * nr + flip(me_r, b), rows], crecv.at[me_e * nr + me_r, rows], 1, a, b, ("column", h))

    for a in (2, 3, 1, 0):
        column = mm(sorted_adj[span(flip(me_e, a) * tile, tile), :], fall[...], plain).astype(bf16)
        for b in range(nr):
            csend[a * nr + b] = column[b * mr:(b + 1) * mr, :]
        send_column(a, 0)
    for h in range(1, cuts):
        for a in (2, 3, 1, 0):
            send_column(a, h)

    arrive("cotangent", kg.at[pl.ds(0, ne * slots)])
    own, far = pl.ds(0, mr), pl.ds(mr, mr)
    near, last = pl.ds(2 * mr, mr), pl.ds(3 * mr, mr)
    send(kg.at[own], kg.at[far], 3, 0, 0, "far cotangent")
    send(kg.at[own], kg.at[near], 1, 0, 0, "near cotangent")

    def turn(index, carry):
        q, s = index // nd, lax.rem(index, nd)
        turned[span(s * tile, tile), span(q * tile, tile)] = sorted_adj[span(q * tile, tile), span(s * tile, tile)].T
        return carry

    lax.fori_loop(0, ne * nd, turn, 0)
    arrive("weights", win.at[pl.ds(0, 2)])
    arrive("far cotangent", kg.at[far])
    send(kg.at[far], kg.at[last], 1, 0, 0, "near cotangent")
    pair, other = pl.ds(0, 2 * mr), pl.ds(2 * mr, 2 * mr)
    send(kg.at[pair], kx.at[pair], 0, 0, 1, "across cotangent")
    for w in range(2):
        for j in range(2):
            ga[w, j] = mm(kg[w * mr:(w + 1) * mr, :], wout[j], cols_cols)

    def hidden(tokens, grad_act, j):
        pre = mm(tokens, win[j], plain)
        tangent = jnp.tanh(gelu_scale * (pre + gelu_cubic * pre * pre * pre))
        act = (0.5 * pre * (1.0 + tangent)).astype(bf16)
        slope = 0.5 * (1.0 + tangent) + 0.5 * pre * (1.0 - tangent * tangent) * gelu_scale * (
            1.0 + 3.0 * gelu_cubic * pre * pre)
        return act, (grad_act * slope).astype(bf16)

    def work(w, h):
        begin = w * mr + h * cut
        rows = pl.ds(begin, cut)
        tokens = tg[rows, :]
        total = None
        for j in range(2):
            act, grad_hidden = hidden(tokens, ga[w, j, h * cut:(h + 1) * cut, :], j)
            if j == 0:
                acts[rows, :] = act
                ghid[rows, :] = grad_hidden
            else:
                acts_far[rows, :] = act
            term = mm(grad_hidden, win[j], cols_cols)
            total = term if total is None else total + term
        return total

    aggs, scales = [], []
    for h in range(cuts):
        arrive(("column", h), crecv.at[pl.ds(0, ne * nr), pl.ds(0, cut)])
        halves = []
        for r in range(nr):
            total = crecv[r, h * cut:(h + 1) * cut, :].astype(f32)
            for e in range(1, ne):
                total = total + crecv[e * nr + r, h * cut:(h + 1) * cut, :].astype(f32)
            halves.append(total)
        agg = jnp.concatenate(halves, axis=1).astype(bf16).astype(f32)
        scale = lax.rsqrt(jnp.mean(agg * agg, axis=-1, keepdims=True) + epsilon)
        tg[h * cut:(h + 1) * cut, :] = (agg * scale).astype(bf16)
        send(tg.at[pl.ds(h * cut, cut)], tg.at[pl.ds(mr + h * cut, cut)], 3, 0, 0, ("tokens", h))
        aggs.append(agg)
        scales.append(scale)
        if h == 0:
            gown[0:cut, :] = work(0, 0)
    send(tg.at[own], tg.at[near], 1, 0, 0, "near tokens")
    for h in range(cuts):
        arrive(("tokens", h), tg.at[pl.ds(0, cut)])
        rows = pl.ds(h * cut, cut)
        gsend[rows, :] = work(1, h).astype(bf16)
        send(gsend.at[rows], grecv.at[rows], 3, 0, 0, ("terms", h))
        if h + 1 < cuts:
            gown[(h + 1) * cut:(h + 2) * cut, :] = work(0, h + 1)
    send(tg.at[pair], tx.at[pair], 0, 0, 1, "across tokens")
    send(tg.at[far], tg.at[last], 1, 0, 0, "near tokens")
    arrive("across cotangent", kx.at[pair])
    send(kx.at[pair], kx.at[other], 1, 0, 0, "near across")

    for h in range(cuts):
        arrive(("terms", h), grecv.at[pl.ds(0, cut)])
        rows = slice(h * cut, (h + 1) * cut)
        agg, scale = aggs[h], scales[h]
        back = (gown[rows, :] + grecv[rows, :].astype(f32)).astype(bf16).astype(f32)
        dot_mean = jnp.mean(agg * back, axis=-1, keepdims=True)
        grad_agg = (kg[rows, :].astype(f32) + scale * back - agg * (scale * scale * scale) * dot_mean).astype(bf16)
        for r in range(nr):
            asend[r, rows, :] = grad_agg[:, r * half:(r + 1) * half]
        there = span(me_e * tile + me_r * mr + h * cut, cut)
        for a, b in all_steps:
            send(asend.at[flip(me_r, b), pl.ds(h * cut, cut)], gall.at[there], 1, a, b, "gradients")

    def outputs(w):
        rows = slice(w * mr, (w + 1) * mr)
        return mm(acts[rows, :], wout[0], plain) + mm(acts_far[rows, :], wout[1], plain)

    osend[...] = outputs(1).astype(bf16)
    send(osend, orecv, 3, 0, 0, "halves")
    oown[...] = outputs(0)
    arrive("near cotangent", kg.at[pair])
    arrive("near tokens", tg.at[pair])
    act, grad_hidden = hidden(tg[2 * mr:, :], mm(kg[2 * mr:, :], wout[0], cols_cols), 0)
    acts[2 * mr:, :] = act
    ghid[2 * mr:, :] = grad_hidden
    gwi[0] = mm(tg[...], ghid[...], rows_rows)
    gwo[0] = mm(acts[...], kg[...], rows_rows)

    arrive("across tokens", tx.at[pair])
    send(tx.at[pair], tx.at[other], 1, 0, 0, "near across")

    def across(begin):
        rows = slice(begin, begin + 2 * mr)
        act, grad_hidden = hidden(tx[rows, :], mm(kx[rows, :], wout[0], cols_cols), 0)
        gwi[0] += mm(tx[rows, :], grad_hidden, rows_rows)
        gwo[0] += mm(act, kx[rows, :], rows_rows)

    across(0)
    arrive("halves", orecv)
    agg = jnp.concatenate(aggs, axis=0)
    routed = (oown[...] + orecv[...].astype(f32)).astype(bf16).astype(f32)
    ored[...] = (agg + routed).astype(bf16)
    for a in (2, 3, 1, 0):
        send(ored.at[span(flip(me_e, a) * slots, slots)], oback.at[here], 1, a, 0, "results")

    arrive("gradients", gall)
    for k in (2, 3, 1, 0):
        term = mm(turned[span(flip(me_d, k) * tile, tile), :], gall[...], plain)
        bsend[k] = term.astype(bf16)
        if k > 0:
            send(bsend.at[k], brecv.at[k - 1], k, 0, 0, "backterms")
    arrive("near across", kx)
    across(2 * mr)
    arrive("results", oback)
    out[...] = mm(place, oback[...], plain).astype(bf16)
    arrive("backterms", brecv)
    total = bsend[0].astype(f32)
    for k in range(1, nd):
        total = total + brecv[k - 1].astype(f32)
    gf[...] = total
    copy_of(sent, sent, 0, 0, 0, "features").wait_send()


def paired(nd, ne, nr, slots, features, tile_values, tile_pairs, dispatch, w_in, w_out, cotangent):
    tile, half = features.shape
    tps = tile_values.shape[3]
    mr, width = cotangent.shape
    inner = w_in.shape[2]
    rows = nd * mr
    cuts = 2
    vm = pltpu.VMEM
    steps = ne * nr - 1
    words = (2 * (nd - 1) * tile * half + 2 * steps * 8 * 128 + 2 * ne * slots * width + 2 * width * inner
             + 2 * ne * nr * mr * half + 8 * mr * width + 2 * rows * width)
    scratch = [
        vm((nd, tps, tile, tile), bf16), pltpu.SMEM(tile_pairs.shape, jnp.int32), vm(dispatch.shape, jnp.int32),
        vm((mr, width), bf16), vm((2, width, inner), bf16), vm((2, inner, width), bf16),
        vm((nd * tile, half), bf16), vm((ne * tile, nd * tile), bf16), vm((ne * tile, nd * tile), bf16),
        vm((nd * tile, ne * tile), bf16), vm((8, 128), jnp.int32), vm((ne * nr, 8, 128), jnp.int32),
        vm((ne * nr, mr, half), bf16), vm((ne * nr, mr, half), bf16),
        vm((mr, width), bf16), vm((rows, width), bf16), vm((rows, width), bf16),
        vm((rows, width), bf16), vm((rows, width), bf16),
        vm((2, 2, mr, inner), f32), vm((rows, inner), bf16), vm((rows, inner), bf16), vm((2 * mr, inner), bf16),
        vm((mr, width), f32), vm((mr, width), bf16), vm((mr, width), bf16),
        vm((mr, width), f32), vm((mr, width), bf16), vm((mr, width), bf16), vm((mr, width), bf16), vm((mr, width), bf16),
        vm((nr, mr, half), bf16), vm((ne * tile, half), bf16),
        vm((nd, tile, half), bf16), vm((nd - 1, tile, half), bf16),
        vm((words // 128, 128), bf16),
        pltpu.SemaphoreType.REGULAR((2,)), pltpu.SemaphoreType.DMA((7,)), pltpu.SemaphoreType.DMA((1,)), pltpu.SemaphoreType.DMA((17 + 3 * (cuts - 1),)),
    ]
    in_vmem = pl.BlockSpec(memory_space=pltpu.VMEM)
    in_hbm = pl.BlockSpec(memory_space=pl.ANY)
    arguments = (features, tile_values, tile_pairs, dispatch, w_in, w_out, cotangent)
    return leave(pl.pallas_call(
        functools.partial(body_paired, (nd, ne, nr, slots, cuts)),
        name="layer",
        out_shape=(
            vm((mr, width), bf16), vm((tile, half), f32), vm((1, width, inner), f32), vm((1, inner, width), f32),
        ),
        in_specs=[in_hbm] * 7,
        out_specs=[in_vmem] * 4,
        scratch_shapes=scratch,
        compiler_params=pltpu.CompilerParams(
            collective_id=0, has_side_effects=True, vmem_limit_bytes=56 * 1024 * 1024
        ),
    )(*[pltpu.with_memory_space_constraint(a, pltpu.HBM) for a in arguments]))


def store(*refs):
    count = len(refs) // 2
    copies = [pltpu.make_async_copy(refs[n], refs[count + n], refs[-1].at[n]) for n in range(count)]
    for copy in copies:
        copy.start()
    for copy in copies:
        copy.wait()


def leave(arrays):
    arrays = [pltpu.with_memory_space_constraint(a, pltpu.VMEM) for a in arrays]
    return pl.pallas_call(
        store,
        name="leave",
        out_shape=tuple(jax.ShapeDtypeStruct(a.shape, a.dtype) for a in arrays),
        in_specs=[pl.BlockSpec(memory_space=pltpu.VMEM)] * len(arrays),
        out_specs=[pl.BlockSpec(memory_space=pl.ANY)] * len(arrays),
        scratch_shapes=[pltpu.SemaphoreType.DMA((len(arrays),))],
    )(*arrays)


def on_device(nd, ne, nr, features, tile_values, tile_pairs, dispatch, w_in, w_out, cotangent):
    tile, half = features.shape
    tps = tile_values.shape[3]
    mr, width = cotangent.shape
    inner = w_in.shape[2]
    own = mr // ne
    slots = -(-own // 16) * 16
    if (nd, ne, nr) == (4, 4, 2) and slots == own and mr <= 128:
        return paired(nd, ne, nr, slots, features, tile_values, tile_pairs, dispatch, w_in, w_out, cotangent)
    if slots != own:
        dispatch = jnp.pad(dispatch.reshape(ne, own), ((0, 0), (0, slots - own)), constant_values=-1).reshape(1, -1)
    seg = ne * slots
    rows = nd * seg
    chunk = min(rows, 256)
    keep_turned = ne * nd <= 64
    dma = pltpu.SemaphoreType.DMA
    vm = pltpu.VMEM
    scratch = [
        vm((nd, tps, tile, tile), bf16), vm((width, inner), bf16), vm((inner, width), bf16),
        vm((width, inner), f32), vm((inner, width), f32),
        vm((nd * tile, half), bf16), vm((ne * tile, nd * tile), bf16),
        vm((nd * tile, ne * tile) if keep_turned else (16, 128), bf16),
        vm((ne, nr, mr, half), bf16), vm((ne, nr, mr, half), bf16),
        vm((seg, width), bf16), vm((rows, width), bf16), vm((nr - 1, rows, width), bf16),
        vm((seg, width), bf16), vm((rows, width), bf16), vm((nr - 1, rows, width), bf16),
        vm((rows, width), bf16), vm((nd, seg, width), bf16), vm((seg, width), bf16), vm((seg, width), bf16),
        vm((rows, width), bf16), vm((nd, seg, width), bf16), vm((seg, width), bf16), vm((seg, width), bf16),
        vm((nr, mr, half), bf16), vm((ne * tile, half), bf16),
        vm((nd, tile, half), bf16), vm((nd, tile, half), bf16),
        vm((chunk, inner), f32), vm((chunk, inner), bf16), vm((chunk, inner), bf16),
        dma((5,)),
    ]
    for count in (nd - 1, ne * nr - 1, ne - 1, nd - 1, nr - 1, ne - 1, nd - 1, nr - 1,
                  nd - 1, ne - 1, nd - 1, ne - 1, ne * nr - 1, nd - 1):
        scratch += [dma((count,)), dma((count,))]
    in_vmem = pl.BlockSpec(memory_space=pltpu.VMEM)
    in_hbm = pl.BlockSpec(memory_space=pl.ANY)
    return placed(pl.pallas_call(
        functools.partial(body, (nd, ne, nr, slots, chunk, keep_turned)),
        name="layer",
        out_shape=(
            jax.ShapeDtypeStruct((mr, width), bf16),
            jax.ShapeDtypeStruct((tile, half), f32),
            jax.ShapeDtypeStruct((1, width, inner), f32),
            jax.ShapeDtypeStruct((1, inner, width), f32),
        ),
        in_specs=[in_vmem, in_hbm, pl.BlockSpec(memory_space=pltpu.SMEM), in_vmem, in_hbm, in_hbm, in_vmem],
        out_specs=[in_vmem, in_vmem, in_hbm, in_hbm],
        scratch_shapes=scratch,
        compiler_params=pltpu.CompilerParams(
            collective_id=0, has_side_effects=True, vmem_limit_bytes=60 * 1024 * 1024
        ),
    )(features, tile_values, tile_pairs, dispatch, w_in, w_out, cotangent))


def hand_over(pieces, *refs):
    count = len(refs) // 3
    sources, targets, held = refs[:count], refs[count:2 * count], refs[2 * count:3 * count]
    come, go = refs[3 * count:]
    cuts = []
    for source, target, middle, number in zip(sources, targets, held, pieces):
        size = source.shape[-2] // number
        for piece in range(number):
            where = (0,) * (len(source.shape) - 2) + (pl.ds(piece * size, size),)
            n = len(cuts)
            cuts.append((
                pltpu.make_async_copy(source.at[where], middle.at[where], come.at[n]),
                pltpu.make_async_copy(middle.at[where], target.at[where], go.at[n]),
            ))
    for first, _ in cuts:
        first.start()
    for first, second in cuts:
        first.wait()
        second.start()
    for _, second in cuts:
        second.wait()


def placed(arrays):
    in_hbm = pl.BlockSpec(memory_space=pl.ANY)
    pieces = tuple(4 if a.size * a.dtype.itemsize >= 2 ** 19 else 1 for a in arrays)
    return pl.pallas_call(
        functools.partial(hand_over, pieces),
        name="hand_over",
        out_shape=tuple(jax.ShapeDtypeStruct(a.shape, a.dtype) for a in arrays),
        in_specs=[in_hbm] * len(arrays),
        out_specs=[in_hbm] * len(arrays),
        scratch_shapes=[pltpu.VMEM(a.shape, a.dtype) for a in arrays]
        + [pltpu.SemaphoreType.DMA((sum(pieces),)), pltpu.SemaphoreType.DMA((sum(pieces),))],
    )(*arrays)


def solution(mesh):
    in_specs = (
        P(("dom", "expert"), "rep"),
        P("dom", "expert", None, None, None, None),
        P("dom", "expert", None, None),
        P(("dom", "expert", "rep"), None),
        P("expert", None, "dom"),
        P("expert", "dom", None),
        P(("dom", "expert", "rep"), None),
    )
    out_specs = (
        P(("dom", "expert", "rep"), None),
        P(("dom", "expert"), "rep"),
        P("expert", None, "dom"),
        P("expert", "dom", None),
    )
    sizes = (mesh.shape["dom"], mesh.shape["expert"], mesh.shape["rep"])
    return jax.shard_map(
        functools.partial(on_device, *sizes), mesh=mesh, in_specs=in_specs, out_specs=out_specs, check_vma=False
    )
```

```python
import functools

import jax
import jax.numpy as jnp
from jax import lax
from jax.experimental import pallas as pl
from jax.experimental.pallas import tpu as pltpu
from jax.sharding import PartitionSpec as P

epsilon = 1e-06
gelu_scale = 0.7978845608028654
gelu_cubic = 0.044715
bf16 = jnp.bfloat16
f32 = jnp.float32


def mm(left, right, dims):
    return lax.dot_general(left, right, (dims, ((), ())), preferred_element_type=f32)


plain = ((1,), (0,))
rows_rows = ((0,), (0,))
cols_cols = ((1,), (1,))


def body(sizes, *refs):
    nd, ne, nr, slots, chunk, keep_turned = sizes
    (feat, tv_hbm, pairs, disp, win_hbm, wout_hbm, cot,
     out, gf, gwi_hbm, gwo_hbm,
     tv, win, wout, gwi, gwo, fall, adj, turned, csend, crecv,
     tsend, tg, tx, ksend, kg, kx,
     gsend, grecv, gred, gback, osend, orecv, ored, oback,
     asend, gall, bsend, brecv, ga, acts, ghid,
     lsem, fs, fr, cs, cr, tzs, tzr, tds, tdr, txs, txr, kzs, kzr, kds, kdr, kxs, kxr,
     gds, gdr, gzs, gzr, ods, odr, ozs, ozr, ps, pr, bs, br) = refs
    me_d, me_e, me_r = lax.axis_index("dom"), lax.axis_index("expert"), lax.axis_index("rep")
    tile = feat.shape[0]
    half = feat.shape[1]
    tps = tv.shape[1]
    mr = cot.shape[0]
    seg = ne * slots
    rows = nd * seg
    pending = []

    def ring(me, step, count):
        return lax.rem(me + step, count)

    def send(src, dst, ssem, rsem, d, e, r):
        copy = pltpu.make_async_remote_copy(
            src_ref=src, dst_ref=dst, send_sem=ssem, recv_sem=rsem,
            device_id={"dom": d, "expert": e, "rep": r},
            device_id_type=pl.DeviceIdType.MESH,
        )
        copy.start()
        pending.append(copy)
        return copy

    def local(src, dst, index):
        copy = pltpu.make_async_copy(src, dst, lsem.at[index])
        copy.start()
        return copy

    def arrive(copies):
        for copy in copies:
            copy.wait_recv()

    def span(start, size):
        return pl.ds(pl.multiple_of(start, size), size)

    load_tv = local(tv_hbm.at[0, 0], tv, 0)
    load_wout = local(wout_hbm.at[0], wout, 1)
    load_win = local(win_hbm.at[0], win, 2)

    dom_steps = list(range(1, nd))
    flips = nd & (nd - 1) == 0

    def dom_to(k):
        if not flips:
            return ring(me_d, k, nd)
        place, bit = me_d, 1
        while bit < nd:
            if k & bit:
                place = place + bit - 2 * bit * lax.rem(me_d // bit, 2)
            bit *= 2
        return place

    def dom_from(k):
        return dom_to(k) if flips else ring(me_d, nd - k, nd)

    exp_steps = list(range(1, ne))
    pair_steps = [(a, b) for a in range(ne) for b in range(nr) if (a, b) != (0, 0)]

    barrier = pltpu.get_barrier_semaphore()
    for k in dom_steps:
        pl.semaphore_signal(barrier, inc=1, device_id={"dom": dom_to(k), "expert": me_e, "rep": me_r},
                            device_id_type=pl.DeviceIdType.MESH)
    for a, b in pair_steps:
        pl.semaphore_signal(barrier, inc=1,
                            device_id={"dom": me_d, "expert": ring(me_e, a, ne), "rep": ring(me_r, b, nr)},
                            device_id_type=pl.DeviceIdType.MESH)

    place = (lax.broadcasted_iota(jnp.int32, (mr, seg), 0) == disp[...]).astype(f32).astype(bf16)
    fall[span(me_d * tile, tile), :] = feat[...]
    ksend[...] = mm(place, cot[...], rows_rows).astype(bf16)
    load_tv.wait()

    def build(index, carry):
        q, s = index // nd, lax.rem(index, nd)
        total = jnp.zeros((tile, tile), f32)
        for k in range(tps):
            hit = jnp.where(pairs[0, 0, s, k] == q, 1.0, 0.0).astype(f32)
            total = total + tv[s, k].astype(f32) * hit
        adj[span(q * tile, tile), span(s * tile, tile)] = total.astype(bf16)
        return carry

    lax.fori_loop(0, ne * nd, build, 0)
    pl.semaphore_wait(barrier, len(dom_steps) + len(pair_steps))

    f_copies = [
        send(feat, fall.at[span(me_d * tile, tile)], fs.at[k - 1], fr.at[k - 1], dom_to(k), me_e, me_r)
        for k in dom_steps
    ]

    def to_experts(source, target, ssem, rsem):
        copies = []
        for k in exp_steps:
            x = ring(me_e, k, ne)
            copies.append(send(source.at[span(x * slots, slots)], target.at[span((me_d * ne + me_e) * slots, slots)],
                               ssem.at[k - 1], rsem.at[k - 1], me_d, x, me_r))
        mine = span((me_d * ne + me_e) * slots, slots)
        target[mine, :] = source[span(me_e * slots, slots), :]
        return copies

    def to_doms(target, ssem, rsem):
        block = target.at[span(me_d * seg, seg)]
        return [send(block, block, ssem.at[k - 1], rsem.at[k - 1], dom_to(k), me_e, me_r) for k in dom_steps]

    def to_reps(source, target, ssem, rsem):
        return [send(source, target.at[k - 1], ssem.at[k - 1], rsem.at[k - 1], me_d, me_e, ring(me_r, k, nr))
                for k in range(1, nr)]

    kz = to_experts(ksend, kg, kzs, kzr)

    def turn(index, carry):
        q, s = index // nd, lax.rem(index, nd)
        turned[span(s * tile, tile), span(q * tile, tile)] = adj[span(q * tile, tile), span(s * tile, tile)].T
        return carry


    arrive(f_copies)
    c_copies = []
    for a in list(range(1, ne)) + [0]:
        q = ring(me_e, a, ne)
        column = mm(adj[span(q * tile, tile), :], fall[...], plain).astype(bf16)
        for b in range(nr):
            csend[q, b] = column[b * mr:(b + 1) * mr, :]
        for b in range(nr):
            r = ring(me_r, b, nr)
            if (a, b) != (0, 0):
                n = a * nr + b - 1
                c_copies.append(send(csend.at[q, r], crecv.at[me_e, me_r], cs.at[n], cr.at[n], me_d, q, r))
    crecv[me_e, me_r] = csend[me_e, me_r]

    arrive(kz)
    kd = to_doms(kg, kds, kdr)
    load_wout.wait()
    load_win.wait()
    if keep_turned:
        lax.fori_loop(0, ne * nd, turn, 0)
    arrive(kd)
    whole_rows = rows == chunk
    if whole_rows:
        ga[...] = mm(kg[...], wout[...], cols_cols)

    arrive(c_copies)
    parts = []
    for r in range(nr):
        total = crecv[0, r].astype(f32)
        for e in range(1, ne):
            total = total + crecv[e, r].astype(f32)
        parts.append(total)
    agg = jnp.concatenate(parts, axis=1).astype(bf16).astype(f32)
    width = agg.shape[1]
    scale = lax.rsqrt(jnp.mean(agg * agg, axis=-1, keepdims=True) + epsilon)
    normed = (agg * scale).astype(bf16)
    tsend[...] = mm(place, normed, rows_rows).astype(bf16)
    tz = to_experts(tsend, tg, tzs, tzr)
    kxc = to_reps(kg, kx, kxs, kxr)
    arrive(tz)
    td = to_doms(tg, tds, tdr)

    def hidden(tokens, grad_act):
        pre = mm(tokens, win[...], plain)
        tangent = jnp.tanh(gelu_scale * (pre + gelu_cubic * pre * pre * pre))
        act = (0.5 * pre * (1.0 + tangent)).astype(bf16)
        slope = 0.5 * (1.0 + tangent) + 0.5 * pre * (1.0 - tangent * tangent) * gelu_scale * (
            1.0 + 3.0 * gelu_cubic * pre * pre)
        return act, (grad_act * slope).astype(bf16)

    def add_grads(tokens, grads, act, grad_hidden, first):
        one = mm(tokens, grad_hidden, rows_rows)
        two = mm(act, grads, rows_rows)
        if first:
            gwi[...] = one
            gwo[...] = two
        else:
            gwi[...] += one
            gwo[...] += two

    def scatter(source, target, ssem, rsem):
        copies = [
            send(source.at[span(dom_to(k) * seg, seg)], target.at[me_d], ssem.at[k - 1], rsem.at[k - 1],
                 dom_to(k), me_e, me_r)
            for k in dom_steps
        ]
        target[me_d] = source[span(me_d * seg, seg), :]
        return copies

    if whole_rows:
        gd = []
        for k in [0] + dom_steps:
            if k > 0:
                arrive([td[k - 1]])
            d = dom_from(k)
            where = span(d * seg, seg)
            act, grad_hidden = hidden(tg[where, :], ga[where, :])
            term = mm(grad_hidden, win[...], cols_cols).astype(bf16)
            acts[where, :] = act
            ghid[where, :] = grad_hidden
            if k == 0:
                grecv[me_d] = term
            else:
                gsend[where, :] = term
                gd.append(send(gsend.at[where], grecv.at[me_d], gds.at[k - 1], gdr.at[k - 1], d, me_e, me_r))
        txc = to_reps(tg, tx, txs, txr)
        osend[...] = mm(acts[...], wout[...], plain).astype(bf16)
        add_grads(tg[...], kg[...], acts[...], ghid[...], True)
    else:
        arrive(td)
        txc = to_reps(tg, tx, txs, txr)
        gwi[...] = jnp.zeros_like(gwi)
        gwo[...] = jnp.zeros_like(gwo)

        def one_chunk(index, carry):
            where = span(index * chunk, chunk)
            act, grad_hidden = hidden(tg[where, :], mm(kg[where, :], wout[...], cols_cols))
            gsend[where, :] = mm(grad_hidden, win[...], cols_cols).astype(bf16)
            osend[where, :] = mm(act, wout[...], plain).astype(bf16)
            add_grads(tg[where, :], kg[where, :], act, grad_hidden, False)
            return carry

        lax.fori_loop(0, rows // chunk, one_chunk, 0)
        gd = scatter(gsend, grecv, gds, gdr)

    def summed(target):
        total = target[0].astype(f32)
        for d in range(1, nd):
            total = total + target[d].astype(f32)
        return total.astype(bf16)

    def to_nodes(source, target, ssem, rsem):
        copies = []
        for k in exp_steps:
            e = ring(me_e, k, ne)
            copies.append(send(source.at[span(e * slots, slots)], target.at[span(me_e * slots, slots)],
                               ssem.at[k - 1], rsem.at[k - 1], me_d, e, me_r))
        mine = span(me_e * slots, slots)
        target[mine, :] = source[mine, :]
        return copies

    arrive(gd)
    gred[...] = summed(grecv)
    gz = to_nodes(gred, gback, gzs, gzr)
    od = scatter(osend, orecv, ods, odr)

    arrive(gz)
    back = mm(place, gback[...], plain)
    dot_mean = jnp.mean(agg * back, axis=-1, keepdims=True)
    grad_agg = (cot[...].astype(f32) + scale * back - agg * (scale * scale * scale) * dot_mean).astype(bf16)
    for r in range(nr):
        asend[r] = grad_agg[:, r * half:(r + 1) * half]
    here = span(me_e * tile + me_r * mr, mr)
    p_copies = []
    for a, b in pair_steps:
        n = a * nr + b - 1
        r = ring(me_r, b, nr)
        p_copies.append(send(asend.at[r], gall.at[here], ps.at[n], pr.at[n], me_d, ring(me_e, a, ne), r))
    gall[here, :] = asend[me_r]

    arrive(kxc)
    arrive(txc)
    for n in range(nr - 1):
        if whole_rows:
            act, grad_hidden = hidden(tx[n], mm(kx[n], wout[...], cols_cols))
            add_grads(tx[n], kx[n], act, grad_hidden, False)
        else:
            def other_chunk(index, carry):
                where = span(index * chunk, chunk)
                act, grad_hidden = hidden(tx[n, where, :], mm(kx[n, where, :], wout[...], cols_cols))
                add_grads(tx[n, where, :], kx[n, where, :], act, grad_hidden, False)
                return carry

            lax.fori_loop(0, rows // chunk, other_chunk, 0)
    store_i = local(gwi, gwi_hbm.at[0], 3)
    store_o = local(gwo, gwo_hbm.at[0], 4)

    arrive(od)
    ored[...] = summed(orecv)
    arrive(p_copies)
    oz = to_nodes(ored, oback, ozs, ozr)
    b_copies = []
    for k in dom_steps[::-1] + [0]:
        s = dom_to(k)
        if keep_turned:
            term = mm(turned[span(s * tile, tile), :], gall[...], plain)
        else:
            term = mm(adj[:, span(s * tile, tile)], gall[...], rows_rows)
        if k > 0:
            bsend[s] = term.astype(bf16)
            b_copies.append(send(bsend.at[s], brecv.at[me_d], bs.at[k - 1], br.at[k - 1], s, me_e, me_r))
        else:
            brecv[me_d] = term.astype(bf16)
    arrive(oz)
    out[...] = (agg + mm(place, oback[...], plain)).astype(bf16)
    arrive(b_copies)
    total = brecv[0].astype(f32)
    for d in range(1, nd):
        total = total + brecv[d].astype(f32)
    gf[...] = total
    store_i.wait()
    store_o.wait()
    for copy in pending:
        copy.wait_send()


def flip(me, k):
    place, bit = me, 1
    while bit <= k:
        if k & bit:
            place = place + bit - 2 * bit * lax.rem(me // bit, 2)
        bit *= 2
    return place


def body_paired(sizes, *refs):
    nd, ne, nr, slots, cuts = sizes
    (feat_hbm, tv_hbm, pairs_hbm, disp_hbm, win_hbm, wout_hbm, cot_hbm,
     out, gf, gwi, gwo,
     tv, pairs, disp, cot, win, wout, fall, adj, sorted_adj, turned, dsend, dall, csend, crecv,
     ksend, kg, kx, tg, tx, ga, acts, ghid, acts_far, gown, gsend, grecv, oown, osend, orecv, ored, oback,
     asend, gall, bsend, brecv, sent, ready, lsem, ssem, rsem) = refs
    me_d, me_e, me_r = lax.axis_index("dom"), lax.axis_index("expert"), lax.axis_index("rep")
    tile, half = fall.shape[0] // nd, fall.shape[1]
    tps = tv.shape[1]
    mr, width = cot.shape
    inner = win.shape[2]
    cut = mr // cuts
    groups = {}

    def copy_of(src, dst, d, e, r, group):
        return pltpu.make_async_remote_copy(
            src_ref=src, dst_ref=dst, send_sem=ssem.at[0], recv_sem=rsem.at[groups.setdefault(group, len(groups))],
            device_id={"dom": flip(me_d, d), "expert": flip(me_e, e), "rep": flip(me_r, r)},
            device_id_type=pl.DeviceIdType.MESH,
        )

    def send(src, dst, d, e, r, group):
        copy_of(src, dst, d, e, r, group).start()

    def local(src, dst, index):
        copy = pltpu.make_async_copy(src, dst, lsem.at[index])
        copy.start()
        return copy

    def arrive(group, ref):
        copy_of(ref, ref, 0, 0, 0, group).wait_recv()

    def span(start, size):
        return pl.ds(pl.multiple_of(start, size), size)

    pair_steps = [(a, b) for a in (2, 3, 1, 0) for b in range(nr) if (a, b) != (0, 0)]
    all_steps = pair_steps + [(0, 0)]
    barrier = pltpu.get_barrier_semaphore()
    core = lax.rem(me_d, 2)

    def tell(semaphore, d, e, r):
        pl.semaphore_signal(semaphore, inc=1,
                            device_id={"dom": flip(me_d, d), "expert": flip(me_e, e), "rep": flip(me_r, r)},
                            device_id_type=pl.DeviceIdType.MESH)

    @pl.when(core == 0)
    def _():
        tell(barrier, 2, 0, 0)
        for a, b in pair_steps:
            tell(barrier, 1, a, b)

    @pl.when(core == 1)
    def _():
        tell(barrier, 1, 0, 0)
        tell(barrier, 3, 0, 0)
        for a, b in pair_steps:
            tell(barrier, 0, a, b)

    own_feat = fall.at[span(me_d * tile, tile)]
    load_feat = local(feat_hbm, own_feat, 0)
    load_disp = local(disp_hbm, disp, 1)
    load_cot = local(cot_hbm, cot, 2)
    load_pairs = local(pairs_hbm, pairs, 3)
    load_tv = local(tv_hbm.at[0, 0], tv, 4)
    load_win = local(win_hbm.at[0], win.at[0], 5)
    load_wout = local(wout_hbm.at[0], wout.at[0], 6)

    load_disp.wait()
    dsend[...] = jnp.zeros_like(dsend)
    dsend[:, 0:mr] = jnp.broadcast_to(disp[...], (dsend.shape[0], mr))
    dall[me_e * nr + me_r] = dsend[...]
    load_feat.wait()

    @pl.when(core == 0)
    def _():
        pl.semaphore_wait(barrier, nd - 1)
        tell(ready.at[0], 1, 0, 0)

    @pl.when(core == 1)
    def _():
        pl.semaphore_wait(ready.at[0], 1)

    for k in (2, 3, 1):
        send(own_feat, own_feat, k, 0, 0, "features")

    place = (lax.broadcasted_iota(jnp.int32, (mr, ne * slots), 0) == disp[...]).astype(f32).astype(bf16)
    load_cot.wait()
    ksend[...] = mm(place, cot[...], rows_rows).astype(bf16)
    @pl.when(core == 1)
    def _():
        pl.semaphore_wait(barrier, 2 * len(pair_steps))
        tell(ready.at[1], 1, 0, 0)

    @pl.when(core == 0)
    def _():
        pl.semaphore_wait(ready.at[1], 1)

    for a, b in pair_steps:
        send(dsend, dall.at[me_e * nr + me_r], 0, a, b, "order")

    here = span(me_e * slots, slots)
    for a in (2, 3, 1, 0):
        send(ksend.at[span(flip(me_e, a) * slots, slots)], kg.at[here], 1, a, 0, "cotangent")
    load_pairs.wait()
    load_tv.wait()

    def build(index, carry):
        q, s = index // nd, lax.rem(index, nd)
        total = jnp.zeros((tile, tile), f32)
        for k in range(tps):
            hit = jnp.where(pairs[0, 0, s, k] == q, 1.0, 0.0).astype(f32)
            total = total + tv[s, k].astype(f32) * hit
        adj[span(q * tile, tile), span(s * tile, tile)] = total.astype(bf16)
        return carry

    lax.fori_loop(0, ne * nd, build, 0)
    load_win.wait()
    load_wout.wait()
    send(win.at[0], win.at[1], 1, 0, 0, "weights")
    send(wout.at[0], wout.at[1], 1, 0, 0, "weights")

    arrive("order", dall.at[pl.ds(0, ne * nr - 1)])
    for e in range(ne):
        for r in range(nr):
            group = (lax.broadcasted_iota(jnp.int32, (mr, mr), 0) == dall[e * nr + r, 0:1, 0:mr]).astype(f32).astype(bf16)
            begin = e * tile + r * mr
            moved = mm(group, adj[begin:begin + mr, :], rows_rows).astype(bf16)
            for x in range(ne):
                begin = x * tile + r * mr + e * slots
                sorted_adj[begin:begin + slots, :] = moved[x * slots:(x + 1) * slots, :]

    arrive("features", fall.at[pl.ds(0, (nd - 1) * tile)])

    def send_column(a, h):
        rows = pl.ds(h * cut, cut)
        for b in range(nr):
            send(csend.at[a * nr + flip(me_r, b), rows], crecv.at[me_e * nr + me_r, rows], 1, a, b, ("column", h))

    for a in (2, 3, 1, 0):
        column = mm(sorted_adj[span(flip(me_e, a) * tile, tile), :], fall[...], plain).astype(bf16)
        for b in range(nr):
            csend[a * nr + b] = column[b * mr:(b + 1) * mr, :]
        send_column(a, 0)
    for h in range(1, cuts):
        for a in (2, 3, 1, 0):
            send_column(a, h)

    arrive("cotangent", kg.at[pl.ds(0, ne * slots)])
    own, far = pl.ds(0, mr), pl.ds(mr, mr)
    near, last = pl.ds(2 * mr, mr), pl.ds(3 * mr, mr)
    send(kg.at[own], kg.at[far], 3, 0, 0, "far cotangent")
    send(kg.at[own], kg.at[near], 1, 0, 0, "near cotangent")

    def turn(index, carry):
        q, s = index // nd, lax.rem(index, nd)
        turned[span(s * tile, tile), span(q * tile, tile)] = sorted_adj[span(q * tile, tile), span(s * tile, tile)].T
        return carry

    lax.fori_loop(0, ne * nd, turn, 0)
    arrive("weights", win.at[pl.ds(0, 2)])
    arrive("far cotangent", kg.at[far])
    send(kg.at[far], kg.at[last], 1, 0, 0, "near cotangent")
    pair, other = pl.ds(0, 2 * mr), pl.ds(2 * mr, 2 * mr)
    send(kg.at[pair], kx.at[pair], 0, 0, 1, "across cotangent")
    for w in range(2):
        for j in range(2):
            ga[w, j] = mm(kg[w * mr:(w + 1) * mr, :], wout[j], cols_cols)

    def hidden(tokens, grad_act, j):
        pre = mm(tokens, win[j], plain)
        tangent = jnp.tanh(gelu_scale * (pre + gelu_cubic * pre * pre * pre))
        act = (0.5 * pre * (1.0 + tangent)).astype(bf16)
        slope = 0.5 * (1.0 + tangent) + 0.5 * pre * (1.0 - tangent * tangent) * gelu_scale * (
            1.0 + 3.0 * gelu_cubic * pre * pre)
        return act, (grad_act * slope).astype(bf16)

    def work(w, h):
        begin = w * mr + h * cut
        rows = pl.ds(begin, cut)
        tokens = tg[rows, :]
        total = None
        for j in range(2):
            act, grad_hidden = hidden(tokens, ga[w, j, h * cut:(h + 1) * cut, :], j)
            if j == 0:
                acts[rows, :] = act
                ghid[rows, :] = grad_hidden
            else:
                acts_far[rows, :] = act
            term = mm(grad_hidden, win[j], cols_cols)
            total = term if total is None else total + term
        return total

    aggs, scales = [], []
    for h in range(cuts):
        arrive(("column", h), crecv.at[pl.ds(0, ne * nr), pl.ds(0, cut)])
        halves = []
        for r in range(nr):
            total = crecv[r, h * cut:(h + 1) * cut, :].astype(f32)
            for e in range(1, ne):
                total = total + crecv[e * nr + r, h * cut:(h + 1) * cut, :].astype(f32)
            halves.append(total)
        agg = jnp.concatenate(halves, axis=1).astype(bf16).astype(f32)
        scale = lax.rsqrt(jnp.mean(agg * agg, axis=-1, keepdims=True) + epsilon)
        tg[h * cut:(h + 1) * cut, :] = (agg * scale).astype(bf16)
        send(tg.at[pl.ds(h * cut, cut)], tg.at[pl.ds(mr + h * cut, cut)], 3, 0, 0, ("tokens", h))
        aggs.append(agg)
        scales.append(scale)
        if h == 0:
            gown[0:cut, :] = work(0, 0)
    send(tg.at[own], tg.at[near], 1, 0, 0, "near tokens")
    for h in range(cuts):
        arrive(("tokens", h), tg.at[pl.ds(0, cut)])
        rows = pl.ds(h * cut, cut)
        gsend[rows, :] = work(1, h).astype(bf16)
        send(gsend.at[rows], grecv.at[rows], 3, 0, 0, ("terms", h))
        if h + 1 < cuts:
            gown[(h + 1) * cut:(h + 2) * cut, :] = work(0, h + 1)
    send(tg.at[pair], tx.at[pair], 0, 0, 1, "across tokens")
    send(tg.at[far], tg.at[last], 1, 0, 0, "near tokens")
    arrive("across cotangent", kx.at[pair])
    send(kx.at[pair], kx.at[other], 1, 0, 0, "near across")

    for h in range(cuts):
        arrive(("terms", h), grecv.at[pl.ds(0, cut)])
        rows = slice(h * cut, (h + 1) * cut)
        agg, scale = aggs[h], scales[h]
        back = (gown[rows, :] + grecv[rows, :].astype(f32)).astype(bf16).astype(f32)
        dot_mean = jnp.mean(agg * back, axis=-1, keepdims=True)
        grad_agg = (kg[rows, :].astype(f32) + scale * back - agg * (scale * scale * scale) * dot_mean).astype(bf16)
        for r in range(nr):
            asend[r, rows, :] = grad_agg[:, r * half:(r + 1) * half]
        there = span(me_e * tile + me_r * mr + h * cut, cut)
        for a, b in all_steps:
            send(asend.at[flip(me_r, b), pl.ds(h * cut, cut)], gall.at[there], 1, a, b, "gradients")

    def outputs(w):
        rows = slice(w * mr, (w + 1) * mr)
        return mm(acts[rows, :], wout[0], plain) + mm(acts_far[rows, :], wout[1], plain)

    osend[...] = outputs(1).astype(bf16)
    send(osend, orecv, 3, 0, 0, "halves")
    oown[...] = outputs(0)
    arrive("near cotangent", kg.at[pair])
    arrive("near tokens", tg.at[pair])
    act, grad_hidden = hidden(tg[2 * mr:, :], mm(kg[2 * mr:, :], wout[0], cols_cols), 0)
    acts[2 * mr:, :] = act
    ghid[2 * mr:, :] = grad_hidden
    gwi[0] = mm(tg[...], ghid[...], rows_rows)
    gwo[0] = mm(acts[...], kg[...], rows_rows)

    arrive("across tokens", tx.at[pair])
    send(tx.at[pair], tx.at[other], 1, 0, 0, "near across")

    def across(begin):
        rows = slice(begin, begin + 2 * mr)
        act, grad_hidden = hidden(tx[rows, :], mm(kx[rows, :], wout[0], cols_cols), 0)
        gwi[0] += mm(tx[rows, :], grad_hidden, rows_rows)
        gwo[0] += mm(act, kx[rows, :], rows_rows)

    across(0)
    arrive("halves", orecv)
    agg = jnp.concatenate(aggs, axis=0)
    routed = (oown[...] + orecv[...].astype(f32)).astype(bf16).astype(f32)
    ored[...] = (agg + routed).astype(bf16)
    for a in (2, 3, 1, 0):
        send(ored.at[span(flip(me_e, a) * slots, slots)], oback.at[here], 1, a, 0, "results")

    arrive("gradients", gall)
    for k in (2, 3, 1, 0):
        term = mm(turned[span(flip(me_d, k) * tile, tile), :], gall[...], plain)
        bsend[k] = term.astype(bf16)
        if k > 0:
            send(bsend.at[k], brecv.at[k - 1], k, 0, 0, "backterms")
    arrive("near across", kx)
    across(2 * mr)
    arrive("results", oback)
    out[...] = mm(place, oback[...], plain).astype(bf16)
    arrive("backterms", brecv)
    total = bsend[0].astype(f32)
    for k in range(1, nd):
        total = total + brecv[k - 1].astype(f32)
    gf[...] = total
    copy_of(sent, sent, 0, 0, 0, "features").wait_send()


def paired(nd, ne, nr, slots, features, tile_values, tile_pairs, dispatch, w_in, w_out, cotangent):
    tile, half = features.shape
    tps = tile_values.shape[3]
    mr, width = cotangent.shape
    inner = w_in.shape[2]
    rows = nd * mr
    cuts = 2
    vm = pltpu.VMEM
    steps = ne * nr - 1
    words = (2 * (nd - 1) * tile * half + 2 * steps * 8 * 128 + 2 * ne * slots * width + 2 * width * inner
             + 2 * ne * nr * mr * half + 8 * mr * width + 2 * rows * width)
    scratch = [
        vm((nd, tps, tile, tile), bf16), pltpu.SMEM(tile_pairs.shape, jnp.int32), vm(dispatch.shape, jnp.int32),
        vm((mr, width), bf16), vm((2, width, inner), bf16), vm((2, inner, width), bf16),
        vm((nd * tile, half), bf16), vm((ne * tile, nd * tile), bf16), vm((ne * tile, nd * tile), bf16),
        vm((nd * tile, ne * tile), bf16), vm((8, 128), jnp.int32), vm((ne * nr, 8, 128), jnp.int32),
        vm((ne * nr, mr, half), bf16), vm((ne * nr, mr, half), bf16),
        vm((mr, width), bf16), vm((rows, width), bf16), vm((rows, width), bf16),
        vm((rows, width), bf16), vm((rows, width), bf16),
        vm((2, 2, mr, inner), f32), vm((rows, inner), bf16), vm((rows, inner), bf16), vm((2 * mr, inner), bf16),
        vm((mr, width), f32), vm((mr, width), bf16), vm((mr, width), bf16),
        vm((mr, width), f32), vm((mr, width), bf16), vm((mr, width), bf16), vm((mr, width), bf16), vm((mr, width), bf16),
        vm((nr, mr, half), bf16), vm((ne * tile, half), bf16),
        vm((nd, tile, half), bf16), vm((nd - 1, tile, half), bf16),
        vm((words // 128, 128), bf16),
        pltpu.SemaphoreType.REGULAR((2,)), pltpu.SemaphoreType.DMA((7,)), pltpu.SemaphoreType.DMA((1,)), pltpu.SemaphoreType.DMA((17 + 3 * (cuts - 1),)),
    ]
    in_vmem = pl.BlockSpec(memory_space=pltpu.VMEM)
    in_hbm = pl.BlockSpec(memory_space=pl.ANY)
    arguments = (features, tile_values, tile_pairs, dispatch, w_in, w_out, cotangent)
    return leave(pl.pallas_call(
        functools.partial(body_paired, (nd, ne, nr, slots, cuts)),
        name="layer",
        out_shape=(
            vm((mr, width), bf16), vm((tile, half), f32), vm((1, width, inner), f32), vm((1, inner, width), f32),
        ),
        in_specs=[in_hbm] * 7,
        out_specs=[in_vmem] * 4,
        scratch_shapes=scratch,
        compiler_params=pltpu.CompilerParams(
            collective_id=0, has_side_effects=True, vmem_limit_bytes=56 * 1024 * 1024
        ),
    )(*[pltpu.with_memory_space_constraint(a, pltpu.HBM) for a in arguments]))


def store(*refs):
    count = len(refs) // 2
    copies = [pltpu.make_async_copy(refs[n], refs[count + n], refs[-1].at[n]) for n in range(count)]
    for copy in copies:
        copy.start()
    for copy in copies:
        copy.wait()


def leave(arrays):
    arrays = [pltpu.with_memory_space_constraint(a, pltpu.VMEM) for a in arrays]
    return pl.pallas_call(
        store,
        name="leave",
        out_shape=tuple(jax.ShapeDtypeStruct(a.shape, a.dtype) for a in arrays),
        in_specs=[pl.BlockSpec(memory_space=pltpu.VMEM)] * len(arrays),
        out_specs=[pl.BlockSpec(memory_space=pl.ANY)] * len(arrays),
        scratch_shapes=[pltpu.SemaphoreType.DMA((len(arrays),))],
    )(*arrays)


def on_device(nd, ne, nr, features, tile_values, tile_pairs, dispatch, w_in, w_out, cotangent):
    tile, half = features.shape
    tps = tile_values.shape[3]
    mr, width = cotangent.shape
    inner = w_in.shape[2]
    own = mr // ne
    slots = -(-own // 16) * 16
    if (nd, ne, nr) == (4, 4, 2) and slots == own and mr <= 128:
        return paired(nd, ne, nr, slots, features, tile_values, tile_pairs, dispatch, w_in, w_out, cotangent)
    if slots != own:
        dispatch = jnp.pad(dispatch.reshape(ne, own), ((0, 0), (0, slots - own)), constant_values=-1).reshape(1, -1)
    seg = ne * slots
    rows = nd * seg
    chunk = min(rows, 256)
    keep_turned = ne * nd <= 64
    dma = pltpu.SemaphoreType.DMA
    vm = pltpu.VMEM
    scratch = [
        vm((nd, tps, tile, tile), bf16), vm((width, inner), bf16), vm((inner, width), bf16),
        vm((width, inner), f32), vm((inner, width), f32),
        vm((nd * tile, half), bf16), vm((ne * tile, nd * tile), bf16),
        vm((nd * tile, ne * tile) if keep_turned else (16, 128), bf16),
        vm((ne, nr, mr, half), bf16), vm((ne, nr, mr, half), bf16),
        vm((seg, width), bf16), vm((rows, width), bf16), vm((nr - 1, rows, width), bf16),
        vm((seg, width), bf16), vm((rows, width), bf16), vm((nr - 1, rows, width), bf16),
        vm((rows, width), bf16), vm((nd, seg, width), bf16), vm((seg, width), bf16), vm((seg, width), bf16),
        vm((rows, width), bf16), vm((nd, seg, width), bf16), vm((seg, width), bf16), vm((seg, width), bf16),
        vm((nr, mr, half), bf16), vm((ne * tile, half), bf16),
        vm((nd, tile, half), bf16), vm((nd, tile, half), bf16),
        vm((chunk, inner), f32), vm((chunk, inner), bf16), vm((chunk, inner), bf16),
        dma((5,)),
    ]
    for count in (nd - 1, ne * nr - 1, ne - 1, nd - 1, nr - 1, ne - 1, nd - 1, nr - 1,
                  nd - 1, ne - 1, nd - 1, ne - 1, ne * nr - 1, nd - 1):
        scratch += [dma((count,)), dma((count,))]
    in_vmem = pl.BlockSpec(memory_space=pltpu.VMEM)
    in_hbm = pl.BlockSpec(memory_space=pl.ANY)
    return placed(pl.pallas_call(
        functools.partial(body, (nd, ne, nr, slots, chunk, keep_turned)),
        name="layer",
        out_shape=(
            jax.ShapeDtypeStruct((mr, width), bf16),
            jax.ShapeDtypeStruct((tile, half), f32),
            jax.ShapeDtypeStruct((1, width, inner), f32),
            jax.ShapeDtypeStruct((1, inner, width), f32),
        ),
        in_specs=[in_vmem, in_hbm, pl.BlockSpec(memory_space=pltpu.SMEM), in_vmem, in_hbm, in_hbm, in_vmem],
        out_specs=[in_vmem, in_vmem, in_hbm, in_hbm],
        scratch_shapes=scratch,
        compiler_params=pltpu.CompilerParams(
            collective_id=0, has_side_effects=True, vmem_limit_bytes=60 * 1024 * 1024
        ),
    )(features, tile_values, tile_pairs, dispatch, w_in, w_out, cotangent))


def hand_over(pieces, *refs):
    count = len(refs) // 3
    sources, targets, held = refs[:count], refs[count:2 * count], refs[2 * count:3 * count]
    come, go = refs[3 * count:]
    cuts = []
    for source, target, middle, number in zip(sources, targets, held, pieces):
        size = source.shape[-2] // number
        for piece in range(number):
            where = (0,) * (len(source.shape) - 2) + (pl.ds(piece * size, size),)
            n = len(cuts)
            cuts.append((
                pltpu.make_async_copy(source.at[where], middle.at[where], come.at[n]),
                pltpu.make_async_copy(middle.at[where], target.at[where], go.at[n]),
            ))
    for first, _ in cuts:
        first.start()
    for first, second in cuts:
        first.wait()
        second.start()
    for _, second in cuts:
        second.wait()


def placed(arrays):
    in_hbm = pl.BlockSpec(memory_space=pl.ANY)
    pieces = tuple(4 if a.size * a.dtype.itemsize >= 2 ** 19 else 1 for a in arrays)
    return pl.pallas_call(
        functools.partial(hand_over, pieces),
        name="hand_over",
        out_shape=tuple(jax.ShapeDtypeStruct(a.shape, a.dtype) for a in arrays),
        in_specs=[in_hbm] * len(arrays),
        out_specs=[in_hbm] * len(arrays),
        scratch_shapes=[pltpu.VMEM(a.shape, a.dtype) for a in arrays]
        + [pltpu.SemaphoreType.DMA((sum(pieces),)), pltpu.SemaphoreType.DMA((sum(pieces),))],
    )(*arrays)


def solution(mesh):
    in_specs = (
        P(("dom", "expert"), "rep"),
        P("dom", "expert", None, None, None, None),
        P("dom", "expert", None, None),
        P(("dom", "expert", "rep"), None),
        P("expert", None, "dom"),
        P("expert", "dom", None),
        P(("dom", "expert", "rep"), None),
    )
    out_specs = (
        P(("dom", "expert", "rep"), None),
        P(("dom", "expert"), "rep"),
        P("expert", None, "dom"),
        P("expert", "dom", None),
    )
    sizes = (mesh.shape["dom"], mesh.shape["expert"], mesh.shape["rep"])
    return jax.shard_map(
        functools.partial(on_device, *sizes), mesh=mesh, in_specs=in_specs, out_specs=out_specs, check_vma=False
    )
```
